32 devices in a mesh: dp: 4 (over x, core), ctx: 8 (over z, y).
Axes of the slice: x: 2, y: 2, z: 4, core: 2. Of those that a mesh axis runs over, the one named last changes fastest.
Arguments:
- patches: bfloat16 [4, 2304, 1024], P('dp', 'ctx'), may hold values from -6 to 6
- enc_pos: bfloat16 [2304, 1024], P('ctx'), may hold values from -6 to 6
- w_embed: bfloat16 [1024, 1024], replicated, may hold values from -0.1875 to 0.1875
- enc_gain: bfloat16 [1024], replicated, may hold values from 0.25 to 1.75
- w_qkv: bfloat16 [1024, 1536], replicated, may hold values from -0.3125 to 0.3125
- w_out: bfloat16 [512, 1024], replicated, may hold values from -0.25 to 0.25
- enc_out_gain: bfloat16 [1024], replicated, may hold values from 0.25 to 1.75
- w_dec_embed: bfloat16 [1024, 512], replicated, may hold values from -0.1875 to 0.1875
- mask_token: bfloat16 [512], replicated, may hold values from -4 to 4
- dec_pos: bfloat16 [2304, 512], P('ctx'), may hold values from -6 to 6
- dec_attn_gain: bfloat16 [512], replicated, may hold values from 0.25 to 1.75
- decoder_query_key_value_weight: bfloat16 [512, 768], replicated, may hold values from -0.4375 to 0.4375
- w_dec_out: bfloat16 [256, 512], replicated, may hold values from -0.375 to 0.375
- decoder_feed_gain: bfloat16 [512], replicated, may hold values from 0.25 to 1.75
- w_up: bfloat16 [512, 2048], replicated, may hold values from -0.25 to 0.25
- w_down: bfloat16 [2048, 512], replicated, may hold values from -0.125 to 0.125
- head_gain: bfloat16 [512], replicated, may hold values from 0.25 to 1.75
- w_head: bfloat16 [512, 1024], replicated, may hold values from -0.25 to 0.25
- visible_rows: int32 [4, 2304], P('dp', 'ctx'), may hold values from -1 to 287, as said below
- visible_count: int32 [4, 8], P('dp', 'ctx'), may hold values from 0 to 288, as said below
- owner_slot: int32 [4, 2304], P('dp', 'ctx'), may hold values from 0 to 2303, as said below
Outputs:
- reconstruction: bfloat16 [4, 2304, 1024], P('dp', 'ctx')
- grad_head: float32 [512, 1024], replicated
- grad_dec_out: float32 [256, 512], replicated
- loss: float32 [], replicated
The draws below stay inside these ranges and needn't reach their ends.
Inputs may be any that keep to these rules, and one draw needn't show every extreme that they name: `visible_rows`: slots from visible_count onward hold -1; the first visible_count slots hold distinct local indices in increasing order. `visible_count`: the counts of one gather sum to 768; in every gather one device has exactly 288. `owner_slot`: A permutation of each gather's patches; exactly 36 patches of device c go to device d, into rows c * 36 to (c + 1) * 36 - 1 of its local rows.
All inputs are finite; a program needn't handle non-finite values.
Results may differ from the reference program's by a relative error of at most 0.019.
Values may be sent and summed in bfloat16 or wider, within the bound.
No kernel may reach another device: no remote copies, remote signals or barrier semaphores. Data moves between devices by JAX's collectives and lax.ppermute only.
A program may use at most 128 MiB of HBM per device.

```python
import jax
import jax.numpy as jnp
from jax import lax

D = 1024
EH = 8
HD = 64
DD = 512
DH = 8
DHD = 32
DFF = 2048
PIX = 1024
PDEV = 288
VIS_DEV = 96
CAP = 288
EW = 512
DEW = 256
NP = 2304
GATHERS = 4
N_CTX = 8


def visible_plan(key):

    def one_gather(sub):
        key_full, key_units, key_perm = jax.random.split(sub, 3)
        full = jax.random.randint(key_full, (), 0, N_CTX)
        index = jnp.arange(N_CTX, dtype=jnp.int32)
        counts = jnp.where(index == full, CAP, VIS_DEV).astype(jnp.int32)
        starts = jax.random.randint(key_units, (2 * VIS_DEV,), 0, N_CTX).astype(jnp.int32)

        def take(step, current):
            usable = (current > 0) & (index != full)
            distance = (index - starts[step]) % N_CTX
            picked = jnp.argmin(jnp.where(usable, distance, 2 * N_CTX))
            return current - (index == picked).astype(jnp.int32)
        counts = lax.fori_loop(0, 2 * VIS_DEV, take, counts)
        perms = jax.vmap(lambda k: jax.random.permutation(k, PDEV))(jax.random.split(key_perm, N_CTX))
        ranks = jnp.argsort(perms, axis=1)
        chosen = ranks < counts[:, None]
        local = jnp.arange(PDEV, dtype=jnp.int32)[None, :]
        keyed = jnp.where(chosen, local, PDEV + local)
        ordered = jnp.sort(keyed, axis=1)[:, :CAP]
        slot_rows = jnp.where(ordered < PDEV, ordered, -1)
        return (counts.astype(jnp.int32), slot_rows.reshape(-1).astype(jnp.int32))
    subs = jax.random.split(jax.random.fold_in(key, 11), GATHERS)
    return jax.vmap(one_gather)(subs)


def draw_visible_rows(key, part):
    return visible_plan(key)[1].astype(jnp.int32)


def draw_visible_count(key, part):
    return visible_plan(key)[0].astype(jnp.int32)


def draw_owner_slot(key, part):
    share = PDEV // N_CTX

    def one_gather(sub):
        perms = jax.vmap(lambda k: jax.random.permutation(k, PDEV))(jax.random.split(sub, N_CTX))
        ranks = jnp.argsort(perms, axis=1).astype(jnp.int32)
        source = jnp.arange(N_CTX, dtype=jnp.int32)[:, None]
        owners = ranks // share * PDEV + source * share + ranks % share
        return owners.reshape(-1).astype(jnp.int32)
    subs = jax.random.split(jax.random.fold_in(key, 29), GATHERS)
    return jax.vmap(one_gather)(subs)


def levels(key, dims, cuts, smallest, top_value):
    level = 1.0
    for axis_at, parts in cuts:
        steps = jax.random.uniform(jax.random.fold_in(jax.random.fold_in(key, 6), axis_at), (parts,), jnp.float32, smallest / len(cuts), top_value / len(cuts))
        level = level * jnp.repeat(jnp.exp(steps), dims[axis_at] // parts).reshape((-1,) + (1,) * (len(dims) - 1 - axis_at))
    return level


def scatter_about(stream_key, shape, deviation, reach, pieces=(), kind=jnp.bfloat16):
    values = jax.random.normal(stream_key, shape, jnp.float32) * deviation
    if len(pieces) > 0:
        values = levels(stream_key, shape, pieces, -0.22, 0.18) * values
    return jnp.clip(values, min=-reach, max=reach).astype(kind)


def setup_inputs(seed: int = 0) -> dict:
    seeds = jax.random.split(jax.random.key(seed), 22)
    return {
        "patches": scatter_about(seeds[0], (GATHERS, NP, PIX), 1.0, 6.0, ((0, 4), (1, 8))),
        "enc_pos": scatter_about(seeds[1], (NP, D), 1.0, 6.0, ((0, 8),)),
        "w_embed": scatter_about(seeds[2], (PIX, D), PIX ** -0.5, 0.1875),
        "enc_gain": jnp.clip(1.0 + 0.15 * jax.random.normal(seeds[3], (D,), jnp.float32), 0.25, 1.75).astype(jnp.bfloat16),
        "w_qkv": scatter_about(seeds[4], (D, 3 * EW), (2 * D // 5) ** -0.5, 0.3125),
        "w_out": scatter_about(seeds[5], (EW, D), EW ** -0.5, 0.25),
        "enc_out_gain": jnp.clip(1.0 + 0.15 * jax.random.normal(seeds[6], (D,), jnp.float32), 0.25, 1.75).astype(jnp.bfloat16),
        "w_dec_embed": scatter_about(seeds[7], (D, DD), D ** -0.5, 0.1875),
        "mask_token": scatter_about(seeds[8], (DD,), 1.0, 4.0),
        "dec_pos": scatter_about(seeds[9], (NP, DD), 1.0, 6.0, ((0, 8),)),
        "dec_attn_gain": jnp.clip(1.0 + 0.15 * jax.random.normal(seeds[10], (DD,), jnp.float32), 0.25, 1.75).astype(jnp.bfloat16),
        "decoder_query_key_value_weight": scatter_about(seeds[11], (DD, 3 * DEW), (2 * DD // 5) ** -0.5, 0.4375),
        "w_dec_out": scatter_about(seeds[12], (DEW, DD), DEW ** -0.5, 0.375),
        "decoder_feed_gain": jnp.clip(1.0 + 0.15 * jax.random.normal(seeds[13], (DD,), jnp.float32), 0.25, 1.75).astype(jnp.bfloat16),
        "w_up": scatter_about(seeds[14], (DD, DFF), DD ** -0.5, 0.25),
        "w_down": scatter_about(seeds[15], (DFF, DD), DFF ** -0.5, 0.125),
        "head_gain": jnp.clip(1.0 + 0.15 * jax.random.normal(seeds[16], (DD,), jnp.float32), 0.25, 1.75).astype(jnp.bfloat16),
        "w_head": scatter_about(seeds[17], (DD, PIX), DD ** -0.5, 0.25),
        "visible_rows": draw_visible_rows(jax.random.fold_in(seeds[21], 71), 0),
        "visible_count": draw_visible_count(jax.random.fold_in(seeds[21], 71), 0),
        "owner_slot": draw_owner_slot(jax.random.fold_in(seeds[21], 71), 0),
    }


def layer_norm(x, gain):
    row_mean = lax.optimization_barrier(jnp.mean(x, axis=-1, keepdims=True))
    centered_input = x - row_mean
    var = lax.optimization_barrier(jnp.mean(centered_input * centered_input, axis=-1, keepdims=True))
    return centered_input * lax.rsqrt(var + 1e-06) * gain.astype(jnp.float32)

def norm_backward(z, gain, upstream):
    row_mean = lax.optimization_barrier(jnp.mean(z, axis=-1, keepdims=True))
    centered_input = z - row_mean
    inverse_scale = lax.rsqrt(lax.optimization_barrier(jnp.mean(centered_input * centered_input, axis=-1, keepdims=True)) + 1e-06)
    normalized_input = centered_input * inverse_scale
    input_gradient = upstream * gain.astype(jnp.float32)
    return inverse_scale * (input_gradient - lax.optimization_barrier(jnp.mean(input_gradient, axis=-1, keepdims=True)) - normalized_input * lax.optimization_barrier(jnp.mean(input_gradient * normalized_input, axis=-1, keepdims=True)))

def attend(queries, keys, values, heads, block):
    rows = queries.shape[0]
    width = queries.shape[1]
    size = width // heads
    q_heads = queries.reshape(rows // block, block, heads, size).transpose(2, 0, 1, 3)
    k_heads = keys.reshape(-1, heads, size).transpose(1, 0, 2)
    v_heads = values.reshape(-1, heads, size).transpose(1, 0, 2)

    def one_head(items):
        q_one, k_one, v_one = items

        def one_block(q_block):
            score = jnp.dot(q_block, k_one.T, preferred_element_type=jnp.float32) * size ** (-0.5)
            top = lax.optimization_barrier(jnp.max(score, axis=1, keepdims=True))
            weight = jnp.exp(score - top)
            weight = (weight / lax.optimization_barrier(jnp.sum(weight, axis=1, keepdims=True))).astype(jnp.bfloat16)
            return jnp.dot(weight, v_one, preferred_element_type=jnp.float32).astype(jnp.bfloat16)
        return lax.map(one_block, q_one)
    out = lax.map(one_head, (q_heads, k_heads, v_heads))
    return out.transpose(1, 2, 0, 3).reshape(rows, width)

def reference(patches, enc_pos, w_embed, enc_gain, w_qkv, w_out, enc_out_gain, w_dec_embed, mask_token, dec_pos, dec_attn_gain, decoder_query_key_value_weight, w_dec_out, decoder_feed_gain, w_up, w_down, head_gain, w_head, visible_rows, visible_count, owner_slot):
    enc_width = EH * HD
    dec_width = DH * DHD
    grad_head = jnp.zeros((DD, PIX), jnp.float32)
    grad_dec_out = jnp.zeros((dec_width, DD), jnp.float32)
    loss_sum = jnp.zeros((), jnp.float32)
    outputs = []
    for gather_id in range(GATHERS):
        slot_rows = visible_rows[gather_id].reshape(N_CTX, CAP)
        counts = visible_count[gather_id]
        valid = jnp.arange(CAP, dtype=jnp.int32)[None, :] < counts[:, None]
        ids = (jnp.arange(N_CTX, dtype=jnp.int32)[:, None] * PDEV + jnp.maximum(slot_rows, 0)).reshape(-1)
        order = jnp.argsort(jnp.where(valid, 0, 1).reshape(-1).astype(jnp.int32), stable=True)[:VIS_DEV * N_CTX]
        vis_ids = ids[order].astype(jnp.int32)
        source = patches[gather_id]
        tokens = (jnp.dot(source[vis_ids], w_embed, preferred_element_type=jnp.float32) + enc_pos[vis_ids].astype(jnp.float32)).astype(jnp.bfloat16)
        normed = layer_norm(tokens.astype(jnp.float32), enc_gain).astype(jnp.bfloat16)
        qkv = jnp.dot(normed, w_qkv, preferred_element_type=jnp.float32).astype(jnp.bfloat16)
        attended = attend(qkv[:, :enc_width], qkv[:, enc_width:2 * enc_width], qkv[:, 2 * enc_width:], EH, VIS_DEV)
        encoded = tokens.astype(jnp.float32) + jnp.dot(attended, w_out, preferred_element_type=jnp.float32)
        dec_normed = layer_norm(encoded, enc_out_gain).astype(jnp.bfloat16)
        dec_tok = jnp.dot(dec_normed, w_dec_embed, preferred_element_type=jnp.float32).astype(jnp.bfloat16)
        filled = jnp.broadcast_to(mask_token.astype(jnp.float32)[None, :], (NP, DD))
        filled = filled.at[vis_ids].set(dec_tok.astype(jnp.float32))
        decoder_in = (filled + dec_pos.astype(jnp.float32)).astype(jnp.bfloat16)
        masked = jnp.ones((NP,), jnp.float32).at[vis_ids].set(0.0)
        owners = owner_slot[gather_id]
        y_own = jnp.zeros((NP, DD), jnp.bfloat16).at[owners].set(decoder_in)
        target = jnp.zeros((NP, PIX), jnp.bfloat16).at[owners].set(source)
        flag = jnp.zeros((NP,), jnp.float32).at[owners].set(masked)
        attn_in = layer_norm(y_own.astype(jnp.float32), dec_attn_gain).astype(jnp.bfloat16)
        dec_qkv = jnp.dot(attn_in, decoder_query_key_value_weight, preferred_element_type=jnp.float32).astype(jnp.bfloat16)
        dec_att = attend(dec_qkv[:, :dec_width], dec_qkv[:, dec_width:2 * dec_width], dec_qkv[:, 2 * dec_width:], DH, PDEV)
        y_mid = y_own.astype(jnp.float32) + jnp.dot(dec_att, w_dec_out, preferred_element_type=jnp.float32)
        first = layer_norm(y_mid, decoder_feed_gain).astype(jnp.bfloat16)
        pre_act = jnp.dot(first, w_up, preferred_element_type=jnp.float32)
        act = jax.nn.gelu(pre_act).astype(jnp.bfloat16)
        z = y_mid + jnp.dot(act, w_down, preferred_element_type=jnp.float32)
        zn = layer_norm(z, head_gain).astype(jnp.bfloat16)
        pred = jnp.dot(zn, w_head, preferred_element_type=jnp.float32)
        outputs.append(pred.astype(jnp.bfloat16))
        err = (pred - target.astype(jnp.float32)) * flag[:, None]
        loss_sum = loss_sum + jnp.sum(err * err) / PIX
        dpred = (err * (2.0 / PIX)).astype(jnp.bfloat16)
        grad_head = grad_head + jnp.dot(zn.T, dpred, preferred_element_type=jnp.float32)
        upstream = jnp.dot(dpred, w_head.T, preferred_element_type=jnp.float32)
        dz = norm_backward(z, head_gain, upstream).astype(jnp.bfloat16)
        back_act = jnp.dot(dz, w_down.T, preferred_element_type=jnp.float32)
        gelu_back = jax.vjp(jax.nn.gelu, pre_act)[1]
        pre_grad = gelu_back(back_act)[0].astype(jnp.bfloat16)
        back_first = jnp.dot(pre_grad, w_up.T, preferred_element_type=jnp.float32)
        mid_grad = (dz.astype(jnp.float32) + norm_backward(y_mid, decoder_feed_gain, back_first)).astype(jnp.bfloat16)
        grad_dec_out = grad_dec_out + jnp.dot(dec_att.T, mid_grad, preferred_element_type=jnp.float32)
    masked_total = GATHERS * (NP - VIS_DEV * N_CTX)
    return (jnp.stack(outputs), grad_head, grad_dec_out, loss_sum / masked_total)
```

```python
import functools
import math

import jax
import jax.numpy as jnp
from jax import lax
from jax.experimental import pallas as pl
from jax.experimental.pallas import tpu as pltpu
from jax.sharding import PartitionSpec as P

HEADS = 8
BF = jnp.bfloat16
F32 = jnp.float32
LOG2E = math.log2(math.e)
VMEM_LIMIT = 56 << 20


def layer_norm(x, gain):
    row_mean = jnp.mean(x, axis=-1, keepdims=True)
    centered_input = x - row_mean
    var = jnp.mean(centered_input * centered_input, axis=-1, keepdims=True)
    return centered_input * lax.rsqrt(var + 1e-06) * gain.astype(F32)


def norm_backward(z, gain, upstream):
    row_mean = jnp.mean(z, axis=-1, keepdims=True)
    centered_input = z - row_mean
    inverse_scale = lax.rsqrt(
        jnp.mean(centered_input * centered_input, axis=-1, keepdims=True) + 1e-06
    )
    normalized_input = centered_input * inverse_scale
    input_gradient = upstream * gain.astype(F32)
    return inverse_scale * (
        input_gradient
        - jnp.mean(input_gradient, axis=-1, keepdims=True)
        - normalized_input * jnp.mean(input_gradient * normalized_input, axis=-1, keepdims=True)
    )


def dot(a, b):
    return jnp.dot(a, b, preferred_element_type=F32)


def dot_t(a, b):
    return lax.dot_general(a, b, (((1,), (1,)), ((), ())), preferred_element_type=F32)


def swap_halves(x):
    half = x.shape[1] // 2
    return jnp.concatenate([x[:, half:], x[:, :half]], axis=1)


def slot_of_row(slots_row):
    size = slots_row.shape[1]
    row = lax.broadcasted_iota(jnp.int32, (size, size), 0)
    return jnp.where(row == slots_row, 1.0, 0.0)


def embed_kernel(
    patch_ref, pos_ref, w_embed_ref, gain_ref, w_qkv_ref, slots_ref,
    send_ref, tok_ref, normed_ref, qkv_ref,
):
    rows, width = patch_ref.shape
    half = rows // 2
    att = w_qkv_ref.shape[1] // 3
    size = att // HEADS
    tile = 256

    @pl.loop(0, width // tile)
    def _(step):
        cols = pl.ds(pl.multiple_of(step * tile, tile), tile)
        tok_ref[:, cols] = (
            dot(patch_ref[...], w_embed_ref[:, cols]) + pos_ref[:, cols].astype(F32)
        ).astype(BF)

    normed_ref[...] = layer_norm(tok_ref[...].astype(F32), gain_ref[...]).astype(BF)
    pick = slot_of_row(slots_ref[...]).astype(BF)

    @pl.loop(0, 3 * att // tile)
    def _(step):
        cols = pl.ds(pl.multiple_of(step * tile, tile), tile)
        part = dot(normed_ref[...], w_qkv_ref[:, cols]).astype(BF)
        qkv_ref[:, cols] = lax.dot_general(
            pick, part, (((0,), (0,)), ((), ())), preferred_element_type=F32
        ).astype(BF)

    count = jnp.sum(jnp.where(slots_ref[...] >= 0, 1.0, 0.0), axis=1, keepdims=True)
    high = jnp.floor(count * (1.0 / 16))
    lane = lax.broadcasted_iota(jnp.int32, (16, 128), 1)
    info = jnp.where(lane < 64, high, count - 16.0 * high).astype(BF)
    for head in range(HEADS):
        at = head * size
        q = qkv_ref[:, at : at + size]
        k = qkv_ref[:, att + at : att + at + size]
        v = qkv_ref[:, 2 * att + at : 2 * att + at + size]
        send_ref[head, :half, :] = jnp.concatenate([q[:half], q[half:]], axis=1)
        send_ref[head, half : half + rows, :] = jnp.concatenate([k, v], axis=1)
        send_ref[head, half + rows :, :] = info


def enc_attend_kernel(
    first_ref, q_ref, kv_ref, out_ref, q_buf, kv_buf, o_buf, *, q_at, kv_at, rows, cap_q, cap_k
):
    half = rows // 2
    sources = kv_ref.shape[0]
    lane16 = lax.broadcasted_iota(jnp.int32, (16, 128), 1)
    lane_h = lax.broadcasted_iota(jnp.int32, (half, 128), 1)

    def count_of(source):
        info = kv_ref[source, kv_at + rows : kv_at + rows + 16, :].astype(F32)
        high = jnp.max(jnp.where(lane16 < 64, info, 0.0)).astype(jnp.int32)
        low = jnp.max(jnp.where(lane16 >= 64, info, 0.0)).astype(jnp.int32)
        return high * 16 + low

    q_buf[...] = jnp.zeros_like(q_buf)
    o_buf[...] = jnp.zeros_like(o_buf)
    kv_buf[:, :128] = jnp.zeros((kv_buf.shape[0], 128), BF)
    kv_buf[:, 128:] = jnp.ones((kv_buf.shape[0], 128), BF)

    key = lax.broadcasted_iota(jnp.int32, (1, cap_k), 1)
    valid = jnp.zeros((1, cap_k), F32)
    off = jnp.int32(0)
    for source in range(sources):
        count = count_of(source)
        off = pl.multiple_of(off, 16)
        kv_buf[pl.ds(off, rows), :128] = kv_ref[source, kv_at : kv_at + rows, :]
        valid = jnp.where((key >= off) & (key < off + count), 1.0, valid)
        off = off + (count + 15) // 16 * 16
    bias = jnp.where(valid > 0.0, 0.0, -1e30)

    offs = []
    off = jnp.int32(0)
    for source in range(HEADS):
        off = pl.multiple_of(off, 16)
        offs.append(off)
        block = q_ref[source, q_at : q_at + half, :]
        zero = jnp.zeros_like(block)
        q_buf[pl.ds(off, half), :] = jnp.where(lane_h < 64, block, zero)
        q_buf[pl.ds(off + half, half), :] = jnp.where(lane_h < 64, swap_halves(block), zero)
        off = off + (count_of(first_ref[0] + source) + 15) // 16 * 16
    total = off

    tile = 128
    scale = LOG2E * 64**-0.5

    @pl.loop(0, cap_q // tile)
    def _(step):
        @pl.when(step * tile < total)
        def _():
            at = pl.ds(pl.multiple_of(step * tile, tile), tile)
            score = dot_t(q_buf[at, :], kv_buf[:cap_k, :128]) + bias
            top = jnp.max(score, axis=1, keepdims=True)
            weight = jnp.exp2((score - top) * scale).astype(BF)
            mixed = dot(weight, kv_buf[:cap_k, :])
            o_buf[at, :] = (mixed[:, :128] / mixed[:, 128:]).astype(BF)

    for source in range(HEADS):
        upper = o_buf[pl.ds(offs[source], half), :]
        lower = o_buf[pl.ds(pl.multiple_of(offs[source] + half, 16), half), :]
        out_ref[source] = jnp.where(lane_h < 64, swap_halves(upper), lower)


def middle_kernel(
    att_ref, tok_ref, w_out_ref, out_gain_ref, w_dec_ref, mask_ref, pos_ref, gain_ref,
    w_qkv_ref, slots_ref, owner_ref, patch_ref,
    send_ref, y_ref, target_ref, flag_ref, att_buf, qkv_buf, *, groups,
):
    rows, width = tok_ref.shape
    half = rows // 2
    block = rows // groups
    for pair in range(HEADS // 2):
        a, b = att_ref[2 * pair], att_ref[2 * pair + 1]
        cols = slice(128 * pair, 128 * pair + 128)
        att_buf[:half, cols] = jnp.concatenate([a[:, :64], b[:, :64]], axis=1)
        att_buf[half:, cols] = jnp.concatenate([a[:, 64:], b[:, 64:]], axis=1)
    pick = slot_of_row(slots_ref[...])
    seen = jnp.sum(pick, axis=1, keepdims=True)
    attended = dot(pick.astype(BF), att_buf[...]).astype(BF)
    encoded = tok_ref[...].astype(F32) + dot(attended, w_out_ref[...])
    dec_normed = layer_norm(encoded, out_gain_ref[...]).astype(BF)
    dec_tok = dot(dec_normed, w_dec_ref[...]).astype(BF).astype(F32)
    filled = jnp.where(seen > 0.0, dec_tok, mask_ref[...].astype(F32))
    decoder_in = (filled + pos_ref[...].astype(F32)).astype(BF)

    owner = owner_ref[...]
    dest = jnp.zeros_like(owner)
    for device in range(1, groups):
        dest = dest + jnp.where(owner >= device * rows, 1, 0)
    local = owner - dest * rows
    first = jnp.min(local.astype(F32), axis=1, keepdims=True).astype(jnp.int32)
    place = dest * block + local - first
    move = slot_of_row(place).astype(BF)
    y = dot(move, decoder_in)
    y_ref[...] = y.astype(BF)
    target_ref[...] = dot(move, patch_ref[...]).astype(BF)
    hidden = jnp.broadcast_to(1.0 - seen, (rows, 128)).astype(BF)
    flag_ref[...] = dot(move, hidden)
    attn_in = layer_norm(y, gain_ref[...]).astype(BF)
    qkv_buf[...] = dot(attn_in, w_qkv_ref[...]).astype(BF).astype(F32)
    att = w_qkv_ref.shape[1] // 3
    size = att // HEADS
    quarter = rows // 4
    for head in range(HEADS):
        at = head * size
        q = qkv_buf[:, at : at + size]
        k = qkv_buf[:, att + at : att + at + size]
        v = qkv_buf[:, 2 * att + at : 2 * att + at + size]
        send_ref[head, :half, :] = jnp.concatenate(
            [k[:half], v[:half], k[half:], v[half:]], axis=1
        ).astype(BF)
        send_ref[head, half:, :] = jnp.concatenate(
            [q[i * quarter : (i + 1) * quarter] for i in range(4)], axis=1
        ).astype(BF)


def dec_attend_kernel(q_ref, kv_ref, out_ref, k_buf, v_buf, *, q_at, rows):
    half = rows // 2
    quarter = rows // 4
    sources = kv_ref.shape[0]
    for source in range(sources):
        for part in range(2):
            block = kv_ref[source, :half, 64 * part : 64 * part + 64]
            at = source * rows + part * half
            k, v = block[:, :32], block[:, 32:]
            k_buf[at : at + half, :] = jnp.concatenate([k, k, k, k], axis=1)
            v_buf[at : at + half, :128] = jnp.concatenate([v, v, v, v], axis=1)
    v_buf[:, 128:] = jnp.ones((v_buf.shape[0], 128), BF)
    scale = LOG2E * 32**-0.5
    lane = lax.broadcasted_iota(jnp.int32, (quarter, 128), 1)
    zone = [(lane >= 32 * i) & (lane < 32 * i + 32) for i in range(4)]

    @pl.loop(0, HEADS)
    def _(source):
        block = q_ref[source, q_at : q_at + quarter, :].astype(F32)
        q = jnp.concatenate([jnp.where(z, block, 0.0) for z in zone], axis=0).astype(BF)
        score = dot_t(q, k_buf[...])
        top = jnp.max(score, axis=1, keepdims=True)
        weight = jnp.exp2((score - top) * scale).astype(BF)
        mixed = dot(weight, v_buf[...])
        mixed = mixed[:, :128] / mixed[:, 128:]
        out = mixed[:quarter]
        for i in range(1, 4):
            out = jnp.where(zone[i], mixed[i * quarter : (i + 1) * quarter], out)
        out_ref[source] = out.astype(BF)


def vmem_call(kernel, outs, scratch, inputs, smem=(), flops=0):
    space = [
        pl.BlockSpec(memory_space=pltpu.SMEM if i in smem else pltpu.VMEM)
        for i in range(len(inputs))
    ]
    moved = sum(a.size * a.dtype.itemsize for a in inputs)
    return pl.pallas_call(
        kernel,
        out_shape=outs,
        in_specs=space,
        out_specs=[pl.BlockSpec(memory_space=pltpu.VMEM)] * len(outs),
        scratch_shapes=scratch,
        compiler_params=pltpu.CompilerParams(vmem_limit_bytes=VMEM_LIMIT),
        cost_estimate=pl.CostEstimate(flops=flops, bytes_accessed=moved, transcendentals=0),
    )(*inputs)


def swap(x, axis, groups=None):
    return lax.all_to_all(
        x, axis, split_axis=0, concat_axis=0, tiled=True, axis_index_groups=groups
    )


def all_sum(x, groups):
    size = lax.axis_size("dp")
    me = lax.axis_index("dp")
    stages = []
    step = 1
    while step < size:
        pairs = [(i, i ^ step) for i in range(size)]
        upper = (me // step) % 2
        half = x.shape[0] // 2
        mine = lax.dynamic_slice_in_dim(x, upper * half, half, 0)
        other = lax.dynamic_slice_in_dim(x, (1 - upper) * half, half, 0)
        x = mine + lax.ppermute(other, "dp", pairs)
        stages.append((pairs, upper))
        step *= 2
    rows, width = x.shape
    blocks = swap(x.reshape(groups, rows // groups, width), "ctx")
    total = jnp.sum(blocks.astype(F32), axis=0).astype(BF)
    x = swap(jnp.broadcast_to(total[None], blocks.shape), "ctx").reshape(rows, width)
    for pairs, upper in reversed(stages):
        other = lax.ppermute(x, "dp", pairs)
        low = jnp.where(upper == 0, x, other)
        high = jnp.where(upper == 0, other, x)
        x = jnp.concatenate([low, high], axis=0)
    return x


def on_device(
    patches,
    enc_pos,
    w_embed,
    enc_gain,
    w_qkv,
    w_out,
    enc_out_gain,
    w_dec_embed,
    mask_token,
    dec_pos,
    dec_attn_gain,
    decoder_query_key_value_weight,
    w_dec_out,
    decoder_feed_gain,
    w_up,
    w_down,
    head_gain,
    w_head,
    visible_rows,
    visible_count,
    owner_slot,
):
    groups = lax.axis_size("ctx")
    repeat = groups // HEADS
    teams = [list(range(HEADS * i, HEADS * i + HEADS)) for i in range(repeat)]
    teams = None if repeat == 1 else teams
    source = patches[0]
    rows, pixels = source.shape
    half, quarter = rows // 2, rows // 4
    share = rows // 3
    width = w_embed.shape[1]
    dec_width = w_dec_embed.shape[1]
    row = lambda vector: vector.reshape(1, -1)
    shape = jax.ShapeDtypeStruct

    send, tok = vmem_call(
        embed_kernel,
        [shape((HEADS, half + rows + 16, 128), BF), shape((rows, width), BF)],
        [pltpu.VMEM((rows, width), BF), pltpu.VMEM((rows, w_qkv.shape[1]), BF)],
        [source, enc_pos, w_embed, row(enc_gain), w_qkv, visible_rows],
        flops=2 * rows * width * (pixels + w_qkv.shape[1]),
    )
    first = (lax.axis_index("ctx") // HEADS * HEADS).astype(jnp.int32).reshape(1)
    if repeat == 1:
        q = kv = swap(send, "ctx")
        q_at, kv_at = 0, half
    else:
        q = swap(send[:, :half], "ctx", teams)
        kv = swap(jnp.tile(send[:, half:], (repeat, 1, 1)), "ctx")
        q_at, kv_at = 0, 0
    cap_k = (share + 16) * groups
    cap_q = min(HEADS * rows, cap_k)
    (att,) = vmem_call(
        functools.partial(
            enc_attend_kernel, q_at=q_at, kv_at=kv_at, rows=rows, cap_q=cap_q, cap_k=cap_k
        ),
        [shape((HEADS, half, 128), BF)],
        [
            pltpu.VMEM((cap_q + rows, 128), BF),
            pltpu.VMEM((cap_k + rows, 256), BF),
            pltpu.VMEM((cap_q + rows, 128), BF),
        ],
        [first, q, kv],
        smem=(0,),
        flops=4 * cap_q * cap_k * 128,
    )
    att = swap(att, "ctx", teams)
    send, y_own, target, flag = vmem_call(
        functools.partial(middle_kernel, groups=groups),
        [
            shape((HEADS, half + quarter, 128), BF),
            shape((rows, dec_width), BF),
            shape((rows, pixels), BF),
            shape((rows, 128), F32),
        ],
        [
            pltpu.VMEM((rows, w_out.shape[0]), BF),
            pltpu.VMEM((rows, decoder_query_key_value_weight.shape[1]), F32),
        ],
        [
            att, tok, w_out, row(enc_out_gain), w_dec_embed, row(mask_token), dec_pos,
            row(dec_attn_gain), decoder_query_key_value_weight, visible_rows, owner_slot, source,
        ],
        flops=2 * rows * width * 1024,
    )
    if repeat == 1:
        q = kv = swap(send, "ctx")
        q_at = half
    else:
        q = swap(send[:, half:], "ctx", teams)
        kv = swap(jnp.tile(send[:, :half], (repeat, 1, 1)), "ctx")
        q_at = 0
    (att,) = vmem_call(
        functools.partial(dec_attend_kernel, q_at=q_at, rows=rows),
        [shape((HEADS, quarter, 128), BF)],
        [pltpu.VMEM((groups * rows, 128), BF), pltpu.VMEM((groups * rows, 256), BF)],
        [q, kv],
        flops=4 * HEADS * rows * groups * rows * 128,
    )
    att = swap(att, "ctx", teams)
    dec_att = (
        att.reshape(HEADS, quarter, 4, 32).transpose(2, 1, 0, 3).reshape(rows, w_dec_out.shape[0])
    )
    y_mid = y_own.astype(F32) + dot(dec_att, w_dec_out)
    feed = layer_norm(y_mid, decoder_feed_gain).astype(BF)
    pre_act = dot(feed, w_up)
    act = jax.nn.gelu(pre_act).astype(BF)
    z = y_mid + dot(act, w_down)
    zn = layer_norm(z, head_gain).astype(BF)
    pred = dot(zn, w_head)
    err = (pred - target.astype(F32)) * flag[:, :1]
    reconstruction = swap(pred.astype(BF).reshape(groups, rows // groups, pixels), "ctx")
    loss_part = jnp.sum(err * err) / pixels
    dpred = (err * (2.0 / pixels)).astype(BF)
    head_part = dot(zn.T, dpred)
    upstream = dot_t(dpred, w_head)
    dz = norm_backward(z, head_gain, upstream).astype(BF)
    back_act = dot_t(dz, w_down)
    gelu_back = jax.vjp(jax.nn.gelu, pre_act)[1]
    pre_grad = gelu_back(back_act)[0].astype(BF)
    back_feed = dot_t(pre_grad, w_up)
    mid_grad = (dz.astype(F32) + norm_backward(y_mid, decoder_feed_gain, back_feed)).astype(BF)
    out_part = dot(dec_att.T, mid_grad)

    depth = out_part.shape[0] // 2
    loss_high = loss_part.astype(BF)
    loss_low = (loss_part - loss_high.astype(F32)).astype(BF)
    used = dec_width + depth + 2
    unit = lax.axis_size("dp") * groups
    padded = -(-used // unit) * unit
    stacked = jnp.concatenate(
        [
            head_part.astype(BF),
            jnp.concatenate([out_part[:depth], out_part[depth:]], axis=1).astype(BF),
            jnp.broadcast_to(loss_high, (1, pixels)),
            jnp.broadcast_to(loss_low, (1, pixels)),
            jnp.zeros((padded - used, pixels), BF),
        ],
        axis=0,
    )
    total = all_sum(stacked, groups)
    grad_head = total[:dec_width].astype(F32)
    tail = total[dec_width : dec_width + depth].astype(F32)
    grad_dec_out = jnp.concatenate([tail[:, :dec_width], tail[:, dec_width:]], axis=0)
    loss = total[used - 2, 0].astype(F32) + total[used - 1, 0].astype(F32)
    masked_total = lax.axis_size("dp") * (groups * rows - share * groups)
    return (reconstruction.reshape(1, rows, pixels), grad_head, grad_dec_out, loss / masked_total)


def solution(mesh):
    in_specs = (
        P("dp", "ctx", None),
        P("ctx", None),
        P(),
        P(),
        P(),
        P(),
        P(),
        P(),
        P(),
        P("ctx", None),
        P(),
        P(),
        P(),
        P(),
        P(),
        P(),
        P(),
        P(),
        P("dp", "ctx"),
        P("dp", "ctx"),
        P("dp", "ctx"),
    )
    out_specs = (P("dp", "ctx", None), P(), P(), P())
    return jax.shard_map(
        on_device, mesh=mesh, in_specs=in_specs, out_specs=out_specs, check_vma=False
    )
```

```python
import functools
import math

import jax
import jax.numpy as jnp
from jax import lax
from jax.experimental import pallas as pl
from jax.experimental.pallas import tpu as pltpu
from jax.sharding import PartitionSpec as P

HEADS = 8
BF = jnp.bfloat16
F32 = jnp.float32
LOG2E = math.log2(math.e)
VMEM_LIMIT = 56 << 20


def layer_norm(x, gain):
    row_mean = jnp.mean(x, axis=-1, keepdims=True)
    centered_input = x - row_mean
    var = jnp.mean(centered_input * centered_input, axis=-1, keepdims=True)
    return centered_input * lax.rsqrt(var + 1e-06) * gain.astype(F32)


def norm_backward(z, gain, upstream):
    row_mean = jnp.mean(z, axis=-1, keepdims=True)
    centered_input = z - row_mean
    inverse_scale = lax.rsqrt(
        jnp.mean(centered_input * centered_input, axis=-1, keepdims=True) + 1e-06
    )
    normalized_input = centered_input * inverse_scale
    input_gradient = upstream * gain.astype(F32)
    return inverse_scale * (
        input_gradient
        - jnp.mean(input_gradient, axis=-1, keepdims=True)
        - normalized_input * jnp.mean(input_gradient * normalized_input, axis=-1, keepdims=True)
    )


def dot(a, b):
    return jnp.dot(a, b, preferred_element_type=F32)


def dot_t(a, b):
    return lax.dot_general(a, b, (((1,), (1,)), ((), ())), preferred_element_type=F32)


def swap_halves(x):
    half = x.shape[1] // 2
    return jnp.concatenate([x[:, half:], x[:, :half]], axis=1)


def slot_of_row(slots_row):
    size = slots_row.shape[1]
    row = lax.broadcasted_iota(jnp.int32, (size, size), 0)
    return jnp.where(row == slots_row, 1.0, 0.0)


def embed_kernel(
    patch_ref, pos_ref, w_embed_ref, gain_ref, w_qkv_ref, slots_ref,
    send_ref, tok_ref, normed_ref, qkv_ref,
):
    rows, width = patch_ref.shape
    half = rows // 2
    att = w_qkv_ref.shape[1] // 3
    size = att // HEADS
    tile = 256

    @pl.loop(0, width // tile)
    def _(step):
        cols = pl.ds(pl.multiple_of(step * tile, tile), tile)
        tok_ref[:, cols] = (
            dot(patch_ref[...], w_embed_ref[:, cols]) + pos_ref[:, cols].astype(F32)
        ).astype(BF)

    normed_ref[...] = layer_norm(tok_ref[...].astype(F32), gain_ref[...]).astype(BF)
    pick = slot_of_row(slots_ref[...]).astype(BF)

    @pl.loop(0, 3 * att // tile)
    def _(step):
        cols = pl.ds(pl.multiple_of(step * tile, tile), tile)
        part = dot(normed_ref[...], w_qkv_ref[:, cols]).astype(BF)
        qkv_ref[:, cols] = lax.dot_general(
            pick, part, (((0,), (0,)), ((), ())), preferred_element_type=F32
        ).astype(BF)

    count = jnp.sum(jnp.where(slots_ref[...] >= 0, 1.0, 0.0), axis=1, keepdims=True)
    high = jnp.floor(count * (1.0 / 16))
    lane = lax.broadcasted_iota(jnp.int32, (16, 128), 1)
    info = jnp.where(lane < 64, high, count - 16.0 * high).astype(BF)
    for head in range(HEADS):
        at = head * size
        q = qkv_ref[:, at : at + size]
        k = qkv_ref[:, att + at : att + at + size]
        v = qkv_ref[:, 2 * att + at : 2 * att + at + size]
        send_ref[head, :half, :] = jnp.concatenate([q[:half], q[half:]], axis=1)
        send_ref[head, half : half + rows, :] = jnp.concatenate([k, v], axis=1)
        send_ref[head, half + rows :, :] = info


def enc_attend_kernel(
    first_ref, q_ref, kv_ref, out_ref, q_buf, kv_buf, o_buf, *, q_at, kv_at, rows, cap_q, cap_k
):
    half = rows // 2
    sources = kv_ref.shape[0]
    lane16 = lax.broadcasted_iota(jnp.int32, (16, 128), 1)
    lane_h = lax.broadcasted_iota(jnp.int32, (half, 128), 1)

    def count_of(source):
        info = kv_ref[source, kv_at + rows : kv_at + rows + 16, :].astype(F32)
        high = jnp.max(jnp.where(lane16 < 64, info, 0.0)).astype(jnp.int32)
        low = jnp.max(jnp.where(lane16 >= 64, info, 0.0)).astype(jnp.int32)
        return high * 16 + low

    q_buf[...] = jnp.zeros_like(q_buf)
    o_buf[...] = jnp.zeros_like(o_buf)
    kv_buf[:, :128] = jnp.zeros((kv_buf.shape[0], 128), BF)
    kv_buf[:, 128:] = jnp.ones((kv_buf.shape[0], 128), BF)

    key = lax.broadcasted_iota(jnp.int32, (1, cap_k), 1)
    valid = jnp.zeros((1, cap_k), F32)
    off = jnp.int32(0)
    for source in range(sources):
        count = count_of(source)
        off = pl.multiple_of(off, 16)
        kv_buf[pl.ds(off, rows), :128] = kv_ref[source, kv_at : kv_at + rows, :]
        valid = jnp.where((key >= off) & (key < off + count), 1.0, valid)
        off = off + (count + 15) // 16 * 16
    bias = jnp.where(valid > 0.0, 0.0, -1e30)

    offs = []
    off = jnp.int32(0)
    for source in range(HEADS):
        off = pl.multiple_of(off, 16)
        offs.append(off)
        block = q_ref[source, q_at : q_at + half, :]
        zero = jnp.zeros_like(block)
        q_buf[pl.ds(off, half), :] = jnp.where(lane_h < 64, block, zero)
        q_buf[pl.ds(off + half, half), :] = jnp.where(lane_h < 64, swap_halves(block), zero)
        off = off + (count_of(first_ref[0] + source) + 15) // 16 * 16
    total = off

    tile = 128
    scale = LOG2E * 64**-0.5

    @pl.loop(0, cap_q // tile)
    def _(step):
        @pl.when(step * tile < total)
        def _():
            at = pl.ds(pl.multiple_of(step * tile, tile), tile)
            score = dot_t(q_buf[at, :], kv_buf[:cap_k, :128]) + bias
            top = jnp.max(score, axis=1, keepdims=True)
            weight = jnp.exp2((score - top) * scale).astype(BF)
            mixed = dot(weight, kv_buf[:cap_k, :])
            o_buf[at, :] = (mixed[:, :128] / mixed[:, 128:]).astype(BF)

    for source in range(HEADS):
        upper = o_buf[pl.ds(offs[source], half), :]
        lower = o_buf[pl.ds(pl.multiple_of(offs[source] + half, 16), half), :]
        out_ref[source] = jnp.where(lane_h < 64, swap_halves(upper), lower)


def middle_kernel(
    att_ref, tok_ref, w_out_ref, out_gain_ref, w_dec_ref, mask_ref, pos_ref, gain_ref,
    w_qkv_ref, slots_ref, owner_ref, patch_ref,
    send_ref, y_ref, target_ref, flag_ref, att_buf, qkv_buf, *, groups,
):
    rows, width = tok_ref.shape
    half = rows // 2
    block = rows // groups
    for pair in range(HEADS // 2):
        a, b = att_ref[2 * pair], att_ref[2 * pair + 1]
        cols = slice(128 * pair, 128 * pair + 128)
        att_buf[:half, cols] = jnp.concatenate([a[:, :64], b[:, :64]], axis=1)
        att_buf[half:, cols] = jnp.concatenate([a[:, 64:], b[:, 64:]], axis=1)
    pick = slot_of_row(slots_ref[...])
    seen = jnp.sum(pick, axis=1, keepdims=True)
    attended = dot(pick.astype(BF), att_buf[...]).astype(BF)
    encoded = tok_ref[...].astype(F32) + dot(attended, w_out_ref[...])
    dec_normed = layer_norm(encoded, out_gain_ref[...]).astype(BF)
    dec_tok = dot(dec_normed, w_dec_ref[...]).astype(BF).astype(F32)
    filled = jnp.where(seen > 0.0, dec_tok, mask_ref[...].astype(F32))
    decoder_in = (filled + pos_ref[...].astype(F32)).astype(BF)

    owner = owner_ref[...]
    dest = jnp.zeros_like(owner)
    for device in range(1, groups):
        dest = dest + jnp.where(owner >= device * rows, 1, 0)
    local = owner - dest * rows
    first = jnp.min(local.astype(F32), axis=1, keepdims=True).astype(jnp.int32)
    place = dest * block + local - first
    move = slot_of_row(place).astype(BF)
    y = dot(move, decoder_in)
    y_ref[...] = y.astype(BF)
    target_ref[...] = dot(move, patch_ref[...]).astype(BF)
    hidden = jnp.broadcast_to(1.0 - seen, (rows, 128)).astype(BF)
    flag_ref[...] = dot(move, hidden)
    attn_in = layer_norm(y, gain_ref[...]).astype(BF)
    qkv_buf[...] = dot(attn_in, w_qkv_ref[...]).astype(BF).astype(F32)
    att = w_qkv_ref.shape[1] // 3
    size = att // HEADS
    quarter = rows // 4
    for head in range(HEADS):
        at = head * size
        q = qkv_buf[:, at : at + size]
        k = qkv_buf[:, att + at : att + at + size]
        v = qkv_buf[:, 2 * att + at : 2 * att + at + size]
        send_ref[head, :half, :] = jnp.concatenate(
            [k[:half], v[:half], k[half:], v[half:]], axis=1
        ).astype(BF)
        send_ref[head, half:, :] = jnp.concatenate(
            [q[i * quarter : (i + 1) * quarter] for i in range(4)], axis=1
        ).astype(BF)


def dec_attend_kernel(q_ref, kv_ref, out_ref, k_buf, v_buf, *, q_at, rows):
    half = rows // 2
    quarter = rows // 4
    sources = kv_ref.shape[0]
    for source in range(sources):
        for part in range(2):
            block = kv_ref[source, :half, 64 * part : 64 * part + 64]
            at = source * rows + part * half
            k, v = block[:, :32], block[:, 32:]
            k_buf[at : at + half, :] = jnp.concatenate([k, k, k, k], axis=1)
            v_buf[at : at + half, :128] = jnp.concatenate([v, v, v, v], axis=1)
    v_buf[:, 128:] = jnp.ones((v_buf.shape[0], 128), BF)
    scale = LOG2E * 32**-0.5
    lane = lax.broadcasted_iota(jnp.int32, (quarter, 128), 1)
    zone = [(lane >= 32 * i) & (lane < 32 * i + 32) for i in range(4)]

    @pl.loop(0, HEADS)
    def _(source):
        block = q_ref[source, q_at : q_at + quarter, :].astype(F32)
        q = jnp.concatenate([jnp.where(z, block, 0.0) for z in zone], axis=0).astype(BF)
        score = dot_t(q, k_buf[...])
        top = jnp.max(score, axis=1, keepdims=True)
        weight = jnp.exp2((score - top) * scale).astype(BF)
        mixed = dot(weight, v_buf[...])
        mixed = mixed[:, :128] / mixed[:, 128:]
        out = mixed[:quarter]
        for i in range(1, 4):
            out = jnp.where(zone[i], mixed[i * quarter : (i + 1) * quarter], out)
        out_ref[source] = out.astype(BF)


def tail_kernel(
    att_ref, y_ref, w_out_ref, feed_gain_ref, w_up_ref, w_down_ref, head_gain_ref, w_head_ref,
    target_ref, flag_ref,
    pred_ref, dec_att_ref, mid_ref, slope_ref, z_ref, zn_ref, dpred_ref, loss_ref, feed_buf, wide_buf,
):
    rows, width = y_ref.shape
    quarter = rows // 4
    pixels = w_head_ref.shape[1]
    hidden = w_up_ref.shape[1]
    blocks = [att_ref[head].astype(F32) for head in range(HEADS)]
    dec_att_ref[...] = jnp.concatenate(
        [
            jnp.concatenate([b[:, 32 * i : 32 * i + 32] for b in blocks], axis=1)
            for i in range(4)
        ],
        axis=0,
    ).astype(BF)
    mid_ref[...] = y_ref[...].astype(F32) + dot(dec_att_ref[...], w_out_ref[...])
    feed_buf[...] = layer_norm(mid_ref[...], feed_gain_ref[...]).astype(BF)
    z_ref[...] = mid_ref[...]
    tile = 512
    c = math.sqrt(2.0 / math.pi)

    @pl.loop(0, hidden // tile)
    def _(step):
        cols = pl.ds(pl.multiple_of(step * tile, tile), tile)
        pre = dot(feed_buf[...], w_up_ref[:, cols])
        square = pre * pre
        t = jnp.tanh(pre * (c + (c * 0.044715) * square))
        gate = 0.5 + 0.5 * t
        slope = gate + (0.5 * pre) * (1.0 - t * t) * (c + (3 * c * 0.044715) * square)
        slope_ref[:, cols] = slope.astype(BF)
        z_ref[...] += dot((pre * gate).astype(BF), w_down_ref[cols, :])

    zn_ref[...] = layer_norm(z_ref[...], head_gain_ref[...]).astype(BF)
    flag = flag_ref[:, :1]
    loss_ref[...] = jnp.zeros_like(loss_ref)

    @pl.loop(0, pixels // tile)
    def _(step):
        cols = pl.ds(pl.multiple_of(step * tile, tile), tile)
        pred = dot(zn_ref[...], w_head_ref[:, cols])
        wide_buf[:, cols] = pred
        err = (pred - target_ref[:, cols].astype(F32)) * flag
        dpred_ref[:, cols] = (err * (2.0 / pixels)).astype(BF)
        part = jnp.sum(jnp.sum(err * err, axis=1, keepdims=True), axis=0, keepdims=True)
        loss_ref[...] += part * (1.0 / pixels)

    share = pred_ref.shape[1]
    for dest in range(pred_ref.shape[0]):
        pred_ref[dest] = wide_buf[dest * share : (dest + 1) * share, :].astype(BF)


def backward_kernel(
    me_ref, dec_att_ref, mid_ref, slope_ref, z_ref, zn_ref, dpred_ref, loss_ref,
    feed_gain_ref, w_up_ref, w_down_ref, head_gain_ref, w_head_ref,
    keep_ref, send_ref, back_buf, head_buf, out_buf,
):
    hidden = w_up_ref.shape[1]
    width, pixels = w_head_ref.shape
    dz = norm_backward(
        z_ref[...], head_gain_ref[...], dot_t(dpred_ref[...], w_head_ref[...])
    ).astype(BF)
    back_buf[...] = jnp.zeros_like(back_buf)
    tile = 512

    @pl.loop(0, hidden // tile)
    def _(step):
        cols = pl.ds(pl.multiple_of(step * tile, tile), tile)
        back = dot_t(dz, w_down_ref[cols, :]) * slope_ref[:, cols].astype(F32)
        back_buf[...] += dot_t(back.astype(BF), w_up_ref[:, cols])

    mid_grad = (
        dz.astype(F32) + norm_backward(mid_ref[...], feed_gain_ref[...], back_buf[...])
    ).astype(BF)
    first = (((0,), (0,)), ((), ()))
    out_buf[...] = lax.dot_general(
        dec_att_ref[...], mid_grad, first, preferred_element_type=F32
    )

    @pl.loop(0, pixels // tile)
    def _(step):
        cols = pl.ds(pl.multiple_of(step * tile, tile), tile)
        head_buf[:, cols] = lax.dot_general(
            zn_ref[...], dpred_ref[:, cols], first, preferred_element_type=F32
        )

    loss = jnp.broadcast_to(loss_ref[:1, :], (8, 128))
    high = loss.astype(BF)
    low = (loss - high.astype(F32)).astype(BF)
    sums = jnp.concatenate([high.astype(F32), low.astype(F32)], axis=0).astype(BF)
    deep = out_buf.shape[0] // 32
    half = out_buf.shape[1] // 2
    tall = width // 32
    for index in range(32):
        block = index ^ me_ref[0]
        ref = send_ref if index % 2 else keep_ref
        xy, z = index // 2 % 4, index // 8
        ref[xy, z, :, :pixels] = head_buf[
            pl.ds(pl.multiple_of(block * tall, tall), tall), :
        ].astype(BF)
        part = out_buf[pl.ds(pl.multiple_of(block * deep, deep), deep), :]
        ref[xy, z, :, pixels : pixels + half] = jnp.concatenate(
            [part[:, :half], part[:, half:]], axis=0
        ).astype(BF)
        ref[xy, z, :, pixels + half :] = sums


def add_kernel(*refs, count):
    total = refs[0][...].astype(F32)
    for ref in refs[1:count]:
        total = total + ref[...].astype(F32)
    total = total.astype(BF)
    outs = refs[count:]
    if len(outs) == 1:
        outs[0][...] = total
    else:
        for i, ref in enumerate(outs):
            ref[...] = total[i]


def join_kernel(*refs):
    for i, ref in enumerate(refs[:-1]):
        refs[-1][i] = ref[...]


def place_kernel(me_ref, *refs):
    blocks, (head_ref, out_ref, loss_ref) = refs[:8], refs[8:]
    pixels = head_ref.shape[1]
    deep = out_ref.shape[0] // 32
    half = out_ref.shape[1] // 2
    tall = head_ref.shape[0] // 32
    for index in range(32):
        block = index ^ me_ref[0]
        value = blocks[index % 2 * 4 + index // 2 % 4][index // 8].astype(F32)
        head_ref[pl.ds(pl.multiple_of(block * tall, tall), tall), :] = value[:, :pixels]
        at = pl.ds(pl.multiple_of(block * deep, deep), deep)
        out_ref[at, :half] = value[:deep, pixels : pixels + half]
        out_ref[at, half:] = value[deep:, pixels : pixels + half]
    value = blocks[0][0].astype(F32)
    loss_ref[...] = value[:8, pixels + half :] + value[8:, pixels + half :]


def vmem_call(kernel, outs, scratch, inputs, smem=(), flops=0):
    space = [
        pl.BlockSpec(memory_space=pltpu.SMEM if i in smem else pltpu.VMEM)
        for i in range(len(inputs))
    ]
    moved = sum(a.size * a.dtype.itemsize for a in inputs)
    return pl.pallas_call(
        kernel,
        out_shape=outs,
        in_specs=space,
        out_specs=[pl.BlockSpec(memory_space=pltpu.VMEM)] * len(outs),
        scratch_shapes=scratch,
        compiler_params=pltpu.CompilerParams(vmem_limit_bytes=VMEM_LIMIT),
        cost_estimate=pl.CostEstimate(flops=flops, bytes_accessed=moved, transcendentals=0),
    )(*inputs)


def swap(x, axis, groups=None):
    return lax.all_to_all(
        x, axis, split_axis=0, concat_axis=0, tiled=True, axis_index_groups=groups
    )


def all_sum(x, groups):
    size = lax.axis_size("dp")
    me = lax.axis_index("dp")
    stages = []
    step = 1
    while step < size:
        pairs = [(i, i ^ step) for i in range(size)]
        upper = (me // step) % 2
        half = x.shape[0] // 2
        mine = lax.dynamic_slice_in_dim(x, upper * half, half, 0)
        other = lax.dynamic_slice_in_dim(x, (1 - upper) * half, half, 0)
        x = mine + lax.ppermute(other, "dp", pairs)
        stages.append((pairs, upper))
        step *= 2
    rows, width = x.shape
    blocks = swap(x.reshape(groups, rows // groups, width), "ctx")
    total = jnp.sum(blocks.astype(F32), axis=0).astype(BF)
    x = swap(jnp.broadcast_to(total[None], blocks.shape), "ctx").reshape(rows, width)
    for pairs, upper in reversed(stages):
        other = lax.ppermute(x, "dp", pairs)
        low = jnp.where(upper == 0, x, other)
        high = jnp.where(upper == 0, other, x)
        x = jnp.concatenate([low, high], axis=0)
    return x


def across(x, dp_bit, ctx_bits):
    count, groups = lax.axis_size("dp"), lax.axis_size("ctx")
    pairs = [
        (i * groups + j, (i ^ dp_bit) * groups + (j ^ ctx_bits))
        for i in range(count)
        for j in range(groups)
    ]
    return lax.ppermute(x, ("dp", "ctx"), pairs)


PLANE = ((2, 0), (0, 1), (2, 1))
COLUMN = ((0, 2), (0, 4), (0, 6))


def sum_by_permutes(keep, send):
    shape = jax.ShapeDtypeStruct
    add = lambda parts, outs: vmem_call(
        functools.partial(add_kernel, count=len(parts)), outs, [], parts
    )
    part, block = shape(keep.shape[1:], BF), shape(keep.shape[2:], BF)
    parts = add([keep, across(send, 1, 0)], [part] * 4)
    others = [across(p, *bits) for p, bits in zip(parts[1:], PLANE)]
    blocks = add([parts[0], *others], [block] * 4)
    others = [across(b, *bits) for b, bits in zip(blocks[1:], COLUMN)]
    (total,) = add([blocks[0], *others], [block])
    (column,) = vmem_call(
        join_kernel, [part], [], [total] + [across(total, *bits) for bits in COLUMN]
    )
    ours = [column] + [across(column, *bits) for bits in PLANE]
    return ours, [across(x, 1, 0) for x in ours]


def sum_by_blocks(keep, send, groups):
    size = keep.shape[0] * keep.shape[1] * keep.shape[2]
    flat = jnp.concatenate([keep.reshape(size, -1), send.reshape(size, -1)], axis=0)
    unit = lax.axis_size("dp") * groups
    used = flat.shape[0]
    padded = -(-used // unit) * unit
    total = all_sum(jnp.pad(flat, ((0, padded - used), (0, 0))), groups)[:used]
    total = total.reshape(2, *keep.shape)
    return [total[0, i] for i in range(4)], [total[1, i] for i in range(4)]


def on_device(
    patches,
    enc_pos,
    w_embed,
    enc_gain,
    w_qkv,
    w_out,
    enc_out_gain,
    w_dec_embed,
    mask_token,
    dec_pos,
    dec_attn_gain,
    decoder_query_key_value_weight,
    w_dec_out,
    decoder_feed_gain,
    w_up,
    w_down,
    head_gain,
    w_head,
    visible_rows,
    visible_count,
    owner_slot,
):
    groups = lax.axis_size("ctx")
    repeat = groups // HEADS
    teams = [list(range(HEADS * i, HEADS * i + HEADS)) for i in range(repeat)]
    teams = None if repeat == 1 else teams
    source = patches[0]
    rows, pixels = source.shape
    half, quarter = rows // 2, rows // 4
    share = rows // 3
    width = w_embed.shape[1]
    dec_width = w_dec_embed.shape[1]
    row = lambda vector: vector.reshape(1, -1)
    shape = jax.ShapeDtypeStruct

    send, tok = vmem_call(
        embed_kernel,
        [shape((HEADS, half + rows + 16, 128), BF), shape((rows, width), BF)],
        [pltpu.VMEM((rows, width), BF), pltpu.VMEM((rows, w_qkv.shape[1]), BF)],
        [source, enc_pos, w_embed, row(enc_gain), w_qkv, visible_rows],
        flops=2 * rows * width * (pixels + w_qkv.shape[1]),
    )
    first = (lax.axis_index("ctx") // HEADS * HEADS).astype(jnp.int32).reshape(1)
    if repeat == 1:
        q = kv = swap(send, "ctx")
        q_at, kv_at = 0, half
    else:
        q = swap(send[:, :half], "ctx", teams)
        kv = swap(jnp.tile(send[:, half:], (repeat, 1, 1)), "ctx")
        q_at, kv_at = 0, 0
    cap_k = (share + 16) * groups
    cap_q = min(HEADS * rows, cap_k)
    (att,) = vmem_call(
        functools.partial(
            enc_attend_kernel, q_at=q_at, kv_at=kv_at, rows=rows, cap_q=cap_q, cap_k=cap_k
        ),
        [shape((HEADS, half, 128), BF)],
        [
            pltpu.VMEM((cap_q + rows, 128), BF),
            pltpu.VMEM((cap_k + rows, 256), BF),
            pltpu.VMEM((cap_q + rows, 128), BF),
        ],
        [first, q, kv],
        smem=(0,),
        flops=4 * cap_q * cap_k * 128,
    )
    att = swap(att, "ctx", teams)
    send, y_own, target, flag = vmem_call(
        functools.partial(middle_kernel, groups=groups),
        [
            shape((HEADS, half + quarter, 128), BF),
            shape((rows, dec_width), BF),
            shape((rows, pixels), BF),
            shape((rows, 128), F32),
        ],
        [
            pltpu.VMEM((rows, w_out.shape[0]), BF),
            pltpu.VMEM((rows, decoder_query_key_value_weight.shape[1]), F32),
        ],
        [
            att, tok, w_out, row(enc_out_gain), w_dec_embed, row(mask_token), dec_pos,
            row(dec_attn_gain), decoder_query_key_value_weight, visible_rows, owner_slot, source,
        ],
        flops=2 * rows * width * 1024,
    )
    if repeat == 1:
        q = kv = swap(send, "ctx")
        q_at = half
    else:
        q = swap(send[:, half:], "ctx", teams)
        kv = swap(jnp.tile(send[:, :half], (repeat, 1, 1)), "ctx")
        q_at = 0
    (att,) = vmem_call(
        functools.partial(dec_attend_kernel, q_at=q_at, rows=rows),
        [shape((HEADS, quarter, 128), BF)],
        [pltpu.VMEM((groups * rows, 128), BF), pltpu.VMEM((groups * rows, 256), BF)],
        [q, kv],
        flops=4 * HEADS * rows * groups * rows * 128,
    )
    att = swap(att, "ctx", teams)
    hidden = w_up.shape[1]
    pred, dec_att, y_mid, slope, z, zn, dpred, loss_part = vmem_call(
        tail_kernel,
        [
            shape((groups, rows // groups, pixels), BF),
            shape((rows, w_dec_out.shape[0]), BF),
            shape((rows, dec_width), F32),
            shape((rows, hidden), BF),
            shape((rows, dec_width), F32),
            shape((rows, dec_width), BF),
            shape((rows, pixels), BF),
            shape((8, 128), F32),
        ],
        [pltpu.VMEM((rows, dec_width), BF), pltpu.VMEM((rows, pixels), F32)],
        [
            att, y_own, w_dec_out, row(decoder_feed_gain), w_up, w_down, row(head_gain), w_head,
            target, flag,
        ],
        flops=2 * rows * dec_width * (2 * hidden + pixels),
    )
    reconstruction = swap(pred, "ctx")
    dp_me, ctx_me = lax.axis_index("dp"), lax.axis_index("ctx")
    if repeat == 1:
        me = dp_me % 2 + 2 * (dp_me // 2) + 4 * (ctx_me % 2) + 8 * (ctx_me // 2)
    else:
        me = jnp.int32(0)
    me = me.astype(jnp.int32).reshape(1)
    wide = pixels + dec_width // 2 + 128
    keep, send = vmem_call(
        backward_kernel,
        [shape((4, 4, dec_width // 32, wide), BF)] * 2,
        [
            pltpu.VMEM((rows, dec_width), F32),
            pltpu.VMEM((dec_width, pixels), F32),
            pltpu.VMEM((w_dec_out.shape[0], dec_width), F32),
        ],
        [
            me, dec_att, y_mid, slope, z, zn, dpred, loss_part, row(decoder_feed_gain),
            w_up, w_down, row(head_gain), w_head,
        ],
        smem=(0,),
        flops=2 * rows * dec_width * (2 * hidden + 2 * pixels),
    )
    if repeat == 1:
        ours, theirs = sum_by_permutes(keep, send)
    else:
        ours, theirs = sum_by_blocks(keep, send, groups)
    grad_head, grad_dec_out, loss = vmem_call(
        place_kernel,
        [shape(w_head.shape, F32), shape(w_dec_out.shape, F32), shape((8, 128), F32)],
        [],
        [me, *ours, *theirs],
        smem=(0,),
    )
    loss = loss[0, 0]
    masked_total = lax.axis_size("dp") * (groups * rows - share * groups)
    return (reconstruction.reshape(1, rows, pixels), grad_head, grad_dec_out, loss / masked_total)


def solution(mesh):
    in_specs = (
        P("dp", "ctx", None),
        P("ctx", None),
        P(),
        P(),
        P(),
        P(),
        P(),
        P(),
        P(),
        P("ctx", None),
        P(),
        P(),
        P(),
        P(),
        P(),
        P(),
        P(),
        P(),
        P("dp", "ctx"),
        P("dp", "ctx"),
        P("dp", "ctx"),
    )
    out_specs = (P("dp", "ctx", None), P(), P(), P())
    return jax.shard_map(
        on_device, mesh=mesh, in_specs=in_specs, out_specs=out_specs, check_vma=False
    )
```

```python
import functools
import math

import jax
import jax.numpy as jnp
from jax import lax
from jax.experimental import pallas as pl
from jax.experimental.pallas import tpu as pltpu
from jax.sharding import PartitionSpec as P

HEADS = 8
BF = jnp.bfloat16
F32 = jnp.float32
LOG2E = math.log2(math.e)
VMEM_LIMIT = 24 << 20


def as_row(vector):
    return vector.astype(F32).reshape(1, -1)


def layer_norm(x, gain):
    row_mean = jnp.mean(x, axis=-1, keepdims=True)
    centered_input = x - row_mean
    var = jnp.mean(centered_input * centered_input, axis=-1, keepdims=True)
    return centered_input * lax.rsqrt(var + 1e-06) * as_row(gain)


def norm_backward(z, gain, upstream):
    row_mean = jnp.mean(z, axis=-1, keepdims=True)
    centered_input = z - row_mean
    inverse_scale = lax.rsqrt(
        jnp.mean(centered_input * centered_input, axis=-1, keepdims=True) + 1e-06
    )
    normalized_input = centered_input * inverse_scale
    input_gradient = upstream * as_row(gain)
    return inverse_scale * (
        input_gradient
        - jnp.mean(input_gradient, axis=-1, keepdims=True)
        - normalized_input * jnp.mean(input_gradient * normalized_input, axis=-1, keepdims=True)
    )


def dot(a, b):
    return jnp.dot(a, b, preferred_element_type=F32)


def dot_t(a, b):
    return lax.dot_general(a, b, (((1,), (1,)), ((), ())), preferred_element_type=F32)


def swap_halves(x):
    half = x.shape[1] // 2
    return jnp.concatenate([x[:, half:], x[:, :half]], axis=1)


def slot_of_row(slots_row):
    size = slots_row.shape[1]
    row = lax.broadcasted_iota(jnp.int32, (size, size), 0)
    return jnp.where(row == slots_row, 1.0, 0.0)


def embed_kernel(
    patch_ref, pos_ref, w_embed_ref, gain_ref, w_qkv_ref, slots_ref,
    send_ref, tok_ref, normed_ref, qkv_ref,
):
    rows, width = patch_ref.shape
    half = rows // 2
    att = w_qkv_ref.shape[1] // 3
    size = att // HEADS
    tile = 256

    @pl.loop(0, width // tile)
    def _(step):
        cols = pl.ds(pl.multiple_of(step * tile, tile), tile)
        tok_ref[:, cols] = (
            dot(patch_ref[...], w_embed_ref[:, cols]) + pos_ref[:, cols].astype(F32)
        ).astype(BF)

    normed_ref[...] = layer_norm(tok_ref[...].astype(F32), gain_ref[...]).astype(BF)
    pick = slot_of_row(slots_ref[...]).astype(BF)

    @pl.loop(0, 3 * att // tile)
    def _(step):
        cols = pl.ds(pl.multiple_of(step * tile, tile), tile)
        part = dot(normed_ref[...], w_qkv_ref[:, cols]).astype(BF)
        qkv_ref[:, cols] = lax.dot_general(
            pick, part, (((0,), (0,)), ((), ())), preferred_element_type=F32
        ).astype(BF)

    count = jnp.sum(jnp.where(slots_ref[...] >= 0, 1.0, 0.0), axis=1, keepdims=True)
    high = jnp.floor(count * (1.0 / 16))
    lane = lax.broadcasted_iota(jnp.int32, (16, 128), 1)
    info = jnp.where(lane < 64, high, count - 16.0 * high).astype(BF)
    for head in range(HEADS):
        at = head * size
        q = qkv_ref[:, at : at + size]
        k = qkv_ref[:, att + at : att + at + size]
        v = qkv_ref[:, 2 * att + at : 2 * att + at + size]
        send_ref[head, :half, :] = jnp.concatenate([q[:half], q[half:]], axis=1)
        send_ref[head, half : half + rows, :] = jnp.concatenate([k, v], axis=1)
        send_ref[head, half + rows :, :] = info


def enc_attend_kernel(
    first_ref, q_ref, kv_ref, out_ref, q_buf, kv_buf, o_buf, *, q_at, kv_at, rows, cap_q, cap_k
):
    half = rows // 2
    sources = kv_ref.shape[0]
    lane16 = lax.broadcasted_iota(jnp.int32, (16, 128), 1)
    lane_h = lax.broadcasted_iota(jnp.int32, (half, 128), 1)

    def count_of(source):
        info = kv_ref[source, kv_at + rows : kv_at + rows + 16, :].astype(F32)
        high = jnp.max(jnp.where(lane16 < 64, info, 0.0)).astype(jnp.int32)
        low = jnp.max(jnp.where(lane16 >= 64, info, 0.0)).astype(jnp.int32)
        return high * 16 + low

    q_buf[...] = jnp.zeros_like(q_buf)
    o_buf[...] = jnp.zeros_like(o_buf)
    kv_buf[:, :128] = jnp.zeros((kv_buf.shape[0], 128), BF)
    kv_buf[:, 128:] = jnp.ones((kv_buf.shape[0], 128), BF)

    key = lax.broadcasted_iota(jnp.int32, (1, cap_k), 1)
    valid = jnp.zeros((1, cap_k), F32)
    off = jnp.int32(0)
    for source in range(sources):
        count = count_of(source)
        off = pl.multiple_of(off, 16)
        kv_buf[pl.ds(off, rows), :128] = kv_ref[source, kv_at : kv_at + rows, :]
        valid = jnp.where((key >= off) & (key < off + count), 1.0, valid)
        off = off + (count + 15) // 16 * 16
    bias = jnp.where(valid > 0.0, 0.0, -1e30)

    offs = []
    off = jnp.int32(0)
    for source in range(HEADS):
        off = pl.multiple_of(off, 16)
        offs.append(off)
        block = q_ref[source, q_at : q_at + half, :]
        zero = jnp.zeros_like(block)
        q_buf[pl.ds(off, half), :] = jnp.where(lane_h < 64, block, zero)
        q_buf[pl.ds(off + half, half), :] = jnp.where(lane_h < 64, swap_halves(block), zero)
        off = off + (count_of(first_ref[0] + source) + 15) // 16 * 16
    total = off

    tile = 128
    scale = LOG2E * 64**-0.5

    @pl.loop(0, cap_q // tile)
    def _(step):
        @pl.when(step * tile < total)
        def _():
            at = pl.ds(pl.multiple_of(step * tile, tile), tile)
            score = dot_t(q_buf[at, :], kv_buf[:cap_k, :128]) + bias
            top = jnp.max(score, axis=1, keepdims=True)
            weight = jnp.exp2((score - top) * scale).astype(BF)
            mixed = dot(weight, kv_buf[:cap_k, :])
            o_buf[at, :] = (mixed[:, :128] / mixed[:, 128:]).astype(BF)

    for source in range(HEADS):
        upper = o_buf[pl.ds(offs[source], half), :]
        lower = o_buf[pl.ds(pl.multiple_of(offs[source] + half, 16), half), :]
        out_ref[source] = jnp.where(lane_h < 64, swap_halves(upper), lower)


def middle_kernel(
    att_ref, tok_ref, w_out_ref, out_gain_ref, w_dec_ref, mask_ref, pos_ref, gain_ref,
    w_qkv_ref, slots_ref, owner_ref, patch_ref,
    send_ref, y_ref, target_ref, flag_ref, att_buf, qkv_buf, *, groups,
):
    rows, width = tok_ref.shape
    half = rows // 2
    block = rows // groups
    for pair in range(HEADS // 2):
        a, b = att_ref[2 * pair], att_ref[2 * pair + 1]
        cols = slice(128 * pair, 128 * pair + 128)
        att_buf[:half, cols] = jnp.concatenate([a[:, :64], b[:, :64]], axis=1)
        att_buf[half:, cols] = jnp.concatenate([a[:, 64:], b[:, 64:]], axis=1)
    pick = slot_of_row(slots_ref[...])
    seen = jnp.sum(pick, axis=1, keepdims=True)
    attended = dot(pick.astype(BF), att_buf[...]).astype(BF)
    encoded = tok_ref[...].astype(F32) + dot(attended, w_out_ref[...])
    dec_normed = layer_norm(encoded, out_gain_ref[...]).astype(BF)
    dec_tok = dot(dec_normed, w_dec_ref[...]).astype(BF).astype(F32)
    filled = jnp.where(seen > 0.0, dec_tok, as_row(mask_ref[...]))
    decoder_in = (filled + pos_ref[...].astype(F32)).astype(BF)

    owner = owner_ref[...]
    dest = jnp.zeros_like(owner)
    for device in range(1, groups):
        dest = dest + jnp.where(owner >= device * rows, 1, 0)
    local = owner - dest * rows
    first = jnp.min(local.astype(F32), axis=1, keepdims=True).astype(jnp.int32)
    place = dest * block + local - first
    move = slot_of_row(place).astype(BF)
    y = dot(move, decoder_in)
    y_ref[...] = y.astype(BF)
    target_ref[...] = dot(move, patch_ref[...]).astype(BF)
    hidden = jnp.broadcast_to(1.0 - seen, (rows, 128)).astype(BF)
    flag_ref[...] = dot(move, hidden)
    attn_in = layer_norm(y, gain_ref[...]).astype(BF)
    qkv_buf[...] = dot(attn_in, w_qkv_ref[...]).astype(BF).astype(F32)
    att = w_qkv_ref.shape[1] // 3
    size = att // HEADS
    quarter = rows // 4
    for head in range(HEADS):
        at = head * size
        q = qkv_buf[:, at : at + size]
        k = qkv_buf[:, att + at : att + at + size]
        v = qkv_buf[:, 2 * att + at : 2 * att + at + size]
        send_ref[head, :half, :] = jnp.concatenate(
            [k[:half], v[:half], k[half:], v[half:]], axis=1
        ).astype(BF)
        send_ref[head, half:, :] = jnp.concatenate(
            [q[i * quarter : (i + 1) * quarter] for i in range(4)], axis=1
        ).astype(BF)


def dec_attend_kernel(q_ref, kv_ref, out_ref, k_buf, v_buf, *, q_at, rows):
    half = rows // 2
    quarter = rows // 4
    sources = kv_ref.shape[0]
    for source in range(sources):
        for part in range(2):
            block = kv_ref[source, :half, 64 * part : 64 * part + 64]
            at = source * rows + part * half
            k, v = block[:, :32], block[:, 32:]
            k_buf[at : at + half, :] = jnp.concatenate([k, k, k, k], axis=1)
            v_buf[at : at + half, :128] = jnp.concatenate([v, v, v, v], axis=1)
    v_buf[:, 128:] = jnp.ones((v_buf.shape[0], 128), BF)
    scale = LOG2E * 32**-0.5
    lane = lax.broadcasted_iota(jnp.int32, (quarter, 128), 1)
    zone = [(lane >= 32 * i) & (lane < 32 * i + 32) for i in range(4)]

    @pl.loop(0, HEADS)
    def _(source):
        block = q_ref[source, q_at : q_at + quarter, :].astype(F32)
        q = jnp.concatenate([jnp.where(z, block, 0.0) for z in zone], axis=0).astype(BF)
        score = dot_t(q, k_buf[...])
        top = jnp.max(score, axis=1, keepdims=True)
        weight = jnp.exp2((score - top) * scale).astype(BF)
        mixed = dot(weight, v_buf[...])
        mixed = mixed[:, :128] / mixed[:, 128:]
        out = mixed[:quarter]
        for i in range(1, 4):
            out = jnp.where(zone[i], mixed[i * quarter : (i + 1) * quarter], out)
        out_ref[source] = out.astype(BF)


def tail_kernel(
    att_ref, y_ref, w_out_ref, feed_gain_ref, w_up_ref, w_down_ref, head_gain_ref, w_head_ref,
    target_ref, flag_ref,
    pred_ref, dec_att_ref, mid_ref, slope_ref, z_ref, zn_ref, dpred_ref, loss_ref, feed_buf, wide_buf,
):
    rows, width = y_ref.shape
    quarter = rows // 4
    pixels = w_head_ref.shape[1]
    hidden = w_up_ref.shape[1]
    blocks = [att_ref[head].astype(F32) for head in range(HEADS)]
    dec_att_ref[...] = jnp.concatenate(
        [
            jnp.concatenate([b[:, 32 * i : 32 * i + 32] for b in blocks], axis=1)
            for i in range(4)
        ],
        axis=0,
    ).astype(BF)
    mid_ref[...] = y_ref[...].astype(F32) + dot(dec_att_ref[...], w_out_ref[...])
    feed_buf[...] = layer_norm(mid_ref[...], feed_gain_ref[...]).astype(BF)
    z_ref[...] = mid_ref[...]
    tile = 512
    c = math.sqrt(2.0 / math.pi)

    @pl.loop(0, hidden // tile)
    def _(step):
        cols = pl.ds(pl.multiple_of(step * tile, tile), tile)
        pre = dot(feed_buf[...], w_up_ref[:, cols])
        square = pre * pre
        t = jnp.tanh(pre * (c + (c * 0.044715) * square))
        gate = 0.5 + 0.5 * t
        slope = gate + (0.5 * pre) * (1.0 - t * t) * (c + (3 * c * 0.044715) * square)
        slope_ref[:, cols] = slope.astype(BF)
        z_ref[...] += dot((pre * gate).astype(BF), w_down_ref[cols, :])

    zn_ref[...] = layer_norm(z_ref[...], head_gain_ref[...]).astype(BF)
    flag = flag_ref[:, :1]
    loss_ref[...] = jnp.zeros_like(loss_ref)

    @pl.loop(0, pixels // tile)
    def _(step):
        cols = pl.ds(pl.multiple_of(step * tile, tile), tile)
        pred = dot(zn_ref[...], w_head_ref[:, cols])
        wide_buf[:, cols] = pred
        err = (pred - target_ref[:, cols].astype(F32)) * flag
        dpred_ref[:, cols] = (err * (2.0 / pixels)).astype(BF)
        part = jnp.sum(jnp.sum(err * err, axis=1, keepdims=True), axis=0, keepdims=True)
        loss_ref[...] += part * (1.0 / pixels)

    share = pred_ref.shape[1]
    for dest in range(pred_ref.shape[0]):
        pred_ref[dest] = wide_buf[dest * share : (dest + 1) * share, :].astype(BF)


def backward_kernel(
    me_ref, dec_att_ref, mid_ref, slope_ref, z_ref, zn_ref, dpred_ref, loss_ref,
    feed_gain_ref, w_up_ref, w_down_ref, head_gain_ref, w_head_ref,
    keep_ref, send_ref, back_buf, head_buf, out_buf,
):
    hidden = w_up_ref.shape[1]
    width, pixels = w_head_ref.shape
    dz = norm_backward(
        z_ref[...], head_gain_ref[...], dot_t(dpred_ref[...], w_head_ref[...])
    ).astype(BF)
    back_buf[...] = jnp.zeros_like(back_buf)
    tile = 512

    @pl.loop(0, hidden // tile)
    def _(step):
        cols = pl.ds(pl.multiple_of(step * tile, tile), tile)
        back = dot_t(dz, w_down_ref[cols, :]) * slope_ref[:, cols].astype(F32)
        back_buf[...] += dot_t(back.astype(BF), w_up_ref[:, cols])

    mid_grad = (
        dz.astype(F32) + norm_backward(mid_ref[...], feed_gain_ref[...], back_buf[...])
    ).astype(BF)
    first = (((0,), (0,)), ((), ()))
    out_buf[...] = lax.dot_general(
        dec_att_ref[...], mid_grad, first, preferred_element_type=F32
    )

    @pl.loop(0, pixels // tile)
    def _(step):
        cols = pl.ds(pl.multiple_of(step * tile, tile), tile)
        head_buf[:, cols] = lax.dot_general(
            zn_ref[...], dpred_ref[:, cols], first, preferred_element_type=F32
        )

    loss = jnp.broadcast_to(loss_ref[:1, :], (8, 128))
    high = loss.astype(BF)
    low = (loss - high.astype(F32)).astype(BF)
    sums = jnp.concatenate([high.astype(F32), low.astype(F32)], axis=0).astype(BF)
    deep = out_buf.shape[0] // 32
    half = out_buf.shape[1] // 2
    tall = width // 32
    for index in range(32):
        block = index ^ me_ref[0]
        ref = send_ref if index % 2 else keep_ref
        xy, z = index // 2 % 4, index // 8
        ref[xy, z, :, :pixels] = head_buf[
            pl.ds(pl.multiple_of(block * tall, tall), tall), :
        ].astype(BF)
        part = out_buf[pl.ds(pl.multiple_of(block * deep, deep), deep), :]
        ref[xy, z, :, pixels : pixels + half] = jnp.concatenate(
            [part[:, :half], part[:, half:]], axis=0
        ).astype(BF)
        ref[xy, z, :, pixels + half :] = sums


def add_kernel(*refs, count):
    total = refs[0][...].astype(F32)
    for ref in refs[1:count]:
        total = total + ref[...].astype(F32)
    total = total.astype(BF)
    outs = refs[count:]
    if len(outs) == 1:
        outs[0][...] = total
    else:
        for i, ref in enumerate(outs):
            ref[...] = total[i]


def join_kernel(*refs):
    for i, ref in enumerate(refs[:-1]):
        refs[-1][i] = ref[...]


def place_kernel(me_ref, *refs, masked_total):
    blocks, (head_ref, out_ref, loss_ref) = refs[:8], refs[8:]
    pixels = head_ref.shape[1]
    deep = out_ref.shape[0] // 32
    half = out_ref.shape[1] // 2
    tall = head_ref.shape[0] // 32
    for index in range(32):
        block = index ^ me_ref[0]
        value = blocks[index % 2 * 4 + index // 2 % 4][index // 8].astype(F32)
        head_ref[pl.ds(pl.multiple_of(block * tall, tall), tall), :] = value[:, :pixels]
        at = pl.ds(pl.multiple_of(block * deep, deep), deep)
        out_ref[at, :half] = value[:deep, pixels : pixels + half]
        out_ref[at, half:] = value[deep:, pixels : pixels + half]
    value = blocks[0][0].astype(F32)
    total = value[:8, pixels + half :] + value[8:, pixels + half :]
    loss_ref[0, 0] = jnp.max(total) * (1.0 / masked_total)


def vmem_call(kernel, outs, scratch, inputs, smem=(), smem_out=(), flops=0):
    space = [
        pl.BlockSpec(memory_space=pltpu.SMEM if i in smem else pltpu.VMEM)
        for i in range(len(inputs))
    ]
    moved = sum(a.size * a.dtype.itemsize for a in inputs)
    return pl.pallas_call(
        kernel,
        out_shape=outs,
        in_specs=space,
        out_specs=[
            pl.BlockSpec(memory_space=pltpu.SMEM if i in smem_out else pltpu.VMEM)
            for i in range(len(outs))
        ],
        scratch_shapes=scratch,
        compiler_params=pltpu.CompilerParams(vmem_limit_bytes=VMEM_LIMIT),
        cost_estimate=pl.CostEstimate(flops=flops, bytes_accessed=moved, transcendentals=0),
    )(*inputs)


def swap(x, axis, groups=None):
    return lax.all_to_all(
        x, axis, split_axis=0, concat_axis=0, tiled=True, axis_index_groups=groups
    )


def all_sum(x, groups):
    size = lax.axis_size("dp")
    me = lax.axis_index("dp")
    stages = []
    step = 1
    while step < size:
        pairs = [(i, i ^ step) for i in range(size)]
        upper = (me // step) % 2
        half = x.shape[0] // 2
        mine = lax.dynamic_slice_in_dim(x, upper * half, half, 0)
        other = lax.dynamic_slice_in_dim(x, (1 - upper) * half, half, 0)
        x = mine + lax.ppermute(other, "dp", pairs)
        stages.append((pairs, upper))
        step *= 2
    rows, width = x.shape
    blocks = swap(x.reshape(groups, rows // groups, width), "ctx")
    total = jnp.sum(blocks.astype(F32), axis=0).astype(BF)
    x = swap(jnp.broadcast_to(total[None], blocks.shape), "ctx").reshape(rows, width)
    for pairs, upper in reversed(stages):
        other = lax.ppermute(x, "dp", pairs)
        low = jnp.where(upper == 0, x, other)
        high = jnp.where(upper == 0, other, x)
        x = jnp.concatenate([low, high], axis=0)
    return x


def across(x, dp_bit, ctx_bits):
    count, groups = lax.axis_size("dp"), lax.axis_size("ctx")
    pairs = [
        (i * groups + j, (i ^ dp_bit) * groups + (j ^ ctx_bits))
        for i in range(count)
        for j in range(groups)
    ]
    return lax.ppermute(x, ("dp", "ctx"), pairs)


PLANE = ((2, 0), (0, 1), (2, 1))
COLUMN = ((0, 2), (0, 4), (0, 6))


def sum_by_permutes(keep, send, ahead):
    shape = jax.ShapeDtypeStruct
    add = lambda parts, outs: vmem_call(
        functools.partial(add_kernel, count=len(parts)), outs, [], parts
    )
    part, block = shape(keep.shape[1:], BF), shape(keep.shape[2:], BF)
    parts = add([keep, across(send, 1, 0)], [part] * 4)
    others = [across(p, *bits) for p, bits in zip(parts[1:], PLANE)]
    first, ahead = lax.optimization_barrier((parts[0], ahead))
    blocks = add([first, *others], [block] * 4)
    others = [across(b, *bits) for b, bits in zip(blocks[1:], COLUMN)]
    (total,) = add([blocks[0], *others], [block])
    (column,) = vmem_call(
        join_kernel, [part], [], [total] + [across(total, *bits) for bits in COLUMN]
    )
    ours = [column] + [across(column, *bits) for bits in PLANE]
    return ours, [across(x, 1, 0) for x in ours], ahead


def sum_by_blocks(keep, send, groups):
    size = keep.shape[0] * keep.shape[1] * keep.shape[2]
    flat = jnp.concatenate([keep.reshape(size, -1), send.reshape(size, -1)], axis=0)
    unit = lax.axis_size("dp") * groups
    used = flat.shape[0]
    padded = -(-used // unit) * unit
    total = all_sum(jnp.pad(flat, ((0, padded - used), (0, 0))), groups)[:used]
    total = total.reshape(2, *keep.shape)
    return [total[0, i] for i in range(4)], [total[1, i] for i in range(4)]


def on_device(
    patches,
    enc_pos,
    w_embed,
    enc_gain,
    w_qkv,
    w_out,
    enc_out_gain,
    w_dec_embed,
    mask_token,
    dec_pos,
    dec_attn_gain,
    decoder_query_key_value_weight,
    w_dec_out,
    decoder_feed_gain,
    w_up,
    w_down,
    head_gain,
    w_head,
    visible_rows,
    visible_count,
    owner_slot,
):
    groups = lax.axis_size("ctx")
    repeat = groups // HEADS
    teams = [list(range(HEADS * i, HEADS * i + HEADS)) for i in range(repeat)]
    teams = None if repeat == 1 else teams
    source = patches[0]
    rows, pixels = source.shape
    half, quarter = rows // 2, rows // 4
    share = rows // 3
    width = w_embed.shape[1]
    dec_width = w_dec_embed.shape[1]
    shape = jax.ShapeDtypeStruct

    send, tok = vmem_call(
        embed_kernel,
        [shape((HEADS, half + rows + 16, 128), BF), shape((rows, width), BF)],
        [pltpu.VMEM((rows, width), BF), pltpu.VMEM((rows, w_qkv.shape[1]), BF)],
        [source, enc_pos, w_embed, enc_gain, w_qkv, visible_rows],
        flops=2 * rows * width * (pixels + w_qkv.shape[1]),
    )
    first = (lax.axis_index("ctx") // HEADS * HEADS).astype(jnp.int32).reshape(1)
    if repeat == 1:
        q = kv = swap(send, "ctx")
        q_at, kv_at = 0, half
    else:
        q = swap(send[:, :half], "ctx", teams)
        kv = swap(jnp.tile(send[:, half:], (repeat, 1, 1)), "ctx")
        q_at, kv_at = 0, 0
    cap_k = (share + 16) * groups
    cap_q = min(HEADS * rows, cap_k)
    (att,) = vmem_call(
        functools.partial(
            enc_attend_kernel, q_at=q_at, kv_at=kv_at, rows=rows, cap_q=cap_q, cap_k=cap_k
        ),
        [shape((HEADS, half, 128), BF)],
        [
            pltpu.VMEM((cap_q + rows, 128), BF),
            pltpu.VMEM((cap_k + rows, 256), BF),
            pltpu.VMEM((cap_q + rows, 128), BF),
        ],
        [first, q, kv],
        smem=(0,),
        flops=4 * cap_q * cap_k * 128,
    )
    att = swap(att, "ctx", teams)
    send, y_own, target, flag = vmem_call(
        functools.partial(middle_kernel, groups=groups),
        [
            shape((HEADS, half + quarter, 128), BF),
            shape((rows, dec_width), BF),
            shape((rows, pixels), BF),
            shape((rows, 128), F32),
        ],
        [
            pltpu.VMEM((rows, w_out.shape[0]), BF),
            pltpu.VMEM((rows, decoder_query_key_value_weight.shape[1]), F32),
        ],
        [
            att, tok, w_out, enc_out_gain, w_dec_embed, mask_token, dec_pos,
            dec_attn_gain, decoder_query_key_value_weight, visible_rows, owner_slot, source,
        ],
        flops=2 * rows * width * 1024,
    )
    if repeat == 1:
        q = kv = swap(send, "ctx")
        q_at = half
    else:
        q = swap(send[:, half:], "ctx", teams)
        kv = swap(jnp.tile(send[:, :half], (repeat, 1, 1)), "ctx")
        q_at = 0
    (att,) = vmem_call(
        functools.partial(dec_attend_kernel, q_at=q_at, rows=rows),
        [shape((HEADS, quarter, 128), BF)],
        [pltpu.VMEM((groups * rows, 128), BF), pltpu.VMEM((groups * rows, 256), BF)],
        [q, kv],
        flops=4 * HEADS * rows * groups * rows * 128,
    )
    att = swap(att, "ctx", teams)
    hidden = w_up.shape[1]
    pred, dec_att, y_mid, slope, z, zn, dpred, loss_part = vmem_call(
        tail_kernel,
        [
            shape((groups, rows // groups, pixels), BF),
            shape((rows, w_dec_out.shape[0]), BF),
            shape((rows, dec_width), F32),
            shape((rows, hidden), BF),
            shape((rows, dec_width), F32),
            shape((rows, dec_width), BF),
            shape((rows, pixels), BF),
            shape((8, 128), F32),
        ],
        [pltpu.VMEM((rows, dec_width), BF), pltpu.VMEM((rows, pixels), F32)],
        [
            att, y_own, w_dec_out, decoder_feed_gain, w_up, w_down, head_gain, w_head,
            target, flag,
        ],
        flops=2 * rows * dec_width * (2 * hidden + pixels),
    )
    reconstruction = swap(pred, "ctx")
    dp_me, ctx_me = lax.axis_index("dp"), lax.axis_index("ctx")
    if repeat == 1:
        me = dp_me % 2 + 2 * (dp_me // 2) + 4 * (ctx_me % 2) + 8 * (ctx_me // 2)
    else:
        me = jnp.int32(0)
    me = me.astype(jnp.int32).reshape(1)
    wide = pixels + dec_width // 2 + 128
    keep, send = vmem_call(
        backward_kernel,
        [shape((4, 4, dec_width // 32, wide), BF)] * 2,
        [
            pltpu.VMEM((rows, dec_width), F32),
            pltpu.VMEM((dec_width, pixels), F32),
            pltpu.VMEM((w_dec_out.shape[0], dec_width), F32),
        ],
        [
            me, dec_att, y_mid, slope, z, zn, dpred, loss_part, decoder_feed_gain,
            w_up, w_down, head_gain, w_head,
        ],
        smem=(0,),
        flops=2 * rows * dec_width * (2 * hidden + 2 * pixels),
    )
    if repeat == 1:
        ours, theirs, reconstruction = sum_by_permutes(keep, send, reconstruction)
    else:
        ours, theirs = sum_by_blocks(keep, send, groups)
    masked_total = lax.axis_size("dp") * (groups * rows - share * groups)
    grad_head, grad_dec_out, loss = vmem_call(
        functools.partial(place_kernel, masked_total=masked_total),
        [shape(w_head.shape, F32), shape(w_dec_out.shape, F32), shape((1, 1), F32)],
        [],
        [me, *ours, *theirs],
        smem=(0,),
        smem_out=(2,),
    )
    return (reconstruction.reshape(1, rows, pixels), grad_head, grad_dec_out, loss.reshape(()))


def solution(mesh):
    in_specs = (
        P("dp", "ctx", None),
        P("ctx", None),
        P(),
        P(),
        P(),
        P(),
        P(),
        P(),
        P(),
        P("ctx", None),
        P(),
        P(),
        P(),
        P(),
        P(),
        P(),
        P(),
        P(),
        P("dp", "ctx"),
        P("dp", "ctx"),
        P("dp", "ctx"),
    )
    out_specs = (P("dp", "ctx", None), P(), P(), P())
    return jax.shard_map(
        on_device, mesh=mesh, in_specs=in_specs, out_specs=out_specs, check_vma=False
    )
```

```python
import functools
import math

import jax
import jax.numpy as jnp
from jax import lax
from jax.experimental import pallas as pl
from jax.experimental.pallas import tpu as pltpu
from jax.sharding import PartitionSpec as P

HEADS = 8
BF = jnp.bfloat16
F32 = jnp.float32
LOG2E = math.log2(math.e)
VMEM_LIMIT = 24 << 20


def as_row(vector):
    return vector.astype(F32).reshape(1, -1)


def layer_norm(x, gain):
    row_mean = jnp.mean(x, axis=-1, keepdims=True)
    centered_input = x - row_mean
    var = jnp.mean(centered_input * centered_input, axis=-1, keepdims=True)
    return centered_input * lax.rsqrt(var + 1e-06) * as_row(gain)


def norm_backward(z, gain, upstream):
    row_mean = jnp.mean(z, axis=-1, keepdims=True)
    centered_input = z - row_mean
    inverse_scale = lax.rsqrt(
        jnp.mean(centered_input * centered_input, axis=-1, keepdims=True) + 1e-06
    )
    normalized_input = centered_input * inverse_scale
    input_gradient = upstream * as_row(gain)
    return inverse_scale * (
        input_gradient
        - jnp.mean(input_gradient, axis=-1, keepdims=True)
        - normalized_input * jnp.mean(input_gradient * normalized_input, axis=-1, keepdims=True)
    )


def dot(a, b):
    return jnp.dot(a, b, preferred_element_type=F32)


def dot_t(a, b):
    return lax.dot_general(a, b, (((1,), (1,)), ((), ())), preferred_element_type=F32)


def swap_halves(x):
    half = x.shape[1] // 2
    return jnp.concatenate([x[:, half:], x[:, :half]], axis=1)


def slot_of_row(slots_row):
    size = slots_row.shape[1]
    row = lax.broadcasted_iota(jnp.int32, (size, size), 0)
    return jnp.where(row == slots_row, 1.0, 0.0)


def embed_kernel(
    patch_hbm, pos_hbm, w_embed_hbm, gain_ref, w_qkv_hbm, slots_ref,
    send_ref, tok_ref, normed_ref, qkv_ref, patch_ref, pos_ref, w_embed_ref, w_qkv_ref,
    patch_sem, pos_sem, embed_sem, qkv_sem,
):
    rows, width = patch_ref.shape
    half = rows // 2
    att = w_qkv_ref.shape[1] // 3
    size = att // HEADS
    tile = 256

    def piece(hbm, buf, sem, step):
        cols = slice(step * tile, (step + 1) * tile)
        return pltpu.make_async_copy(hbm.at[:, cols], buf.at[:, cols], sem.at[step])

    embed_copies = [
        piece(w_embed_hbm, w_embed_ref, embed_sem, i) for i in range(width // tile)
    ]
    qkv_copies = [piece(w_qkv_hbm, w_qkv_ref, qkv_sem, i) for i in range(3 * att // tile)]
    patch_copy = pltpu.make_async_copy(patch_hbm, patch_ref, patch_sem)
    pos_copy = pltpu.make_async_copy(pos_hbm, pos_ref, pos_sem)
    for copy in [patch_copy, embed_copies[0], pos_copy, *embed_copies[1:], *qkv_copies]:
        copy.start()
    patch_copy.wait()
    for step in range(width // tile):
        embed_copies[step].wait()
        if step == 0:
            pos_copy.wait()
        cols = slice(step * tile, (step + 1) * tile)
        tok_ref[:, cols] = (
            dot(patch_ref[...], w_embed_ref[:, cols]) + pos_ref[:, cols].astype(F32)
        ).astype(BF)

    normed_ref[...] = layer_norm(tok_ref[...].astype(F32), gain_ref[...]).astype(BF)
    pick = slot_of_row(slots_ref[...]).astype(BF)
    for step in range(3 * att // tile):
        qkv_copies[step].wait()
        cols = slice(step * tile, (step + 1) * tile)
        part = dot(normed_ref[...], w_qkv_ref[:, cols]).astype(BF)
        qkv_ref[:, cols] = lax.dot_general(
            pick, part, (((0,), (0,)), ((), ())), preferred_element_type=F32
        ).astype(BF)

    count = jnp.sum(jnp.where(slots_ref[...] >= 0, 1.0, 0.0), axis=1, keepdims=True)
    high = jnp.floor(count * (1.0 / 16))
    lane = lax.broadcasted_iota(jnp.int32, (16, 128), 1)
    info = jnp.where(lane < 64, high, count - 16.0 * high).astype(BF)
    for head in range(HEADS):
        at = head * size
        q = qkv_ref[:, at : at + size]
        k = qkv_ref[:, att + at : att + at + size]
        v = qkv_ref[:, 2 * att + at : 2 * att + at + size]
        send_ref[head, :half, :] = jnp.concatenate([q[:half], q[half:]], axis=1)
        send_ref[head, half : half + rows, :] = jnp.concatenate([k, v], axis=1)
        send_ref[head, half + rows :, :] = info


def enc_attend_kernel(
    me_ref, q_ref, kv_ref, out_ref, q_buf, kv_buf, o_buf, *, q_at, kv_at, rows, cap_q, cap_k
):
    half = rows // 2
    sources = kv_ref.shape[0]
    lane16 = lax.broadcasted_iota(jnp.int32, (16, 128), 1)
    lane_h = lax.broadcasted_iota(jnp.int32, (half, 128), 1)

    def count_of(source):
        info = kv_ref[source, kv_at + rows : kv_at + rows + 16, :].astype(F32)
        high = jnp.max(jnp.where(lane16 < 64, info, 0.0)).astype(jnp.int32)
        low = jnp.max(jnp.where(lane16 >= 64, info, 0.0)).astype(jnp.int32)
        return high * 16 + low

    q_buf[...] = jnp.zeros_like(q_buf)
    o_buf[...] = jnp.zeros_like(o_buf)
    kv_buf[:, :128] = jnp.zeros((kv_buf.shape[0], 128), BF)
    kv_buf[:, 128:] = jnp.ones((kv_buf.shape[0], 128), BF)

    key = lax.broadcasted_iota(jnp.int32, (1, cap_k), 1)
    valid = jnp.zeros((1, cap_k), F32)
    off = jnp.int32(0)
    for source in range(sources):
        count = count_of(source)
        off = pl.multiple_of(off, 16)
        kv_buf[pl.ds(off, rows), :128] = kv_ref[source, kv_at : kv_at + rows, :]
        valid = jnp.where((key >= off) & (key < off + count), 1.0, valid)
        off = off + (count + 15) // 16 * 16
    bias = jnp.where(valid > 0.0, 0.0, -1e30)

    offs = []
    off = jnp.int32(0)
    for source in range(HEADS):
        off = pl.multiple_of(off, 16)
        offs.append(off)
        block = q_ref[source, q_at : q_at + half, :]
        zero = jnp.zeros_like(block)
        q_buf[pl.ds(off, half), :] = jnp.where(lane_h < 64, block, zero)
        q_buf[pl.ds(off + half, half), :] = jnp.where(lane_h < 64, swap_halves(block), zero)
        off = off + (count_of(me_ref[2] + source) + 15) // 16 * 16
    total = off

    tile = 128
    scale = LOG2E * 64**-0.5

    @pl.loop(0, cap_q // tile)
    def _(step):
        @pl.when(step * tile < total)
        def _():
            at = pl.ds(pl.multiple_of(step * tile, tile), tile)
            score = dot_t(q_buf[at, :], kv_buf[:cap_k, :128]) + bias
            top = jnp.max(score, axis=1, keepdims=True)
            weight = jnp.exp2((score - top) * scale).astype(BF)
            mixed = dot(weight, kv_buf[:cap_k, :])
            o_buf[at, :] = (mixed[:, :128] / mixed[:, 128:]).astype(BF)

    for source in range(HEADS):
        upper = o_buf[pl.ds(offs[source], half), :]
        lower = o_buf[pl.ds(pl.multiple_of(offs[source] + half, 16), half), :]
        out_ref[source] = jnp.where(lane_h < 64, swap_halves(upper), lower)


def middle_kernel(
    att_ref, tok_ref, w_out_ref, out_gain_ref, w_dec_ref, mask_ref, pos_ref, gain_ref,
    w_qkv_ref, slots_ref, owner_ref, patch_ref,
    send_ref, y_ref, target_ref, flag_ref, att_buf, qkv_buf, *, groups,
):
    rows, width = tok_ref.shape
    half = rows // 2
    block = rows // groups
    for pair in range(HEADS // 2):
        a, b = att_ref[2 * pair], att_ref[2 * pair + 1]
        cols = slice(128 * pair, 128 * pair + 128)
        att_buf[:half, cols] = jnp.concatenate([a[:, :64], b[:, :64]], axis=1)
        att_buf[half:, cols] = jnp.concatenate([a[:, 64:], b[:, 64:]], axis=1)
    pick = slot_of_row(slots_ref[...])
    seen = jnp.sum(pick, axis=1, keepdims=True)
    attended = dot(pick.astype(BF), att_buf[...]).astype(BF)
    encoded = tok_ref[...].astype(F32) + dot(attended, w_out_ref[...])
    dec_normed = layer_norm(encoded, out_gain_ref[...]).astype(BF)
    dec_tok = dot(dec_normed, w_dec_ref[...]).astype(BF).astype(F32)
    filled = jnp.where(seen > 0.0, dec_tok, as_row(mask_ref[...]))
    decoder_in = (filled + pos_ref[...].astype(F32)).astype(BF)

    owner = owner_ref[...]
    dest = jnp.zeros_like(owner)
    for device in range(1, groups):
        dest = dest + jnp.where(owner >= device * rows, 1, 0)
    local = owner - dest * rows
    first = jnp.min(local.astype(F32), axis=1, keepdims=True).astype(jnp.int32)
    place = dest * block + local - first
    move = slot_of_row(place).astype(BF)
    y = dot(move, decoder_in)
    y_ref[...] = y.astype(BF)
    target_ref[...] = dot(move, patch_ref[...]).astype(BF)
    hidden = jnp.broadcast_to(1.0 - seen, (rows, 128)).astype(BF)
    flag_ref[...] = dot(move, hidden)
    attn_in = layer_norm(y, gain_ref[...]).astype(BF)
    qkv_buf[...] = dot(attn_in, w_qkv_ref[...]).astype(BF).astype(F32)
    att = w_qkv_ref.shape[1] // 3
    size = att // HEADS
    quarter = rows // 4
    for head in range(HEADS):
        at = head * size
        q = qkv_buf[:, at : at + size]
        k = qkv_buf[:, att + at : att + at + size]
        v = qkv_buf[:, 2 * att + at : 2 * att + at + size]
        send_ref[head, :half, :] = jnp.concatenate(
            [k[:half], v[:half], k[half:], v[half:]], axis=1
        ).astype(BF)
        send_ref[head, half:, :] = jnp.concatenate(
            [q[i * quarter : (i + 1) * quarter] for i in range(4)], axis=1
        ).astype(BF)


def dec_attend_kernel(q_ref, kv_ref, out_ref, k_buf, v_buf, *, q_at, rows):
    half = rows // 2
    quarter = rows // 4
    sources = kv_ref.shape[0]
    for source in range(sources):
        for part in range(2):
            block = kv_ref[source, :half, 64 * part : 64 * part + 64]
            at = source * rows + part * half
            k, v = block[:, :32], block[:, 32:]
            k_buf[at : at + half, :] = jnp.concatenate([k, k, k, k], axis=1)
            v_buf[at : at + half, :128] = jnp.concatenate([v, v, v, v], axis=1)
    v_buf[:, 128:] = jnp.ones((v_buf.shape[0], 128), BF)
    scale = LOG2E * 32**-0.5
    lane = lax.broadcasted_iota(jnp.int32, (quarter, 128), 1)
    zone = [(lane >= 32 * i) & (lane < 32 * i + 32) for i in range(4)]

    @pl.loop(0, HEADS)
    def _(source):
        block = q_ref[source, q_at : q_at + quarter, :].astype(F32)
        q = jnp.concatenate([jnp.where(z, block, 0.0) for z in zone], axis=0).astype(BF)
        score = dot_t(q, k_buf[...])
        top = jnp.max(score, axis=1, keepdims=True)
        weight = jnp.exp2((score - top) * scale).astype(BF)
        mixed = dot(weight, v_buf[...])
        mixed = mixed[:, :128] / mixed[:, 128:]
        out = mixed[:quarter]
        for i in range(1, 4):
            out = jnp.where(zone[i], mixed[i * quarter : (i + 1) * quarter], out)
        out_ref[source] = out.astype(BF)


def tail_kernel(
    me_ref, att_ref, y_ref, w_out_ref, feed_gain_ref, w_up_ref, w_down_ref, head_gain_ref,
    w_head_ref, target_ref, flag_ref,
    dec_att_ref, mid_ref, slope_ref, z_ref, zn_ref, dpred_ref, loss_ref, *refs,
):
    *pred_refs, feed_buf, wide_buf, pred_buf = refs
    rows, width = y_ref.shape
    quarter = rows // 4
    pixels = w_head_ref.shape[1]
    hidden = w_up_ref.shape[1]
    blocks = [att_ref[head].astype(F32) for head in range(HEADS)]
    dec_att_ref[...] = jnp.concatenate(
        [
            jnp.concatenate([b[:, 32 * i : 32 * i + 32] for b in blocks], axis=1)
            for i in range(4)
        ],
        axis=0,
    ).astype(BF)
    mid_ref[...] = y_ref[...].astype(F32) + dot(dec_att_ref[...], w_out_ref[...])
    feed_buf[...] = layer_norm(mid_ref[...], feed_gain_ref[...]).astype(BF)
    z_ref[...] = mid_ref[...]
    tile = 512
    c = math.sqrt(2.0 / math.pi)

    @pl.loop(0, hidden // tile)
    def _(step):
        cols = pl.ds(pl.multiple_of(step * tile, tile), tile)
        pre = dot(feed_buf[...], w_up_ref[:, cols])
        square = pre * pre
        t = jnp.tanh(pre * (c + (c * 0.044715) * square))
        gate = 0.5 + 0.5 * t
        slope = gate + (0.5 * pre) * (1.0 - t * t) * (c + (3 * c * 0.044715) * square)
        slope_ref[:, cols] = slope.astype(BF)
        z_ref[...] += dot((pre * gate).astype(BF), w_down_ref[cols, :])

    zn_ref[...] = layer_norm(z_ref[...], head_gain_ref[...]).astype(BF)
    flag = flag_ref[:, :1]
    loss_ref[...] = jnp.zeros_like(loss_ref)

    @pl.loop(0, pixels // tile)
    def _(step):
        cols = pl.ds(pl.multiple_of(step * tile, tile), tile)
        pred = dot(zn_ref[...], w_head_ref[:, cols])
        wide_buf[:, cols] = pred
        err = (pred - target_ref[:, cols].astype(F32)) * flag
        dpred_ref[:, cols] = (err * (2.0 / pixels)).astype(BF)
        part = jnp.sum(jnp.sum(err * err, axis=1, keepdims=True), axis=0, keepdims=True)
        loss_ref[...] += part * (1.0 / pixels)

    share = pred_buf.shape[1]
    for dest in range(pred_buf.shape[0]):
        pred_buf[dest] = wide_buf[dest * share : (dest + 1) * share, :].astype(BF)
    if len(pred_refs) == 1:
        pred_refs[0][...] = pred_buf[...]
    else:
        for index, ref in enumerate(pred_refs):
            ref[...] = pred_buf[me_ref[1] ^ index]


def gather_kernel(me_ref, *refs):
    *parts, out_ref, buf = refs
    share = buf.shape[1]
    for index, ref in enumerate(parts):
        buf[me_ref[1] ^ index] = ref[...].astype(F32)
    for device in range(buf.shape[0]):
        out_ref[device * share : (device + 1) * share, :] = buf[device].astype(BF)


def backward_kernel(
    me_ref, dec_att_ref, mid_ref, slope_ref, z_ref, zn_ref, dpred_ref, loss_ref,
    feed_gain_ref, w_up_ref, w_down_ref, head_gain_ref, w_head_ref,
    keep_ref, send_ref, back_buf, head_buf, out_buf,
):
    hidden = w_up_ref.shape[1]
    width, pixels = w_head_ref.shape
    dz = norm_backward(
        z_ref[...], head_gain_ref[...], dot_t(dpred_ref[...], w_head_ref[...])
    ).astype(BF)
    back_buf[...] = jnp.zeros_like(back_buf)
    tile = 512

    @pl.loop(0, hidden // tile)
    def _(step):
        cols = pl.ds(pl.multiple_of(step * tile, tile), tile)
        back = dot_t(dz, w_down_ref[cols, :]) * slope_ref[:, cols].astype(F32)
        back_buf[...] += dot_t(back.astype(BF), w_up_ref[:, cols])

    mid_grad = (
        dz.astype(F32) + norm_backward(mid_ref[...], feed_gain_ref[...], back_buf[...])
    ).astype(BF)
    first = (((0,), (0,)), ((), ()))
    out_buf[...] = lax.dot_general(
        dec_att_ref[...], mid_grad, first, preferred_element_type=F32
    )

    @pl.loop(0, pixels // tile)
    def _(step):
        cols = pl.ds(pl.multiple_of(step * tile, tile), tile)
        head_buf[:, cols] = lax.dot_general(
            zn_ref[...], dpred_ref[:, cols], first, preferred_element_type=F32
        )

    loss = jnp.broadcast_to(loss_ref[:1, :], (8, 128))
    high = loss.astype(BF)
    low = (loss - high.astype(F32)).astype(BF)
    sums = jnp.concatenate([high.astype(F32), low.astype(F32)], axis=0).astype(BF)
    deep = out_buf.shape[0] // 32
    half = out_buf.shape[1] // 2
    tall = width // 32
    for index in range(32):
        block = index ^ me_ref[0]
        ref = send_ref if index % 2 else keep_ref
        xy, z = index // 2 % 4, index // 8
        ref[xy, z, :, :pixels] = head_buf[
            pl.ds(pl.multiple_of(block * tall, tall), tall), :
        ].astype(BF)
        part = out_buf[pl.ds(pl.multiple_of(block * deep, deep), deep), :]
        ref[xy, z, :, pixels : pixels + half] = jnp.concatenate(
            [part[:, :half], part[:, half:]], axis=0
        ).astype(BF)
        ref[xy, z, :, pixels + half :] = sums


def add_kernel(*refs, count):
    total = refs[0][...].astype(F32)
    for ref in refs[1:count]:
        total = total + ref[...].astype(F32)
    total = total.astype(BF)
    outs = refs[count:]
    if len(outs) == 1:
        outs[0][...] = total
    else:
        for i, ref in enumerate(outs):
            ref[...] = total[i]


def join_kernel(*refs):
    for i, ref in enumerate(refs[:-1]):
        refs[-1][i] = ref[...]


def place_kernel(me_ref, *refs, masked_total):
    blocks, (head_ref, out_ref, loss_ref) = refs[:8], refs[8:]
    pixels = head_ref.shape[1]
    deep = out_ref.shape[0] // 32
    half = out_ref.shape[1] // 2
    tall = head_ref.shape[0] // 32
    for index in range(32):
        block = index ^ me_ref[0]
        value = blocks[index % 2 * 4 + index // 2 % 4][index // 8].astype(F32)
        head_ref[pl.ds(pl.multiple_of(block * tall, tall), tall), :] = value[:, :pixels]
        at = pl.ds(pl.multiple_of(block * deep, deep), deep)
        out_ref[at, :half] = value[:deep, pixels : pixels + half]
        out_ref[at, half:] = value[deep:, pixels : pixels + half]
    value = blocks[0][0].astype(F32)
    total = value[:8, pixels + half :] + value[8:, pixels + half :]
    loss_ref[0, 0] = jnp.max(total) * (1.0 / masked_total)


def vmem_call(kernel, outs, scratch, inputs, smem=(), smem_out=(), anywhere=(),
              vmem=VMEM_LIMIT, flops=0):
    space = [
        pl.BlockSpec(
            memory_space=pltpu.SMEM if i in smem else pl.ANY if i in anywhere else pltpu.VMEM
        )
        for i in range(len(inputs))
    ]
    moved = sum(a.size * a.dtype.itemsize for a in inputs)
    return pl.pallas_call(
        kernel,
        out_shape=outs,
        in_specs=space,
        out_specs=[
            pl.BlockSpec(memory_space=pltpu.SMEM if i in smem_out else pltpu.VMEM)
            for i in range(len(outs))
        ],
        scratch_shapes=scratch,
        compiler_params=pltpu.CompilerParams(vmem_limit_bytes=vmem),
        cost_estimate=pl.CostEstimate(flops=flops, bytes_accessed=moved, transcendentals=0),
    )(*inputs)


def swap(x, axis, groups=None):
    return lax.all_to_all(
        x, axis, split_axis=0, concat_axis=0, tiled=True, axis_index_groups=groups
    )


def all_sum(x, groups):
    size = lax.axis_size("dp")
    me = lax.axis_index("dp")
    stages = []
    step = 1
    while step < size:
        pairs = [(i, i ^ step) for i in range(size)]
        upper = (me // step) % 2
        half = x.shape[0] // 2
        mine = lax.dynamic_slice_in_dim(x, upper * half, half, 0)
        other = lax.dynamic_slice_in_dim(x, (1 - upper) * half, half, 0)
        x = mine + lax.ppermute(other, "dp", pairs)
        stages.append((pairs, upper))
        step *= 2
    rows, width = x.shape
    blocks = swap(x.reshape(groups, rows // groups, width), "ctx")
    total = jnp.sum(blocks.astype(F32), axis=0).astype(BF)
    x = swap(jnp.broadcast_to(total[None], blocks.shape), "ctx").reshape(rows, width)
    for pairs, upper in reversed(stages):
        other = lax.ppermute(x, "dp", pairs)
        low = jnp.where(upper == 0, x, other)
        high = jnp.where(upper == 0, other, x)
        x = jnp.concatenate([low, high], axis=0)
    return x


def across(x, dp_bit, ctx_bits):
    count, groups = lax.axis_size("dp"), lax.axis_size("ctx")
    pairs = [
        (i * groups + j, (i ^ dp_bit) * groups + (j ^ ctx_bits))
        for i in range(count)
        for j in range(groups)
    ]
    return lax.ppermute(x, ("dp", "ctx"), pairs)


PLANE = ((2, 0), (0, 1), (2, 1))
COLUMN = ((0, 2), (0, 4), (0, 6))


def sum_by_permutes(keep, send, ahead):
    shape = jax.ShapeDtypeStruct
    add = lambda parts, outs: vmem_call(
        functools.partial(add_kernel, count=len(parts)), outs, [], parts
    )
    part, block = shape(keep.shape[1:], BF), shape(keep.shape[2:], BF)
    parts = add([keep, across(send, 1, 0)], [part] * 4)
    others = [across(p, *bits) for p, bits in zip(parts[1:], PLANE)]
    first, ahead = lax.optimization_barrier((parts[0], ahead))
    blocks = add([first, *others], [block] * 4)
    others = [across(b, *bits) for b, bits in zip(blocks[1:], COLUMN)]
    (total,) = add([blocks[0], *others], [block])
    (column,) = vmem_call(
        join_kernel, [part], [], [total] + [across(total, *bits) for bits in COLUMN]
    )
    ours = [column] + [across(column, *bits) for bits in PLANE]
    return ours, [across(x, 1, 0) for x in ours], ahead


def sum_by_blocks(keep, send, groups):
    size = keep.shape[0] * keep.shape[1] * keep.shape[2]
    flat = jnp.concatenate([keep.reshape(size, -1), send.reshape(size, -1)], axis=0)
    unit = lax.axis_size("dp") * groups
    used = flat.shape[0]
    padded = -(-used // unit) * unit
    total = all_sum(jnp.pad(flat, ((0, padded - used), (0, 0))), groups)[:used]
    total = total.reshape(2, *keep.shape)
    return [total[0, i] for i in range(4)], [total[1, i] for i in range(4)]


def on_device(
    patches,
    enc_pos,
    w_embed,
    enc_gain,
    w_qkv,
    w_out,
    enc_out_gain,
    w_dec_embed,
    mask_token,
    dec_pos,
    dec_attn_gain,
    decoder_query_key_value_weight,
    w_dec_out,
    decoder_feed_gain,
    w_up,
    w_down,
    head_gain,
    w_head,
    visible_rows,
    visible_count,
    owner_slot,
):
    groups = lax.axis_size("ctx")
    repeat = groups // HEADS
    teams = [list(range(HEADS * i, HEADS * i + HEADS)) for i in range(repeat)]
    teams = None if repeat == 1 else teams
    dp_me, ctx_me = lax.axis_index("dp"), lax.axis_index("ctx")
    place = dp_me % 2 + 2 * (dp_me // 2) + 4 * (ctx_me % 2) + 8 * (ctx_me // 2)
    if repeat > 1:
        place = jnp.zeros_like(place)
    me = jnp.stack([place, ctx_me, ctx_me // HEADS * HEADS]).astype(jnp.int32)
    source, me = lax.optimization_barrier((patches[0], me))
    rows, pixels = source.shape
    half, quarter = rows // 2, rows // 4
    share = rows // 3
    width = w_embed.shape[1]
    dec_width = w_dec_embed.shape[1]
    shape = jax.ShapeDtypeStruct

    send, tok = vmem_call(
        embed_kernel,
        [shape((HEADS, half + rows + 16, 128), BF), shape((rows, width), BF)],
        [
            pltpu.VMEM((rows, width), BF),
            pltpu.VMEM((rows, w_qkv.shape[1]), BF),
            pltpu.VMEM(source.shape, BF),
            pltpu.VMEM(enc_pos.shape, BF),
            pltpu.VMEM(w_embed.shape, BF),
            pltpu.VMEM(w_qkv.shape, BF),
            pltpu.SemaphoreType.DMA,
            pltpu.SemaphoreType.DMA,
            pltpu.SemaphoreType.DMA((width // 256,)),
            pltpu.SemaphoreType.DMA((w_qkv.shape[1] // 256,)),
        ],
        [source, enc_pos, w_embed, enc_gain, w_qkv, visible_rows],
        anywhere=(0, 1, 2, 4),
        vmem=56 << 20,
        flops=2 * rows * width * (pixels + w_qkv.shape[1]),
    )
    if repeat == 1:
        q = kv = swap(send, "ctx")
        q_at, kv_at = 0, half
    else:
        q = swap(send[:, :half], "ctx", teams)
        kv = swap(jnp.tile(send[:, half:], (repeat, 1, 1)), "ctx")
        q_at, kv_at = 0, 0
    cap_k = (share + 16) * groups
    cap_q = min(HEADS * rows, cap_k)
    (att,) = vmem_call(
        functools.partial(
            enc_attend_kernel, q_at=q_at, kv_at=kv_at, rows=rows, cap_q=cap_q, cap_k=cap_k
        ),
        [shape((HEADS, half, 128), BF)],
        [
            pltpu.VMEM((cap_q + rows, 128), BF),
            pltpu.VMEM((cap_k + rows, 256), BF),
            pltpu.VMEM((cap_q + rows, 128), BF),
        ],
        [me, q, kv],
        smem=(0,),
        flops=4 * cap_q * cap_k * 128,
    )
    att = swap(att, "ctx", teams)
    send, y_own, target, flag = vmem_call(
        functools.partial(middle_kernel, groups=groups),
        [
            shape((HEADS, half + quarter, 128), BF),
            shape((rows, dec_width), BF),
            shape((rows, pixels), BF),
            shape((rows, 128), F32),
        ],
        [
            pltpu.VMEM((rows, w_out.shape[0]), BF),
            pltpu.VMEM((rows, decoder_query_key_value_weight.shape[1]), F32),
        ],
        [
            att, tok, w_out, enc_out_gain, w_dec_embed, mask_token, dec_pos,
            dec_attn_gain, decoder_query_key_value_weight, visible_rows, owner_slot, source,
        ],
        flops=2 * rows * width * 1024,
    )
    if repeat == 1:
        q = kv = swap(send, "ctx")
        q_at = half
    else:
        q = swap(send[:, half:], "ctx", teams)
        kv = swap(jnp.tile(send[:, :half], (repeat, 1, 1)), "ctx")
        q_at = 0
    (att,) = vmem_call(
        functools.partial(dec_attend_kernel, q_at=q_at, rows=rows),
        [shape((HEADS, quarter, 128), BF)],
        [pltpu.VMEM((groups * rows, 128), BF), pltpu.VMEM((groups * rows, 256), BF)],
        [q, kv],
        flops=4 * HEADS * rows * groups * rows * 128,
    )
    att = swap(att, "ctx", teams)
    hidden = w_up.shape[1]
    share_rows = rows // groups
    dec_att, y_mid, slope, z, zn, dpred, loss_part, *preds = vmem_call(
        tail_kernel,
        [
            shape((rows, w_dec_out.shape[0]), BF),
            shape((rows, dec_width), F32),
            shape((rows, hidden), BF),
            shape((rows, dec_width), F32),
            shape((rows, dec_width), BF),
            shape((rows, pixels), BF),
            shape((8, 128), F32),
        ]
        + (
            [shape((share_rows, pixels), BF)] * groups
            if repeat == 1
            else [shape((groups, share_rows, pixels), BF)]
        ),
        [
            pltpu.VMEM((rows, dec_width), BF),
            pltpu.VMEM((rows, pixels), F32),
            pltpu.VMEM((groups, share_rows, pixels), BF),
        ],
        [
            me, att, y_own, w_dec_out, decoder_feed_gain, w_up, w_down, head_gain, w_head,
            target, flag,
        ],
        smem=(0,),
        flops=2 * rows * dec_width * (2 * hidden + pixels),
    )
    if repeat == 1:
        preds = [preds[0]] + [across(preds[i], 0, i) for i in range(1, groups)]
    wide = pixels + dec_width // 2 + 128
    keep, send = vmem_call(
        backward_kernel,
        [shape((4, 4, dec_width // 32, wide), BF)] * 2,
        [
            pltpu.VMEM((rows, dec_width), F32),
            pltpu.VMEM((dec_width, pixels), F32),
            pltpu.VMEM((w_dec_out.shape[0], dec_width), F32),
        ],
        [
            me, dec_att, y_mid, slope, z, zn, dpred, loss_part, decoder_feed_gain,
            w_up, w_down, head_gain, w_head,
        ],
        smem=(0,),
        flops=2 * rows * dec_width * (2 * hidden + 2 * pixels),
    )
    if repeat == 1:
        ours, theirs, preds = sum_by_permutes(keep, send, preds)
        (reconstruction,) = vmem_call(
            gather_kernel,
            [shape((rows, pixels), BF)],
            [pltpu.VMEM((groups, share_rows, pixels), F32)],
            [me, *preds],
            smem=(0,),
        )
    else:
        ours, theirs = sum_by_blocks(keep, send, groups)
        reconstruction = swap(preds[0], "ctx")
    masked_total = lax.axis_size("dp") * (groups * rows - share * groups)
    grad_head, grad_dec_out, loss = vmem_call(
        functools.partial(place_kernel, masked_total=masked_total),
        [shape(w_head.shape, F32), shape(w_dec_out.shape, F32), shape((1, 1), F32)],
        [],
        [me, *ours, *theirs],
        smem=(0,),
        smem_out=(2,),
    )
    return (reconstruction.reshape(1, rows, pixels), grad_head, grad_dec_out, loss.reshape(()))


def solution(mesh):
    in_specs = (
        P("dp", "ctx", None),
        P("ctx", None),
        P(),
        P(),
        P(),
        P(),
        P(),
        P(),
        P(),
        P("ctx", None),
        P(),
        P(),
        P(),
        P(),
        P(),
        P(),
        P(),
        P(),
        P("dp", "ctx"),
        P("dp", "ctx"),
        P("dp", "ctx"),
    )
    out_specs = (P("dp", "ctx", None), P(), P(), P())
    return jax.shard_map(
        on_device, mesh=mesh, in_specs=in_specs, out_specs=out_specs, check_vma=False
    )
```

```python
import functools
import math

import jax
import jax.numpy as jnp
from jax import lax
from jax.experimental import pallas as pl
from jax.experimental.pallas import tpu as pltpu
from jax.sharding import PartitionSpec as P

HEADS = 8
BF = jnp.bfloat16
F32 = jnp.float32
LOG2E = math.log2(math.e)
VMEM_LIMIT = 24 << 20


def as_row(vector):
    return vector.astype(F32).reshape(1, -1)


def layer_norm(x, gain):
    row_mean = jnp.mean(x, axis=-1, keepdims=True)
    centered_input = x - row_mean
    var = jnp.mean(centered_input * centered_input, axis=-1, keepdims=True)
    return centered_input * lax.rsqrt(var + 1e-06) * as_row(gain)


def norm_backward(z, gain, upstream):
    row_mean = jnp.mean(z, axis=-1, keepdims=True)
    centered_input = z - row_mean
    inverse_scale = lax.rsqrt(
        jnp.mean(centered_input * centered_input, axis=-1, keepdims=True) + 1e-06
    )
    normalized_input = centered_input * inverse_scale
    input_gradient = upstream * as_row(gain)
    return inverse_scale * (
        input_gradient
        - jnp.mean(input_gradient, axis=-1, keepdims=True)
        - normalized_input * jnp.mean(input_gradient * normalized_input, axis=-1, keepdims=True)
    )


def dot(a, b):
    return jnp.dot(a, b, preferred_element_type=F32)


def dot_t(a, b):
    return lax.dot_general(a, b, (((1,), (1,)), ((), ())), preferred_element_type=F32)


def swap_halves(x):
    half = x.shape[1] // 2
    return jnp.concatenate([x[:, half:], x[:, :half]], axis=1)


def slot_of_row(slots_row):
    size = slots_row.shape[1]
    row = lax.broadcasted_iota(jnp.int32, (size, size), 0)
    return jnp.where(row == slots_row, 1.0, 0.0)


def embed_kernel(
    patch_hbm, pos_hbm, w_embed_hbm, gain_ref, w_qkv_hbm, slots_ref,
    send_ref, tok_ref, normed_ref, qkv_ref, patch_ref, pos_ref, w_embed_ref, w_qkv_ref,
    patch_sem, pos_sem, embed_sem, qkv_sem,
):
    rows, width = patch_ref.shape
    half = rows // 2
    att = w_qkv_ref.shape[1] // 3
    size = att // HEADS
    tile = 256

    def piece(hbm, buf, sem, step):
        cols = slice(step * tile, (step + 1) * tile)
        return pltpu.make_async_copy(hbm.at[:, cols], buf.at[:, cols], sem.at[step])

    embed_copies = [
        piece(w_embed_hbm, w_embed_ref, embed_sem, i) for i in range(width // tile)
    ]
    qkv_copies = [piece(w_qkv_hbm, w_qkv_ref, qkv_sem, i) for i in range(3 * att // tile)]
    patch_copy = pltpu.make_async_copy(patch_hbm, patch_ref, patch_sem)
    pos_copy = pltpu.make_async_copy(pos_hbm, pos_ref, pos_sem)
    for copy in [patch_copy, embed_copies[0], pos_copy, *embed_copies[1:], *qkv_copies]:
        copy.start()
    patch_copy.wait()
    for step in range(width // tile):
        embed_copies[step].wait()
        if step == 0:
            pos_copy.wait()
        cols = slice(step * tile, (step + 1) * tile)
        tok_ref[:, cols] = (
            dot(patch_ref[...], w_embed_ref[:, cols]) + pos_ref[:, cols].astype(F32)
        ).astype(BF)

    pick = slot_of_row(slots_ref[...]).astype(BF)
    normed = layer_norm(tok_ref[...].astype(F32), gain_ref[...]).astype(BF)
    normed_ref[...] = lax.dot_general(
        pick, normed, (((0,), (0,)), ((), ())), preferred_element_type=F32
    ).astype(BF)
    for step in range(3 * att // tile):
        qkv_copies[step].wait()
        cols = slice(step * tile, (step + 1) * tile)
        qkv_ref[:, cols] = dot(normed_ref[...], w_qkv_ref[:, cols]).astype(BF)

    count = jnp.sum(jnp.where(slots_ref[...] >= 0, 1.0, 0.0), axis=1, keepdims=True)
    high = jnp.floor(count * (1.0 / 16))
    lane = lax.broadcasted_iota(jnp.int32, (16, 128), 1)
    info = jnp.where(lane < 64, high, count - 16.0 * high).astype(BF)
    for head in range(HEADS):
        at = head * size
        q = qkv_ref[:, at : at + size]
        k = qkv_ref[:, att + at : att + at + size]
        v = qkv_ref[:, 2 * att + at : 2 * att + at + size]
        send_ref[head, :half, :] = jnp.concatenate([q[:half], q[half:]], axis=1)
        send_ref[head, half : half + rows, :] = jnp.concatenate([k, v], axis=1)
        send_ref[head, half + rows :, :] = info


def enc_attend_kernel(
    me_ref, q_ref, kv_ref, out_ref, q_buf, kv_buf, o_buf, *, q_at, kv_at, rows, cap_q, cap_k
):
    half = rows // 2
    sources = kv_ref.shape[0]
    lane16 = lax.broadcasted_iota(jnp.int32, (16, 128), 1)
    lane_h = lax.broadcasted_iota(jnp.int32, (half, 128), 1)

    def count_of(source):
        info = kv_ref[source, kv_at + rows : kv_at + rows + 16, :].astype(F32)
        high = jnp.max(jnp.where(lane16 < 64, info, 0.0)).astype(jnp.int32)
        low = jnp.max(jnp.where(lane16 >= 64, info, 0.0)).astype(jnp.int32)
        return high * 16 + low

    q_buf[...] = jnp.zeros_like(q_buf)
    o_buf[...] = jnp.zeros_like(o_buf)
    kv_buf[:, :128] = jnp.zeros((kv_buf.shape[0], 128), BF)
    kv_buf[:, 128:] = jnp.ones((kv_buf.shape[0], 128), BF)

    key = lax.broadcasted_iota(jnp.int32, (1, cap_k), 1)
    valid = jnp.zeros((1, cap_k), F32)
    off = jnp.int32(0)
    for source in range(sources):
        count = count_of(source)
        off = pl.multiple_of(off, 16)
        kv_buf[pl.ds(off, rows), :128] = kv_ref[source, kv_at : kv_at + rows, :]
        valid = jnp.where((key >= off) & (key < off + count), 1.0, valid)
        off = off + (count + 15) // 16 * 16
    bias = jnp.where(valid > 0.0, 0.0, -1e30)

    offs = []
    off = jnp.int32(0)
    for source in range(HEADS):
        off = pl.multiple_of(off, 16)
        offs.append(off)
        block = q_ref[source, q_at : q_at + half, :]
        zero = jnp.zeros_like(block)
        q_buf[pl.ds(off, half), :] = jnp.where(lane_h < 64, block, zero)
        q_buf[pl.ds(off + half, half), :] = jnp.where(lane_h < 64, swap_halves(block), zero)
        off = off + (count_of(me_ref[2] + source) + 15) // 16 * 16
    total = off

    tile = 128
    scale = LOG2E * 64**-0.5

    @pl.loop(0, cap_q // tile)
    def _(step):
        @pl.when(step * tile < total)
        def _():
            at = pl.ds(pl.multiple_of(step * tile, tile), tile)
            score = dot_t(q_buf[at, :], kv_buf[:cap_k, :128]) + bias
            top = jnp.max(score, axis=1, keepdims=True)
            weight = jnp.exp2((score - top) * scale).astype(BF)
            mixed = dot(weight, kv_buf[:cap_k, :])
            o_buf[at, :] = (mixed[:, :128] / mixed[:, 128:]).astype(BF)

    for source in range(HEADS):
        upper = o_buf[pl.ds(offs[source], half), :]
        lower = o_buf[pl.ds(pl.multiple_of(offs[source] + half, 16), half), :]
        out_ref[source] = jnp.where(lane_h < 64, swap_halves(upper), lower)


def middle_kernel(
    att_ref, tok_ref, w_out_ref, out_gain_ref, w_dec_ref, mask_ref, pos_ref, gain_ref,
    w_qkv_ref, slots_ref, owner_ref, patch_ref,
    send_ref, y_ref, target_ref, flag_ref, att_buf, qkv_buf, *, groups,
):
    rows, width = tok_ref.shape
    half = rows // 2
    block = rows // groups
    for pair in range(HEADS // 2):
        a, b = att_ref[2 * pair], att_ref[2 * pair + 1]
        cols = slice(128 * pair, 128 * pair + 128)
        att_buf[:half, cols] = jnp.concatenate([a[:, :64], b[:, :64]], axis=1)
        att_buf[half:, cols] = jnp.concatenate([a[:, 64:], b[:, 64:]], axis=1)
    pick = slot_of_row(slots_ref[...])
    seen = jnp.sum(pick, axis=1, keepdims=True)
    attended = dot(pick.astype(BF), att_buf[...]).astype(BF)
    encoded = tok_ref[...].astype(F32) + dot(attended, w_out_ref[...])
    dec_normed = layer_norm(encoded, out_gain_ref[...]).astype(BF)
    dec_tok = dot(dec_normed, w_dec_ref[...]).astype(BF).astype(F32)
    filled = jnp.where(seen > 0.0, dec_tok, as_row(mask_ref[...]))
    decoder_in = (filled + pos_ref[...].astype(F32)).astype(BF)

    owner = owner_ref[...]
    dest = jnp.zeros_like(owner)
    for device in range(1, groups):
        dest = dest + jnp.where(owner >= device * rows, 1, 0)
    local = owner - dest * rows
    first = jnp.min(local.astype(F32), axis=1, keepdims=True).astype(jnp.int32)
    place = dest * block + local - first
    move = slot_of_row(place).astype(BF)
    y = dot(move, decoder_in)
    y_ref[...] = y.astype(BF)
    target_ref[...] = dot(move, patch_ref[...]).astype(BF)
    hidden = jnp.broadcast_to(1.0 - seen, (rows, 128)).astype(BF)
    flag_ref[...] = dot(move, hidden)
    attn_in = layer_norm(y, gain_ref[...]).astype(BF)
    qkv_buf[...] = dot(attn_in, w_qkv_ref[...]).astype(BF).astype(F32)
    att = w_qkv_ref.shape[1] // 3
    size = att // HEADS
    quarter = rows // 4
    for head in range(HEADS):
        at = head * size
        q = qkv_buf[:, at : at + size]
        k = qkv_buf[:, att + at : att + at + size]
        v = qkv_buf[:, 2 * att + at : 2 * att + at + size]
        send_ref[head, :half, :] = jnp.concatenate(
            [k[:half], v[:half], k[half:], v[half:]], axis=1
        ).astype(BF)
        send_ref[head, half:, :] = jnp.concatenate(
            [q[i * quarter : (i + 1) * quarter] for i in range(4)], axis=1
        ).astype(BF)


def dec_attend_kernel(q_ref, kv_ref, out_ref, k_buf, v_buf, *, q_at, rows):
    half = rows // 2
    quarter = rows // 4
    sources = kv_ref.shape[0]
    for source in range(sources):
        for part in range(2):
            block = kv_ref[source, :half, 64 * part : 64 * part + 64]
            at = source * rows + part * half
            k, v = block[:, :32], block[:, 32:]
            k_buf[at : at + half, :] = jnp.concatenate([k, k, k, k], axis=1)
            v_buf[at : at + half, :128] = jnp.concatenate([v, v, v, v], axis=1)
    v_buf[:, 128:] = jnp.ones((v_buf.shape[0], 128), BF)
    scale = LOG2E * 32**-0.5
    lane = lax.broadcasted_iota(jnp.int32, (quarter, 128), 1)
    zone = [(lane >= 32 * i) & (lane < 32 * i + 32) for i in range(4)]

    chunk = 256
    unroll = 4 if sources == HEADS else 1

    def attend(source):
        block = q_ref[source, q_at : q_at + quarter, :].astype(F32)
        q = jnp.concatenate([jnp.where(z, block, 0.0) for z in zone], axis=0).astype(BF)
        top = mixed = None
        for at in range(0, k_buf.shape[0], chunk):
            score = dot_t(q, k_buf[at : at + chunk, :])
            peak = jnp.max(score, axis=1, keepdims=True)
            new = peak if top is None else jnp.maximum(top, peak)
            weight = jnp.exp2((score - new) * scale).astype(BF)
            part = dot(weight, v_buf[at : at + chunk, :])
            mixed = part if top is None else mixed * jnp.exp2((top - new) * scale) + part
            top = new
        mixed = mixed[:, :128] / mixed[:, 128:]
        out = mixed[:quarter]
        for i in range(1, 4):
            out = jnp.where(zone[i], mixed[i * quarter : (i + 1) * quarter], out)
        out_ref[source] = out.astype(BF)

    @pl.loop(0, HEADS // unroll)
    def _(step):
        for i in range(unroll):
            attend(step * unroll + i)


def tail_kernel(
    me_ref, att_ref, y_ref, w_out_ref, feed_gain_ref, w_up_ref, w_down_ref, head_gain_ref,
    w_head_ref, target_ref, flag_ref,
    dec_att_ref, mid_ref, slope_ref, z_ref, dpred_ref, loss_ref, keep_ref, send_ref, *refs,
):
    *zn_refs, feed_buf, zn_buf, split_buf, head_buf = refs
    rows, width = y_ref.shape
    pixels = w_head_ref.shape[1]
    hidden = w_up_ref.shape[1]
    blocks = [att_ref[head].astype(F32) for head in range(HEADS)]
    dec_att_ref[...] = jnp.concatenate(
        [
            jnp.concatenate([b[:, 32 * i : 32 * i + 32] for b in blocks], axis=1)
            for i in range(4)
        ],
        axis=0,
    ).astype(BF)
    mid_ref[...] = y_ref[...].astype(F32) + dot(dec_att_ref[...], w_out_ref[...])
    feed_buf[...] = layer_norm(mid_ref[...], feed_gain_ref[...]).astype(BF)
    z_ref[...] = mid_ref[...]
    tile = 512
    c = math.sqrt(2.0 / math.pi)
    for at in range(0, hidden, tile):
        cols = slice(at, at + tile)
        pre = dot(feed_buf[...], w_up_ref[:, cols])
        square = pre * pre
        t = jnp.tanh(pre * (c + (c * 0.044715) * square))
        gate = 0.5 + 0.5 * t
        slope = gate + (0.5 * pre) * (1.0 - t * t) * (c + (3 * c * 0.044715) * square)
        slope_ref[:, cols] = slope.astype(BF)
        z_ref[...] += dot((pre * gate).astype(BF), w_down_ref[cols, :])

    zn = layer_norm(z_ref[...], head_gain_ref[...])
    zn_buf[...] = zn.astype(BF)
    share = split_buf.shape[1]
    for dest in range(split_buf.shape[0]):
        split_buf[dest] = zn[dest * share : (dest + 1) * share, :].astype(BF)
    if len(zn_refs) == 1:
        zn_refs[0][...] = split_buf[...]
    else:
        for index in range(2 * zn_refs[0].shape[0]):
            zn_refs[index % 2][index // 2] = split_buf[me_ref[1] ^ index]
    flag = flag_ref[:, :1]
    loss = jnp.zeros((1, 1), F32)
    for at in range(0, pixels, tile):
        cols = slice(at, at + tile)
        pred = dot(zn_buf[...], w_head_ref[:, cols])
        err = (pred - target_ref[:, cols].astype(F32)) * flag
        dpred_ref[:, cols] = (err * (2.0 / pixels)).astype(BF)
        loss += jnp.sum(jnp.sum(err * err, axis=1, keepdims=True), axis=0, keepdims=True)
        head_buf[:, cols] = lax.dot_general(
            zn_buf[...], dpred_ref[:, cols], (((0,), (0,)), ((), ())), preferred_element_type=F32
        )
    loss_ref[...] = jnp.broadcast_to(loss * (1.0 / pixels), loss_ref.shape)
    tall = width // 32
    for index in range(32):
        at = pl.multiple_of((index ^ me_ref[0]) * tall, tall)
        ref = send_ref if index % 2 else keep_ref
        ref[index // 2 % 4, index // 8] = head_buf[pl.ds(at, tall), :].astype(BF)


def gather_kernel(me_ref, w_head_ref, *refs, places):
    *parts, out_ref, split_buf, zn_buf = refs
    share = split_buf.shape[1]
    for ref, indices in zip(parts, places):
        for i, index in enumerate(indices):
            split_buf[me_ref[3] ^ index] = ref[i].astype(F32)
    zn_buf[...] = jnp.concatenate(
        [split_buf[device] for device in range(split_buf.shape[0])], axis=0
    ).astype(BF)
    tile = 512
    for at in range(0, w_head_ref.shape[1], tile):
        cols = slice(at, at + tile)
        out_ref[:, cols] = dot(zn_buf[...], w_head_ref[:, cols]).astype(BF)


def head_back_kernel(dpred_ref, z_ref, head_gain_ref, w_head_ref, dz_ref):
    dz_ref[...] = norm_backward(
        z_ref[...], head_gain_ref[...], dot_t(dpred_ref[...], w_head_ref[...])
    ).astype(BF)


def backward_kernel(
    me_ref, dec_att_ref, mid_ref, slope_ref, dz_ref, loss_ref, feed_gain_ref, w_up_ref, w_down_ref,
    keep_ref, send_ref, back_buf, out_buf,
):
    hidden = w_up_ref.shape[1]
    dz = dz_ref[...]
    tile = 512
    for at in range(0, hidden, tile):
        cols = slice(at, at + tile)
        back = dot_t(dz, w_down_ref[cols, :]) * slope_ref[:, cols].astype(F32)
        part = dot_t(back.astype(BF), w_up_ref[:, cols])
        back_buf[...] = part if at == 0 else back_buf[...] + part

    mid_grad = (
        dz.astype(F32) + norm_backward(mid_ref[...], feed_gain_ref[...], back_buf[...])
    ).astype(BF)
    out_buf[...] = lax.dot_general(
        dec_att_ref[...], mid_grad, (((0,), (0,)), ((), ())), preferred_element_type=F32
    )
    loss = loss_ref[...]
    high = loss.astype(BF)
    low = (loss - high.astype(F32)).astype(BF)
    sums = jnp.concatenate([high.astype(F32), low.astype(F32)], axis=0).astype(BF)
    deep = out_buf.shape[0] // 32
    half = out_buf.shape[1] // 2
    for index in range(32):
        at = pl.multiple_of((index ^ me_ref[0]) * deep, deep)
        ref = send_ref if index % 2 else keep_ref
        xy, z = index // 2 % 4, index // 8
        part = out_buf[pl.ds(at, deep), :]
        ref[xy, z, :, :half] = jnp.concatenate([part[:, :half], part[:, half:]], axis=0).astype(BF)
        ref[xy, z, :, half:] = sums


def pair_kernel(keep_ref, got_ref, mine_ref, other_ref, *refs):
    total = (keep_ref[...].astype(F32) + got_ref[...].astype(F32)).astype(BF)
    for i in range(4):
        refs[i][...] = total[i]
    for i in range(1, 4):
        refs[3 + i][0] = mine_ref[i]
        refs[3 + i][1] = other_ref[i]


def merge_kernel(*refs):
    head = sum(ref[...].astype(F32) for ref in refs[:4]).astype(BF)
    out = sum(ref[...].astype(F32) for ref in refs[4:8]).astype(BF)
    pixels = head.shape[2]
    for i, ref in enumerate(refs[8:]):
        ref[:, :pixels] = head[i]
        ref[:, pixels:] = out[i]


def add_kernel(*refs, count):
    total = refs[0][...].astype(F32)
    for ref in refs[1:count]:
        total = total + ref[...].astype(F32)
    total = total.astype(BF)
    outs = refs[count:]
    if len(outs) == 1:
        outs[0][...] = total
    else:
        for i, ref in enumerate(outs):
            ref[...] = total[i]


def join_kernel(*refs):
    for i, ref in enumerate(refs[:-1]):
        refs[-1][i] = ref[...]


def place_kernel(me_ref, *refs, masked_total):
    blocks, (head_ref, out_ref, loss_ref) = refs[:8], refs[8:]
    pixels = head_ref.shape[1]
    deep = out_ref.shape[0] // 32
    half = out_ref.shape[1] // 2
    tall = head_ref.shape[0] // 32
    for index in range(32):
        block = index ^ me_ref[0]
        value = blocks[index % 2 * 4 + index // 2 % 4][index // 8].astype(F32)
        head_ref[pl.ds(pl.multiple_of(block * tall, tall), tall), :] = value[:, :pixels]
        at = pl.ds(pl.multiple_of(block * deep, deep), deep)
        out_ref[at, :half] = value[:deep, pixels : pixels + half]
        out_ref[at, half:] = value[deep:, pixels : pixels + half]
    value = blocks[0][0].astype(F32)
    total = value[:8, pixels + half :] + value[8:, pixels + half :]
    loss_ref[0, 0] = jnp.max(total) * (1.0 / masked_total)


def vmem_call(kernel, outs, scratch, inputs, smem=(), smem_out=(), anywhere=(),
              vmem=VMEM_LIMIT, flops=0):
    space = [
        pl.BlockSpec(
            memory_space=pltpu.SMEM if i in smem else pl.ANY if i in anywhere else pltpu.VMEM
        )
        for i in range(len(inputs))
    ]
    moved = sum(a.size * a.dtype.itemsize for a in inputs)
    return pl.pallas_call(
        kernel,
        out_shape=outs,
        in_specs=space,
        out_specs=[
            pl.BlockSpec(memory_space=pltpu.SMEM if i in smem_out else pltpu.VMEM)
            for i in range(len(outs))
        ],
        scratch_shapes=scratch,
        compiler_params=pltpu.CompilerParams(vmem_limit_bytes=vmem),
        cost_estimate=pl.CostEstimate(flops=flops, bytes_accessed=moved, transcendentals=0),
    )(*inputs)


def swap(x, axis, groups=None):
    return lax.all_to_all(
        x, axis, split_axis=0, concat_axis=0, tiled=True, axis_index_groups=groups
    )


def all_sum(x, groups):
    size = lax.axis_size("dp")
    me = lax.axis_index("dp")
    stages = []
    step = 1
    while step < size:
        pairs = [(i, i ^ step) for i in range(size)]
        upper = (me // step) % 2
        half = x.shape[0] // 2
        mine = lax.dynamic_slice_in_dim(x, upper * half, half, 0)
        other = lax.dynamic_slice_in_dim(x, (1 - upper) * half, half, 0)
        x = mine + lax.ppermute(other, "dp", pairs)
        stages.append((pairs, upper))
        step *= 2
    rows, width = x.shape
    blocks = swap(x.reshape(groups, rows // groups, width), "ctx")
    total = jnp.sum(blocks.astype(F32), axis=0).astype(BF)
    x = swap(jnp.broadcast_to(total[None], blocks.shape), "ctx").reshape(rows, width)
    for pairs, upper in reversed(stages):
        other = lax.ppermute(x, "dp", pairs)
        low = jnp.where(upper == 0, x, other)
        high = jnp.where(upper == 0, other, x)
        x = jnp.concatenate([low, high], axis=0)
    return x


def across(x, dp_bit, ctx_bits):
    count, groups = lax.axis_size("dp"), lax.axis_size("ctx")
    pairs = [
        (i * groups + j, (i ^ dp_bit) * groups + (j ^ ctx_bits))
        for i in range(count)
        for j in range(groups)
    ]
    return lax.ppermute(x, ("dp", "ctx"), pairs)


PLANE = ((2, 0), (0, 1), (2, 1))
COLUMN = ((0, 2), (0, 4), (0, 6))


def sum_by_permutes(head_keep, head_send, zn_keep, zn_send, head_back, backward):
    shape = jax.ShapeDtypeStruct
    head_got = across(head_send, 1, 0)
    zn_got = across(zn_send, 0, 1)
    dz = head_back()
    heads = vmem_call(
        functools.partial(add_kernel, count=2),
        [shape(head_keep.shape[1:], BF)] * 4,
        [],
        [head_keep, head_got],
    )
    mine, dz = lax.optimization_barrier((heads[0], dz))
    heads = [mine] + [across(p, *bits) for p, bits in zip(heads[1:], PLANE)]
    out_keep, out_send = backward(dz)
    out_got = across(out_send, 1, 0)
    *outs, zn1, zn2, zn3 = vmem_call(
        pair_kernel,
        [shape(out_keep.shape[1:], BF)] * 4 + [shape((2, *zn_keep.shape[1:]), BF)] * 3,
        [],
        [out_keep, out_got, zn_keep, zn_got],
    )
    outs = [outs[0]] + [across(p, *bits) for p, bits in zip(outs[1:], PLANE)]
    rest = [across(p, *bits) for p, bits in zip((zn1, zn2, zn3), COLUMN)]
    block = shape((head_keep.shape[2], head_keep.shape[3] + out_keep.shape[3]), BF)
    blocks = vmem_call(merge_kernel, [block] * 4, [], [*heads, *outs])
    others = [across(b, *bits) for b, bits in zip(blocks[1:], COLUMN)]
    (total,) = vmem_call(
        functools.partial(add_kernel, count=4), [block], [], [blocks[0], *others]
    )
    total, *rest = lax.optimization_barrier((total, *rest))
    (column,) = vmem_call(
        join_kernel,
        [shape((4, *block.shape), BF)],
        [],
        [total] + [across(total, *bits) for bits in COLUMN],
    )
    ours = [column] + [across(column, *bits) for bits in PLANE]
    return ours, [across(x, 1, 0) for x in ours], [zn_keep, zn_got, *rest]


def sum_by_blocks(keep, send, groups):
    size = keep.shape[0] * keep.shape[1] * keep.shape[2]
    flat = jnp.concatenate([keep.reshape(size, -1), send.reshape(size, -1)], axis=0)
    unit = lax.axis_size("dp") * groups
    used = flat.shape[0]
    padded = -(-used // unit) * unit
    total = all_sum(jnp.pad(flat, ((0, padded - used), (0, 0))), groups)[:used]
    total = total.reshape(2, *keep.shape)
    return [total[0, i] for i in range(4)], [total[1, i] for i in range(4)]


def on_device(
    patches,
    enc_pos,
    w_embed,
    enc_gain,
    w_qkv,
    w_out,
    enc_out_gain,
    w_dec_embed,
    mask_token,
    dec_pos,
    dec_attn_gain,
    decoder_query_key_value_weight,
    w_dec_out,
    decoder_feed_gain,
    w_up,
    w_down,
    head_gain,
    w_head,
    visible_rows,
    visible_count,
    owner_slot,
):
    groups = lax.axis_size("ctx")
    repeat = groups // HEADS
    teams = [list(range(HEADS * i, HEADS * i + HEADS)) for i in range(repeat)]
    teams = None if repeat == 1 else teams
    dp_me, ctx_me = lax.axis_index("dp"), lax.axis_index("ctx")
    place = dp_me % 2 + 2 * (dp_me // 2) + 4 * (ctx_me % 2) + 8 * (ctx_me // 2)
    if repeat > 1:
        place = jnp.zeros_like(place)
    me = jnp.stack(
        [place, ctx_me, ctx_me // HEADS * HEADS, ctx_me if repeat == 1 else place]
    ).astype(jnp.int32)
    source, me = lax.optimization_barrier((patches[0], me))
    rows, pixels = source.shape
    half, quarter = rows // 2, rows // 4
    share = rows // 3
    width = w_embed.shape[1]
    dec_width = w_dec_embed.shape[1]
    shape = jax.ShapeDtypeStruct

    send, tok = vmem_call(
        embed_kernel,
        [shape((HEADS, half + rows + 16, 128), BF), shape((rows, width), BF)],
        [
            pltpu.VMEM((rows, width), BF),
            pltpu.VMEM((rows, w_qkv.shape[1]), BF),
            pltpu.VMEM(source.shape, BF),
            pltpu.VMEM(enc_pos.shape, BF),
            pltpu.VMEM(w_embed.shape, BF),
            pltpu.VMEM(w_qkv.shape, BF),
            pltpu.SemaphoreType.DMA,
            pltpu.SemaphoreType.DMA,
            pltpu.SemaphoreType.DMA((width // 256,)),
            pltpu.SemaphoreType.DMA((w_qkv.shape[1] // 256,)),
        ],
        [source, enc_pos, w_embed, enc_gain, w_qkv, visible_rows],
        anywhere=(0, 1, 2, 4),
        vmem=56 << 20,
        flops=2 * rows * width * (pixels + w_qkv.shape[1]),
    )
    if repeat == 1:
        q = kv = swap(send, "ctx")
        q_at, kv_at = 0, half
    else:
        q = swap(send[:, :half], "ctx", teams)
        kv = swap(jnp.tile(send[:, half:], (repeat, 1, 1)), "ctx")
        q_at, kv_at = 0, 0
    cap_k = (share + 16) * groups
    cap_q = min(HEADS * rows, cap_k)
    (att,) = vmem_call(
        functools.partial(
            enc_attend_kernel, q_at=q_at, kv_at=kv_at, rows=rows, cap_q=cap_q, cap_k=cap_k
        ),
        [shape((HEADS, half, 128), BF)],
        [
            pltpu.VMEM((cap_q + rows, 128), BF),
            pltpu.VMEM((cap_k + rows, 256), BF),
            pltpu.VMEM((cap_q + rows, 128), BF),
        ],
        [me, q, kv],
        smem=(0,),
        flops=4 * cap_q * cap_k * 128,
    )
    att = swap(att, "ctx", teams)
    send, y_own, target, flag = vmem_call(
        functools.partial(middle_kernel, groups=groups),
        [
            shape((HEADS, half + quarter, 128), BF),
            shape((rows, dec_width), BF),
            shape((rows, pixels), BF),
            shape((rows, 128), F32),
        ],
        [
            pltpu.VMEM((rows, w_out.shape[0]), BF),
            pltpu.VMEM((rows, decoder_query_key_value_weight.shape[1]), F32),
        ],
        [
            att, tok, w_out, enc_out_gain, w_dec_embed, mask_token, dec_pos,
            dec_attn_gain, decoder_query_key_value_weight, visible_rows, owner_slot, source,
        ],
        flops=2 * rows * width * 1024,
    )
    if repeat == 1:
        q = kv = swap(send, "ctx")
        q_at = half
    else:
        q = swap(send[:, half:], "ctx", teams)
        kv = swap(jnp.tile(send[:, :half], (repeat, 1, 1)), "ctx")
        q_at = 0
    (att,) = vmem_call(
        functools.partial(dec_attend_kernel, q_at=q_at, rows=rows),
        [shape((HEADS, quarter, 128), BF)],
        [pltpu.VMEM((groups * rows, 128), BF), pltpu.VMEM((groups * rows, 256), BF)],
        [q, kv],
        flops=4 * HEADS * rows * groups * rows * 128,
    )
    att = swap(att, "ctx", teams)
    hidden = w_up.shape[1]
    share_rows = rows // groups
    tall = dec_width // 32
    split = (groups, share_rows, dec_width)
    dec_att, y_mid, slope, z, dpred, loss_part, head_keep, head_send, *zn = vmem_call(
        tail_kernel,
        [
            shape((rows, w_dec_out.shape[0]), BF),
            shape((rows, dec_width), F32),
            shape((rows, hidden), BF),
            shape((rows, dec_width), F32),
            shape((rows, pixels), BF),
            shape((8, 128), F32),
        ]
        + [shape((4, 4, tall, pixels), BF)] * 2
        + ([shape((4, *split[1:]), BF)] * 2 if repeat == 1 else [shape(split, BF)]),
        [
            pltpu.VMEM((rows, dec_width), BF),
            pltpu.VMEM((rows, dec_width), BF),
            pltpu.VMEM(split, BF),
            pltpu.VMEM((dec_width, pixels), F32),
        ],
        [
            me, att, y_own, w_dec_out, decoder_feed_gain, w_up, w_down, head_gain, w_head,
            target, flag,
        ],
        smem=(0,),
        flops=2 * rows * dec_width * (2 * hidden + 2 * pixels),
    )

    def head_back():
        return vmem_call(
            head_back_kernel,
            [shape((rows, dec_width), BF)],
            [],
            [dpred, z, head_gain, w_head],
            flops=2 * rows * dec_width * pixels,
        )[0]

    def backward(dz):
        return vmem_call(
            backward_kernel,
            [shape((4, 4, tall, dec_width // 2 + 128), BF)] * 2,
            [
                pltpu.VMEM((rows, dec_width), F32),
                pltpu.VMEM((w_dec_out.shape[0], dec_width), F32),
            ],
            [me, dec_att, y_mid, slope, dz, loss_part, decoder_feed_gain, w_up, w_down],
            smem=(0,),
            flops=40 * rows * dec_width * hidden,
        )

    if repeat == 1:
        ours, theirs, zn = sum_by_permutes(head_keep, head_send, *zn, head_back, backward)
        places = [(0,), (1,), (2, 3), (4, 5), (6, 7)]
    else:
        out_keep, out_send = backward(head_back())
        ours, theirs = sum_by_blocks(
            jnp.concatenate([head_keep, out_keep], axis=3),
            jnp.concatenate([head_send, out_send], axis=3),
            groups,
        )
        zn = [swap(zn[0], "ctx")]
        places = [tuple(range(groups))]
    (reconstruction,) = vmem_call(
        functools.partial(gather_kernel, places=places),
        [shape((rows, pixels), BF)],
        [pltpu.VMEM(split, F32), pltpu.VMEM((rows, dec_width), BF)],
        [me, w_head, *zn],
        smem=(0,),
        flops=2 * rows * dec_width * pixels,
    )
    masked_total = lax.axis_size("dp") * (groups * rows - share * groups)
    grad_head, grad_dec_out, loss = vmem_call(
        functools.partial(place_kernel, masked_total=masked_total),
        [shape(w_head.shape, F32), shape(w_dec_out.shape, F32), shape((1, 1), F32)],
        [],
        [me, *ours, *theirs],
        smem=(0,),
        smem_out=(2,),
    )
    return (reconstruction.reshape(1, rows, pixels), grad_head, grad_dec_out, loss.reshape(()))


def solution(mesh):
    in_specs = (
        P("dp", "ctx", None),
        P("ctx", None),
        P(),
        P(),
        P(),
        P(),
        P(),
        P(),
        P(),
        P("ctx", None),
        P(),
        P(),
        P(),
        P(),
        P(),
        P(),
        P(),
        P(),
        P("dp", "ctx"),
        P("dp", "ctx"),
        P("dp", "ctx"),
    )
    out_specs = (P("dp", "ctx", None), P(), P(), P())
    return jax.shard_map(
        on_device, mesh=mesh, in_specs=in_specs, out_specs=out_specs, check_vma=False
    )
```

```python
import functools
import math

import jax
import jax.numpy as jnp
from jax import lax
from jax.experimental import pallas as pl
from jax.experimental.pallas import tpu as pltpu
from jax.sharding import PartitionSpec as P

HEADS = 8
ORDER = (6, 7, 4, 5, 2, 3, 1, 0)
BF = jnp.bfloat16
F32 = jnp.float32
LOG2E = math.log2(math.e)
VMEM_LIMIT = 24 << 20


def as_row(vector):
    return vector.astype(F32).reshape(1, -1)


def layer_norm(x, gain):
    row_mean = jnp.mean(x, axis=-1, keepdims=True)
    centered_input = x - row_mean
    var = jnp.mean(centered_input * centered_input, axis=-1, keepdims=True)
    return centered_input * lax.rsqrt(var + 1e-06) * as_row(gain)


def norm_backward(z, gain, upstream):
    row_mean = jnp.mean(z, axis=-1, keepdims=True)
    centered_input = z - row_mean
    inverse_scale = lax.rsqrt(
        jnp.mean(centered_input * centered_input, axis=-1, keepdims=True) + 1e-06
    )
    normalized_input = centered_input * inverse_scale
    input_gradient = upstream * as_row(gain)
    return inverse_scale * (
        input_gradient
        - jnp.mean(input_gradient, axis=-1, keepdims=True)
        - normalized_input * jnp.mean(input_gradient * normalized_input, axis=-1, keepdims=True)
    )


def dot(a, b):
    return jnp.dot(a, b, preferred_element_type=F32)


def dot_t(a, b):
    return lax.dot_general(a, b, (((1,), (1,)), ((), ())), preferred_element_type=F32)


def swap_halves(x):
    half = x.shape[1] // 2
    return jnp.concatenate([x[:, half:], x[:, :half]], axis=1)


def slot_of_row(slots_row):
    size = slots_row.shape[1]
    row = lax.broadcasted_iota(jnp.int32, (size, size), 0)
    return jnp.where(row == slots_row, 1.0, 0.0)


def embed_kernel(
    me_ref, patch_hbm, pos_hbm, w_embed_hbm, gain_ref, w_qkv_hbm, slots_ref, *refs,
):
    tok_ref, *send_refs = refs[:-12]
    normed_ref, qkv_ref, patch_ref, pos_ref, w_embed_ref, w_qkv_ref, send_buf = refs[-12:-5]
    patch_sem, pos_sem, embed_sem, qkv_sem, send_sem = refs[-5:]
    rows, width = patch_ref.shape
    half = rows // 2
    att = w_qkv_ref.shape[1] // 3
    size = att // HEADS
    tile = 256

    def pieces(hbm, buf, sem):
        return [
            pltpu.make_async_copy(
                hbm.at[at : at + tile], buf.at[at : at + tile], sem.at[at // tile]
            )
            for at in range(0, buf.shape[0], tile)
        ]

    embed_copies = pieces(w_embed_hbm, w_embed_ref, embed_sem)
    qkv_copies = pieces(w_qkv_hbm, w_qkv_ref, qkv_sem)
    patch_copy = pltpu.make_async_copy(patch_hbm, patch_ref, patch_sem)
    pos_copy = pltpu.make_async_copy(pos_hbm, pos_ref, pos_sem)
    for copy in [patch_copy, *embed_copies, pos_copy, *qkv_copies]:
        copy.start()
    patch_copy.wait()
    total = None
    for step, copy in enumerate(embed_copies):
        copy.wait()
        cols = slice(step * tile, (step + 1) * tile)
        part = dot(patch_ref[:, cols], w_embed_ref[cols, :])
        total = part if total is None else total + part
    pos_copy.wait()
    tok_ref[...] = (total + pos_ref[...].astype(F32)).astype(BF)
    pick = slot_of_row(slots_ref[...]).astype(BF)
    normed = layer_norm(tok_ref[...].astype(F32), gain_ref[...]).astype(BF)
    normed_ref[...] = lax.dot_general(
        pick, normed, (((0,), (0,)), ((), ())), preferred_element_type=F32
    ).astype(BF)
    for copy in qkv_copies:
        copy.wait()
    for step in range(3 * att // tile):
        cols = slice(step * tile, (step + 1) * tile)
        qkv_ref[:, cols] = dot(normed_ref[...], w_qkv_ref[:, cols]).astype(BF)

    count = jnp.sum(jnp.where(slots_ref[...] >= 0, 1.0, 0.0), axis=1, keepdims=True)
    high = jnp.floor(count * (1.0 / 16))
    lane = lax.broadcasted_iota(jnp.int32, (16, 128), 1)
    info = jnp.where(lane < 64, high, count - 16.0 * high).astype(BF)
    for head in range(HEADS):
        at = head * size
        q = qkv_ref[:, at : at + size]
        k = qkv_ref[:, att + at : att + at + size]
        v = qkv_ref[:, 2 * att + at : 2 * att + at + size]
        send_buf[head, :half, :] = jnp.concatenate([q[:half], q[half:]], axis=1)
        send_buf[head, half : half + rows, :] = jnp.concatenate([k, v], axis=1)
        send_buf[head, half + rows :, :] = info
    if len(send_refs) == 1:
        copies = [pltpu.make_async_copy(send_buf, send_refs[0], send_sem.at[0])]
    else:
        copies = [
            pltpu.make_async_copy(send_buf.at[me_ref[1] ^ index], ref, send_sem.at[index])
            for index, ref in enumerate(send_refs)
        ]
    for copy in copies:
        copy.start()
    for copy in copies:
        copy.wait()


def enc_attend_kernel(me_ref, *refs, q_at, kv_at, rows, cap_q, cap_k):
    *blocks, out_ref, q_buf, kv_buf, o_buf = refs
    if len(blocks) == HEADS:
        q_of = kv_of = lambda source: blocks[source]
        place_of = lambda source: me_ref[1] ^ ORDER[source]
        sources, first = HEADS, 0
    else:
        q_of, kv_of = blocks[0].at.__getitem__, blocks[1].at.__getitem__
        place_of = lambda source: source
        sources, first = blocks[1].shape[0], me_ref[2]
    half = rows // 2
    lane16 = lax.broadcasted_iota(jnp.int32, (16, 128), 1)
    lane_h = lax.broadcasted_iota(jnp.int32, (half, 128), 1)

    def count_of(source):
        info = kv_of(source)[kv_at + rows : kv_at + rows + 16, :].astype(F32)
        high = jnp.max(jnp.where(lane16 < 64, info, 0.0)).astype(jnp.int32)
        low = jnp.max(jnp.where(lane16 >= 64, info, 0.0)).astype(jnp.int32)
        return high * 16 + low

    q_buf[...] = jnp.zeros_like(q_buf)
    o_buf[...] = jnp.zeros_like(o_buf)
    kv_buf[:, :128] = jnp.zeros((kv_buf.shape[0], 128), BF)
    kv_buf[:, 128:] = jnp.ones((kv_buf.shape[0], 128), BF)

    key = lax.broadcasted_iota(jnp.int32, (1, cap_k), 1)
    valid = jnp.zeros((1, cap_k), F32)
    off = jnp.int32(0)
    for source in range(sources):
        count = count_of(source)
        off = pl.multiple_of(off, 16)
        kv_buf[pl.ds(off, rows), :128] = kv_of(source)[kv_at : kv_at + rows, :]
        valid = jnp.where((key >= off) & (key < off + count), 1.0, valid)
        off = off + (count + 15) // 16 * 16
    bias = jnp.where(valid > 0.0, 0.0, -1e30)

    offs = []
    off = jnp.int32(0)
    for source in range(HEADS):
        off = pl.multiple_of(off, 16)
        offs.append(off)
        block = q_of(source)[q_at : q_at + half, :]
        zero = jnp.zeros_like(block)
        q_buf[pl.ds(off, half), :] = jnp.where(lane_h < 64, block, zero)
        q_buf[pl.ds(off + half, half), :] = jnp.where(lane_h < 64, swap_halves(block), zero)
        off = off + (count_of(first + source) + 15) // 16 * 16
    total = off

    tile = 128
    scale = LOG2E * 64**-0.5

    @pl.loop(0, cap_q // tile)
    def _(step):
        @pl.when(step * tile < total)
        def _():
            at = pl.ds(pl.multiple_of(step * tile, tile), tile)
            score = dot_t(q_buf[at, :], kv_buf[:cap_k, :128]) + bias
            top = jnp.max(score, axis=1, keepdims=True)
            weight = jnp.exp2((score - top) * scale).astype(BF)
            mixed = dot(weight, kv_buf[:cap_k, :])
            o_buf[at, :] = (mixed[:, :128] / mixed[:, 128:]).astype(BF)

    for source in range(HEADS):
        upper = o_buf[pl.ds(offs[source], half), :]
        lower = o_buf[pl.ds(pl.multiple_of(offs[source] + half, 16), half), :]
        out_ref[place_of(source)] = jnp.where(lane_h < 64, swap_halves(upper), lower)


def middle_kernel(
    att_ref, tok_ref, w_out_ref, out_gain_ref, w_dec_ref, mask_ref, pos_ref, gain_ref,
    w_qkv_ref, slots_ref, owner_ref, patch_ref,
    send_ref, y_ref, target_ref, flag_ref, att_buf, qkv_buf, *, groups,
):
    rows, width = tok_ref.shape
    half = rows // 2
    block = rows // groups
    for pair in range(HEADS // 2):
        a, b = att_ref[2 * pair], att_ref[2 * pair + 1]
        cols = slice(128 * pair, 128 * pair + 128)
        att_buf[:half, cols] = jnp.concatenate([a[:, :64], b[:, :64]], axis=1)
        att_buf[half:, cols] = jnp.concatenate([a[:, 64:], b[:, 64:]], axis=1)
    pick = slot_of_row(slots_ref[...])
    seen = jnp.sum(pick, axis=1, keepdims=True)
    attended = dot(pick.astype(BF), att_buf[...]).astype(BF)
    encoded = tok_ref[...].astype(F32) + dot(attended, w_out_ref[...])
    dec_normed = layer_norm(encoded, out_gain_ref[...]).astype(BF)
    dec_tok = dot(dec_normed, w_dec_ref[...]).astype(BF).astype(F32)
    filled = jnp.where(seen > 0.0, dec_tok, as_row(mask_ref[...]))
    decoder_in = (filled + pos_ref[...].astype(F32)).astype(BF)

    owner = owner_ref[...]
    dest = jnp.zeros_like(owner)
    for device in range(1, groups):
        dest = dest + jnp.where(owner >= device * rows, 1, 0)
    local = owner - dest * rows
    first = jnp.min(local.astype(F32), axis=1, keepdims=True).astype(jnp.int32)
    place = dest * block + local - first
    move = slot_of_row(place).astype(BF)
    y = dot(move, decoder_in)
    y_ref[...] = y.astype(BF)
    target_ref[...] = dot(move, patch_ref[...]).astype(BF)
    hidden = jnp.broadcast_to(1.0 - seen, (rows, 128)).astype(BF)
    flag_ref[...] = dot(move, hidden)
    attn_in = layer_norm(y, gain_ref[...]).astype(BF)
    qkv_buf[...] = dot(attn_in, w_qkv_ref[...]).astype(BF).astype(F32)
    att = w_qkv_ref.shape[1] // 3
    size = att // HEADS
    quarter = rows // 4
    for head in range(HEADS):
        at = head * size
        q = qkv_buf[:, at : at + size]
        k = qkv_buf[:, att + at : att + at + size]
        v = qkv_buf[:, 2 * att + at : 2 * att + at + size]
        send_ref[head, :half, :] = jnp.concatenate(
            [k[:half], v[:half], k[half:], v[half:]], axis=1
        ).astype(BF)
        send_ref[head, half:, :] = jnp.concatenate(
            [q[i * quarter : (i + 1) * quarter] for i in range(4)], axis=1
        ).astype(BF)


def dec_attend_kernel(q_ref, kv_ref, out_ref, k_buf, v_buf, *, q_at, rows):
    half = rows // 2
    quarter = rows // 4
    sources = kv_ref.shape[0]
    for source in range(sources):
        for part in range(2):
            block = kv_ref[source, :half, 64 * part : 64 * part + 64]
            at = source * rows + part * half
            k, v = block[:, :32], block[:, 32:]
            k_buf[at : at + half, :] = jnp.concatenate([k, k, k, k], axis=1)
            v_buf[at : at + half, :128] = jnp.concatenate([v, v, v, v], axis=1)
    v_buf[:, 128:] = jnp.ones((v_buf.shape[0], 128), BF)
    scale = LOG2E * 32**-0.5
    lane = lax.broadcasted_iota(jnp.int32, (quarter, 128), 1)
    zone = [(lane >= 32 * i) & (lane < 32 * i + 32) for i in range(4)]

    chunk = 256
    unroll = 4 if sources == HEADS else 1

    def attend(source):
        block = q_ref[source, q_at : q_at + quarter, :].astype(F32)
        q = jnp.concatenate([jnp.where(z, block, 0.0) for z in zone], axis=0).astype(BF)
        top = mixed = None
        for at in range(0, k_buf.shape[0], chunk):
            score = dot_t(q, k_buf[at : at + chunk, :])
            peak = jnp.max(score, axis=1, keepdims=True)
            new = peak if top is None else jnp.maximum(top, peak)
            weight = jnp.exp2((score - new) * scale).astype(BF)
            part = dot(weight, v_buf[at : at + chunk, :])
            mixed = part if top is None else mixed * jnp.exp2((top - new) * scale) + part
            top = new
        mixed = mixed[:, :128] / mixed[:, 128:]
        out = mixed[:quarter]
        for i in range(1, 4):
            out = jnp.where(zone[i], mixed[i * quarter : (i + 1) * quarter], out)
        out_ref[source] = out.astype(BF)

    @pl.loop(0, HEADS // unroll)
    def _(step):
        for i in range(unroll):
            attend(step * unroll + i)


def tail_kernel(
    me_ref, att_ref, y_ref, w_out_ref, feed_gain_ref, w_up_ref, w_down_ref, head_gain_ref,
    w_head_ref, target_ref, flag_ref,
    dec_att_ref, mid_ref, slope_ref, z_ref, dpred_ref, loss_ref, keep_ref, send_ref, *refs,
):
    *zn_refs, feed_buf, zn_buf, split_buf, head_buf = refs
    rows, width = y_ref.shape
    pixels = w_head_ref.shape[1]
    hidden = w_up_ref.shape[1]
    blocks = [att_ref[head].astype(F32) for head in range(HEADS)]
    dec_att_ref[...] = jnp.concatenate(
        [
            jnp.concatenate([b[:, 32 * i : 32 * i + 32] for b in blocks], axis=1)
            for i in range(4)
        ],
        axis=0,
    ).astype(BF)
    mid_ref[...] = y_ref[...].astype(F32) + dot(dec_att_ref[...], w_out_ref[...])
    feed_buf[...] = layer_norm(mid_ref[...], feed_gain_ref[...]).astype(BF)
    z_ref[...] = mid_ref[...]
    tile = 512
    c = math.sqrt(2.0 / math.pi)
    for at in range(0, hidden, tile):
        cols = slice(at, at + tile)
        pre = dot(feed_buf[...], w_up_ref[:, cols])
        square = pre * pre
        t = jnp.tanh(pre * (c + (c * 0.044715) * square))
        gate = 0.5 + 0.5 * t
        slope = gate + (0.5 * pre) * (1.0 - t * t) * (c + (3 * c * 0.044715) * square)
        slope_ref[:, cols] = slope.astype(BF)
        z_ref[...] += dot((pre * gate).astype(BF), w_down_ref[cols, :])

    zn = layer_norm(z_ref[...], head_gain_ref[...])
    zn_buf[...] = zn.astype(BF)
    share = split_buf.shape[1]
    for dest in range(split_buf.shape[0]):
        split_buf[dest] = zn[dest * share : (dest + 1) * share, :].astype(BF)
    if len(zn_refs) == 1:
        zn_refs[0][...] = split_buf[...]
    else:
        for index in range(2 * zn_refs[0].shape[0]):
            zn_refs[index % 2][index // 2] = split_buf[me_ref[1] ^ index]
    flag = flag_ref[:, :1]
    loss = jnp.zeros((1, 1), F32)
    for at in range(0, pixels, tile):
        cols = slice(at, at + tile)
        pred = dot(zn_buf[...], w_head_ref[:, cols])
        err = (pred - target_ref[:, cols].astype(F32)) * flag
        dpred_ref[:, cols] = (err * (2.0 / pixels)).astype(BF)
        loss += jnp.sum(jnp.sum(err * err, axis=1, keepdims=True), axis=0, keepdims=True)
        head_buf[:, cols] = lax.dot_general(
            zn_buf[...], dpred_ref[:, cols], (((0,), (0,)), ((), ())), preferred_element_type=F32
        )
    loss_ref[...] = jnp.broadcast_to(loss * (1.0 / pixels), loss_ref.shape)
    tall = width // 32
    for index in range(32):
        at = pl.multiple_of((index ^ me_ref[0]) * tall, tall)
        ref = send_ref if index % 2 else keep_ref
        ref[index // 2 % 4, index // 8] = head_buf[pl.ds(at, tall), :].astype(BF)


def gather_kernel(me_ref, w_head_ref, *refs, places):
    *parts, out_ref, split_buf, zn_buf = refs
    share = split_buf.shape[1]
    for ref, indices in zip(parts, places):
        for i, index in enumerate(indices):
            split_buf[me_ref[3] ^ index] = ref[i].astype(F32)
    zn_buf[...] = jnp.concatenate(
        [split_buf[device] for device in range(split_buf.shape[0])], axis=0
    ).astype(BF)
    tile = 512
    for at in range(0, w_head_ref.shape[1], tile):
        cols = slice(at, at + tile)
        out_ref[:, cols] = dot(zn_buf[...], w_head_ref[:, cols]).astype(BF)


def head_back_kernel(dpred_ref, z_ref, head_gain_ref, w_head_ref, dz_ref):
    dz_ref[...] = norm_backward(
        z_ref[...], head_gain_ref[...], dot_t(dpred_ref[...], w_head_ref[...])
    ).astype(BF)


def backward_kernel(
    me_ref, dec_att_ref, mid_ref, slope_ref, dz_ref, loss_ref, feed_gain_ref, w_up_ref, w_down_ref,
    keep_ref, send_ref, back_buf, out_buf,
):
    hidden = w_up_ref.shape[1]
    dz = dz_ref[...]
    tile = 512
    for at in range(0, hidden, tile):
        cols = slice(at, at + tile)
        back = dot_t(dz, w_down_ref[cols, :]) * slope_ref[:, cols].astype(F32)
        part = dot_t(back.astype(BF), w_up_ref[:, cols])
        back_buf[...] = part if at == 0 else back_buf[...] + part

    mid_grad = (
        dz.astype(F32) + norm_backward(mid_ref[...], feed_gain_ref[...], back_buf[...])
    ).astype(BF)
    out_buf[...] = lax.dot_general(
        dec_att_ref[...], mid_grad, (((0,), (0,)), ((), ())), preferred_element_type=F32
    )
    loss = loss_ref[...]
    high = loss.astype(BF)
    low = (loss - high.astype(F32)).astype(BF)
    sums = jnp.concatenate([high.astype(F32), low.astype(F32)], axis=0).astype(BF)
    deep = out_buf.shape[0] // 32
    half = out_buf.shape[1] // 2
    for index in range(32):
        at = pl.multiple_of((index ^ me_ref[0]) * deep, deep)
        ref = send_ref if index % 2 else keep_ref
        xy, z = index // 2 % 4, index // 8
        part = out_buf[pl.ds(at, deep), :]
        ref[xy, z, :, :half] = jnp.concatenate([part[:, :half], part[:, half:]], axis=0).astype(BF)
        ref[xy, z, :, half:] = sums


def merge_kernel(
    head_keep_ref, head_got_ref, out_keep_ref, out_got_ref, mine_ref, other_ref, *refs
):
    head = (head_keep_ref[...].astype(F32) + head_got_ref[...].astype(F32)).astype(BF)
    out = (out_keep_ref[...].astype(F32) + out_got_ref[...].astype(F32)).astype(BF)
    pixels = head.shape[3]
    for i in range(4):
        refs[i][:, :, :pixels] = head[i]
        refs[i][:, :, pixels:] = out[i]
    for i in range(1, 4):
        refs[3 + i][0] = mine_ref[i]
        refs[3 + i][1] = other_ref[i]


def add_kernel(*refs, count):
    total = refs[0][...].astype(F32)
    for ref in refs[1:count]:
        total = total + ref[...].astype(F32)
    total = total.astype(BF)
    outs = refs[count:]
    if len(outs) == 1:
        outs[0][...] = total
    else:
        for i, ref in enumerate(outs):
            ref[...] = total[i]


def join_kernel(*refs):
    for i, ref in enumerate(refs[:-1]):
        refs[-1][i] = ref[...]


def place_kernel(me_ref, *refs, masked_total):
    blocks, (head_ref, out_ref, loss_ref) = refs[:8], refs[8:]
    pixels = head_ref.shape[1]
    deep = out_ref.shape[0] // 32
    half = out_ref.shape[1] // 2
    tall = head_ref.shape[0] // 32
    for index in range(32):
        block = index ^ me_ref[0]
        value = blocks[index % 2 * 4 + index // 2 % 4][index // 8].astype(F32)
        head_ref[pl.ds(pl.multiple_of(block * tall, tall), tall), :] = value[:, :pixels]
        at = pl.ds(pl.multiple_of(block * deep, deep), deep)
        out_ref[at, :half] = value[:deep, pixels : pixels + half]
        out_ref[at, half:] = value[deep:, pixels : pixels + half]
    value = blocks[0][0].astype(F32)
    total = value[:8, pixels + half :] + value[8:, pixels + half :]
    loss_ref[0, 0] = jnp.max(total) * (1.0 / masked_total)


def vmem_call(kernel, outs, scratch, inputs, smem=(), smem_out=(), anywhere=(),
              anywhere_out=(), vmem=VMEM_LIMIT, flops=0):
    space = [
        pl.BlockSpec(
            memory_space=pltpu.SMEM if i in smem else pl.ANY if i in anywhere else pltpu.VMEM
        )
        for i in range(len(inputs))
    ]
    moved = sum(a.size * a.dtype.itemsize for a in inputs)
    return pl.pallas_call(
        kernel,
        out_shape=outs,
        in_specs=space,
        out_specs=[
            pl.BlockSpec(
                memory_space=pltpu.SMEM
                if i in smem_out
                else pl.ANY
                if i in anywhere_out
                else pltpu.VMEM
            )
            for i in range(len(outs))
        ],
        scratch_shapes=scratch,
        compiler_params=pltpu.CompilerParams(vmem_limit_bytes=vmem),
        cost_estimate=pl.CostEstimate(flops=flops, bytes_accessed=moved, transcendentals=0),
    )(*inputs)


def swap(x, axis, groups=None):
    return lax.all_to_all(
        x, axis, split_axis=0, concat_axis=0, tiled=True, axis_index_groups=groups
    )


def all_sum(x, groups):
    size = lax.axis_size("dp")
    me = lax.axis_index("dp")
    stages = []
    step = 1
    while step < size:
        pairs = [(i, i ^ step) for i in range(size)]
        upper = (me // step) % 2
        half = x.shape[0] // 2
        mine = lax.dynamic_slice_in_dim(x, upper * half, half, 0)
        other = lax.dynamic_slice_in_dim(x, (1 - upper) * half, half, 0)
        x = mine + lax.ppermute(other, "dp", pairs)
        stages.append((pairs, upper))
        step *= 2
    rows, width = x.shape
    blocks = swap(x.reshape(groups, rows // groups, width), "ctx")
    total = jnp.sum(blocks.astype(F32), axis=0).astype(BF)
    x = swap(jnp.broadcast_to(total[None], blocks.shape), "ctx").reshape(rows, width)
    for pairs, upper in reversed(stages):
        other = lax.ppermute(x, "dp", pairs)
        low = jnp.where(upper == 0, x, other)
        high = jnp.where(upper == 0, other, x)
        x = jnp.concatenate([low, high], axis=0)
    return x


def across(x, dp_bit, ctx_bits):
    count, groups = lax.axis_size("dp"), lax.axis_size("ctx")
    pairs = [
        (i * groups + j, (i ^ dp_bit) * groups + (j ^ ctx_bits))
        for i in range(count)
        for j in range(groups)
    ]
    return lax.ppermute(x, ("dp", "ctx"), pairs)


PLANE = ((2, 0), (0, 1), (2, 1))
COLUMN = ((0, 2), (0, 4), (0, 6))


def sum_by_permutes(head_keep, head_send, zn_keep, zn_send, head_back, backward, rebuild):
    shape = jax.ShapeDtypeStruct
    head_got = across(head_send, 1, 0)
    zn_got = across(zn_send, 0, 1)
    dz, head_got = lax.optimization_barrier((head_back(), head_got))
    out_keep, out_send = backward(dz)
    out_send, zn_got = lax.optimization_barrier((out_send, zn_got))
    out_got = across(out_send, 1, 0)
    block = shape((head_keep.shape[2], head_keep.shape[3] + out_keep.shape[3]), BF)
    part = shape((4, *block.shape), BF)
    pair = shape((2, *zn_keep.shape[1:]), BF)
    *parts, zn1, zn2, zn3 = vmem_call(
        merge_kernel,
        [part] * 4 + [pair] * 3,
        [],
        [head_keep, head_got, out_keep, out_got, zn_keep, zn_got],
    )
    rest = [across(p, *bits) for p, bits in zip((zn1, zn2, zn3), COLUMN)]
    others = [across(p, *bits) for p, bits in zip(parts[1:], PLANE)]
    mine, *rest = lax.optimization_barrier((parts[0], *rest))
    blocks = vmem_call(
        functools.partial(add_kernel, count=4), [block] * 4, [], [*reversed(others), mine]
    )
    others = [across(b, *bits) for b, bits in zip(blocks[1:], COLUMN)]
    (total,) = vmem_call(
        functools.partial(add_kernel, count=4), [block], [], [*reversed(others), blocks[0]]
    )
    (column,) = vmem_call(
        join_kernel,
        [part],
        [],
        [total] + [across(total, *bits) for bits in COLUMN],
    )
    column, reconstruction = lax.optimization_barrier(
        (column, rebuild([zn_keep, zn_got, *rest]))
    )
    ours = [column] + [across(column, *bits) for bits in PLANE]
    return ours, [across(x, 1, 0) for x in ours], reconstruction


def sum_by_blocks(keep, send, groups):
    size = keep.shape[0] * keep.shape[1] * keep.shape[2]
    flat = jnp.concatenate([keep.reshape(size, -1), send.reshape(size, -1)], axis=0)
    unit = lax.axis_size("dp") * groups
    used = flat.shape[0]
    padded = -(-used // unit) * unit
    total = all_sum(jnp.pad(flat, ((0, padded - used), (0, 0))), groups)[:used]
    total = total.reshape(2, *keep.shape)
    return [total[0, i] for i in range(4)], [total[1, i] for i in range(4)]


def on_device(
    patches,
    enc_pos,
    w_embed,
    enc_gain,
    w_qkv,
    w_out,
    enc_out_gain,
    w_dec_embed,
    mask_token,
    dec_pos,
    dec_attn_gain,
    decoder_query_key_value_weight,
    w_dec_out,
    decoder_feed_gain,
    w_up,
    w_down,
    head_gain,
    w_head,
    visible_rows,
    visible_count,
    owner_slot,
):
    groups = lax.axis_size("ctx")
    repeat = groups // HEADS
    teams = [list(range(HEADS * i, HEADS * i + HEADS)) for i in range(repeat)]
    teams = None if repeat == 1 else teams
    dp_me, ctx_me = lax.axis_index("dp"), lax.axis_index("ctx")
    place = dp_me % 2 + 2 * (dp_me // 2) + 4 * (ctx_me % 2) + 8 * (ctx_me // 2)
    if repeat > 1:
        place = jnp.zeros_like(place)
    me = jnp.stack(
        [place, ctx_me, ctx_me // HEADS * HEADS, ctx_me if repeat == 1 else place]
    ).astype(jnp.int32)
    source, me = lax.optimization_barrier((patches[0], me))
    rows, pixels = source.shape
    half, quarter = rows // 2, rows // 4
    share = rows // 3
    width = w_embed.shape[1]
    dec_width = w_dec_embed.shape[1]
    shape = jax.ShapeDtypeStruct

    tall_block = half + rows + 16
    tok, *send = vmem_call(
        embed_kernel,
        [shape((rows, width), BF)]
        + (
            [shape((tall_block, 128), BF)] * HEADS
            if repeat == 1
            else [shape((HEADS, tall_block, 128), BF)]
        ),
        [
            pltpu.VMEM((rows, width), BF),
            pltpu.VMEM((rows, w_qkv.shape[1]), BF),
            pltpu.VMEM(source.shape, BF),
            pltpu.VMEM(enc_pos.shape, BF),
            pltpu.VMEM(w_embed.shape, BF),
            pltpu.VMEM(w_qkv.shape, BF),
            pltpu.VMEM((HEADS, tall_block, 128), BF),
            pltpu.SemaphoreType.DMA,
            pltpu.SemaphoreType.DMA,
            pltpu.SemaphoreType.DMA((pixels // 256,)),
            pltpu.SemaphoreType.DMA((width // 256,)),
            pltpu.SemaphoreType.DMA((HEADS,)),
        ],
        [me, source, enc_pos, w_embed, enc_gain, w_qkv, visible_rows],
        smem=(0,),
        anywhere=(1, 2, 3, 5),
        anywhere_out=range(1, 1 + HEADS),
        vmem=56 << 20,
        flops=2 * rows * width * (pixels + w_qkv.shape[1]),
    )
    if repeat == 1:
        blocks = [across(send[i], 0, i) if i else send[0] for i in ORDER]
        q_at, kv_at = 0, half
    else:
        blocks = [
            swap(send[0][:, :half], "ctx", teams),
            swap(jnp.tile(send[0][:, half:], (repeat, 1, 1)), "ctx"),
        ]
        q_at, kv_at = 0, 0
    cap_k = (share + 16) * groups
    cap_q = min(HEADS * rows, cap_k)
    (att,) = vmem_call(
        functools.partial(
            enc_attend_kernel, q_at=q_at, kv_at=kv_at, rows=rows, cap_q=cap_q, cap_k=cap_k
        ),
        [shape((HEADS, half, 128), BF)],
        [
            pltpu.VMEM((cap_q + rows, 128), BF),
            pltpu.VMEM((cap_k + rows, 256), BF),
            pltpu.VMEM((cap_q + rows, 128), BF),
        ],
        [me, *blocks],
        smem=(0,),
        flops=4 * cap_q * cap_k * 128,
    )
    att = swap(att, "ctx", teams)
    send, y_own, target, flag = vmem_call(
        functools.partial(middle_kernel, groups=groups),
        [
            shape((HEADS, half + quarter, 128), BF),
            shape((rows, dec_width), BF),
            shape((rows, pixels), BF),
            shape((rows, 128), F32),
        ],
        [
            pltpu.VMEM((rows, w_out.shape[0]), BF),
            pltpu.VMEM((rows, decoder_query_key_value_weight.shape[1]), F32),
        ],
        [
            att, tok, w_out, enc_out_gain, w_dec_embed, mask_token, dec_pos,
            dec_attn_gain, decoder_query_key_value_weight, visible_rows, owner_slot, source,
        ],
        flops=2 * rows * width * 1024,
    )
    if repeat == 1:
        q = kv = swap(send, "ctx")
        q_at = half
    else:
        q = swap(send[:, half:], "ctx", teams)
        kv = swap(jnp.tile(send[:, :half], (repeat, 1, 1)), "ctx")
        q_at = 0
    (att,) = vmem_call(
        functools.partial(dec_attend_kernel, q_at=q_at, rows=rows),
        [shape((HEADS, quarter, 128), BF)],
        [pltpu.VMEM((groups * rows, 128), BF), pltpu.VMEM((groups * rows, 256), BF)],
        [q, kv],
        flops=4 * HEADS * rows * groups * rows * 128,
    )
    att = swap(att, "ctx", teams)
    hidden = w_up.shape[1]
    share_rows = rows // groups
    tall = dec_width // 32
    split = (groups, share_rows, dec_width)
    dec_att, y_mid, slope, z, dpred, loss_part, head_keep, head_send, *zn = vmem_call(
        tail_kernel,
        [
            shape((rows, w_dec_out.shape[0]), BF),
            shape((rows, dec_width), F32),
            shape((rows, hidden), BF),
            shape((rows, dec_width), F32),
            shape((rows, pixels), BF),
            shape((8, 128), F32),
        ]
        + [shape((4, 4, tall, pixels), BF)] * 2
        + ([shape((4, *split[1:]), BF)] * 2 if repeat == 1 else [shape(split, BF)]),
        [
            pltpu.VMEM((rows, dec_width), BF),
            pltpu.VMEM((rows, dec_width), BF),
            pltpu.VMEM(split, BF),
            pltpu.VMEM((dec_width, pixels), F32),
        ],
        [
            me, att, y_own, w_dec_out, decoder_feed_gain, w_up, w_down, head_gain, w_head,
            target, flag,
        ],
        smem=(0,),
        flops=2 * rows * dec_width * (2 * hidden + 2 * pixels),
    )

    def head_back():
        return vmem_call(
            head_back_kernel,
            [shape((rows, dec_width), BF)],
            [],
            [dpred, z, head_gain, w_head],
            flops=2 * rows * dec_width * pixels,
        )[0]

    def backward(dz):
        return vmem_call(
            backward_kernel,
            [shape((4, 4, tall, dec_width // 2 + 128), BF)] * 2,
            [
                pltpu.VMEM((rows, dec_width), F32),
                pltpu.VMEM((w_dec_out.shape[0], dec_width), F32),
            ],
            [me, dec_att, y_mid, slope, dz, loss_part, decoder_feed_gain, w_up, w_down],
            smem=(0,),
            flops=40 * rows * dec_width * hidden,
        )

    places = [(0,), (1,), (2, 3), (4, 5), (6, 7)] if repeat == 1 else [tuple(range(groups))]

    def rebuild(parts):
        return vmem_call(
            functools.partial(gather_kernel, places=places),
            [shape((rows, pixels), BF)],
            [pltpu.VMEM(split, F32), pltpu.VMEM((rows, dec_width), BF)],
            [me, w_head, *parts],
            smem=(0,),
            flops=2 * rows * dec_width * pixels,
        )[0]

    if repeat == 1:
        ours, theirs, reconstruction = sum_by_permutes(
            head_keep, head_send, *zn, head_back, backward, rebuild
        )
    else:
        out_keep, out_send = backward(head_back())
        ours, theirs = sum_by_blocks(
            jnp.concatenate([head_keep, out_keep], axis=3),
            jnp.concatenate([head_send, out_send], axis=3),
            groups,
        )
        reconstruction = rebuild([swap(zn[0], "ctx")])
    masked_total = lax.axis_size("dp") * (groups * rows - share * groups)
    grad_head, grad_dec_out, loss = vmem_call(
        functools.partial(place_kernel, masked_total=masked_total),
        [shape(w_head.shape, F32), shape(w_dec_out.shape, F32), shape((1, 1), F32)],
        [],
        [me, *ours, *theirs],
        smem=(0,),
        smem_out=(2,),
    )
    return (reconstruction.reshape(1, rows, pixels), grad_head, grad_dec_out, loss.reshape(()))


def solution(mesh):
    in_specs = (
        P("dp", "ctx", None),
        P("ctx", None),
        P(),
        P(),
        P(),
        P(),
        P(),
        P(),
        P(),
        P("ctx", None),
        P(),
        P(),
        P(),
        P(),
        P(),
        P(),
        P(),
        P(),
        P("dp", "ctx"),
        P("dp", "ctx"),
        P("dp", "ctx"),
    )
    out_specs = (P("dp", "ctx", None), P(), P(), P())
    return jax.shard_map(
        on_device, mesh=mesh, in_specs=in_specs, out_specs=out_specs, check_vma=False
    )
```

```python
import functools
import math

import jax
import jax.numpy as jnp
from jax import lax
from jax.experimental import pallas as pl
from jax.experimental.pallas import tpu as pltpu
from jax.sharding import PartitionSpec as P

HEADS = 8
ORDER = (6, 7, 4, 5, 2, 3, 1, 0)
BF = jnp.bfloat16
F32 = jnp.float32
LOG2E = math.log2(math.e)
VMEM_LIMIT = 24 << 20


def as_row(vector):
    return vector.astype(F32).reshape(1, -1)


def layer_norm(x, gain):
    row_mean = jnp.mean(x, axis=-1, keepdims=True)
    centered_input = x - row_mean
    var = jnp.mean(centered_input * centered_input, axis=-1, keepdims=True)
    return centered_input * lax.rsqrt(var + 1e-06) * as_row(gain)


def norm_backward(z, gain, upstream):
    row_mean = jnp.mean(z, axis=-1, keepdims=True)
    centered_input = z - row_mean
    inverse_scale = lax.rsqrt(
        jnp.mean(centered_input * centered_input, axis=-1, keepdims=True) + 1e-06
    )
    normalized_input = centered_input * inverse_scale
    input_gradient = upstream * as_row(gain)
    return inverse_scale * (
        input_gradient
        - jnp.mean(input_gradient, axis=-1, keepdims=True)
        - normalized_input * jnp.mean(input_gradient * normalized_input, axis=-1, keepdims=True)
    )


def dot(a, b):
    return jnp.dot(a, b, preferred_element_type=F32)


def dot_t(a, b):
    return lax.dot_general(a, b, (((1,), (1,)), ((), ())), preferred_element_type=F32)


def swap_halves(x):
    half = x.shape[1] // 2
    return jnp.concatenate([x[:, half:], x[:, :half]], axis=1)


def slot_of_row(slots_row):
    size = slots_row.shape[1]
    row = lax.broadcasted_iota(jnp.int32, (size, size), 0)
    return jnp.where(row == slots_row, 1.0, 0.0)


def embed_kernel(
    me_ref, patch_hbm, pos_hbm, w_embed_hbm, gain_ref, w_qkv_hbm, slots_ref, *refs,
):
    tok_ref, *send_refs = refs[:-12]
    normed_ref, qkv_ref, patch_ref, pos_ref, w_embed_ref, w_qkv_ref, send_buf = refs[-12:-5]
    patch_sem, pos_sem, embed_sem, qkv_sem, send_sem = refs[-5:]
    rows, width = patch_ref.shape
    half = rows // 2
    att = w_qkv_ref.shape[1] // 3
    size = att // HEADS
    tile = 256

    def pieces(hbm, buf, sem):
        return [
            pltpu.make_async_copy(
                hbm.at[at : at + tile], buf.at[at : at + tile], sem.at[at // tile]
            )
            for at in range(0, buf.shape[0], tile)
        ]

    embed_copies = pieces(w_embed_hbm, w_embed_ref, embed_sem)
    qkv_copies = pieces(w_qkv_hbm, w_qkv_ref, qkv_sem)
    patch_copy = pltpu.make_async_copy(patch_hbm, patch_ref, patch_sem)
    pos_copy = pltpu.make_async_copy(pos_hbm, pos_ref, pos_sem)
    for copy in [patch_copy, *embed_copies, pos_copy, *qkv_copies]:
        copy.start()
    patch_copy.wait()
    total = None
    for step, copy in enumerate(embed_copies):
        copy.wait()
        cols = slice(step * tile, (step + 1) * tile)
        part = dot(patch_ref[:, cols], w_embed_ref[cols, :])
        total = part if total is None else total + part
    pos_copy.wait()
    tok_ref[...] = (total + pos_ref[...].astype(F32)).astype(BF)
    pick = slot_of_row(slots_ref[...]).astype(BF)
    normed = layer_norm(tok_ref[...].astype(F32), gain_ref[...]).astype(BF)
    normed_ref[...] = lax.dot_general(
        pick, normed, (((0,), (0,)), ((), ())), preferred_element_type=F32
    ).astype(BF)
    for copy in qkv_copies:
        copy.wait()
    for step in range(3 * att // tile):
        cols = slice(step * tile, (step + 1) * tile)
        qkv_ref[:, cols] = dot(normed_ref[...], w_qkv_ref[:, cols]).astype(BF)

    count = jnp.sum(jnp.where(slots_ref[...] >= 0, 1.0, 0.0), axis=1, keepdims=True)
    high = jnp.floor(count * (1.0 / 16))
    lane = lax.broadcasted_iota(jnp.int32, (16, 128), 1)
    info = jnp.where(lane < 64, high, count - 16.0 * high).astype(BF)
    for head in range(HEADS):
        at = head * size
        q = qkv_ref[:, at : at + size]
        k = qkv_ref[:, att + at : att + at + size]
        v = qkv_ref[:, 2 * att + at : 2 * att + at + size]
        send_buf[head, :half, :] = jnp.concatenate([q[:half], q[half:]], axis=1)
        send_buf[head, half : half + rows, :] = jnp.concatenate([k, v], axis=1)
        send_buf[head, half + rows :, :] = info
    if len(send_refs) == 1:
        copies = [pltpu.make_async_copy(send_buf, send_refs[0], send_sem.at[0])]
    else:
        copies = [
            pltpu.make_async_copy(send_buf.at[me_ref[1] ^ index], ref, send_sem.at[index])
            for index, ref in enumerate(send_refs)
        ]
    for copy in copies:
        copy.start()
    for copy in copies:
        copy.wait()


def enc_attend_kernel(me_ref, *refs, q_at, kv_at, rows, cap_q, cap_k):
    *blocks, out_ref, q_buf, kv_buf, o_buf = refs
    if len(blocks) == HEADS:
        q_of = kv_of = lambda source: blocks[source]
        place_of = lambda source: me_ref[1] ^ ORDER[source]
        sources, first = HEADS, 0
    else:
        q_of, kv_of = blocks[0].at.__getitem__, blocks[1].at.__getitem__
        place_of = lambda source: source
        sources, first = blocks[1].shape[0], me_ref[2]
    half = rows // 2
    lane16 = lax.broadcasted_iota(jnp.int32, (16, 128), 1)
    lane_h = lax.broadcasted_iota(jnp.int32, (half, 128), 1)

    def count_of(source):
        info = kv_of(source)[kv_at + rows : kv_at + rows + 16, :].astype(F32)
        high = jnp.max(jnp.where(lane16 < 64, info, 0.0)).astype(jnp.int32)
        low = jnp.max(jnp.where(lane16 >= 64, info, 0.0)).astype(jnp.int32)
        return high * 16 + low

    q_buf[...] = jnp.zeros_like(q_buf)
    o_buf[...] = jnp.zeros_like(o_buf)
    kv_buf[:, :128] = jnp.zeros((kv_buf.shape[0], 128), BF)
    kv_buf[:, 128:] = jnp.ones((kv_buf.shape[0], 128), BF)

    key = lax.broadcasted_iota(jnp.int32, (1, cap_k), 1)
    valid = jnp.zeros((1, cap_k), F32)
    off = jnp.int32(0)
    for source in range(sources):
        count = count_of(source)
        off = pl.multiple_of(off, 16)
        kv_buf[pl.ds(off, rows), :128] = kv_of(source)[kv_at : kv_at + rows, :]
        valid = jnp.where((key >= off) & (key < off + count), 1.0, valid)
        off = off + (count + 15) // 16 * 16
    bias = jnp.where(valid > 0.0, 0.0, -1e30)

    offs = []
    off = jnp.int32(0)
    for source in range(HEADS):
        off = pl.multiple_of(off, 16)
        offs.append(off)
        block = q_of(source)[q_at : q_at + half, :]
        zero = jnp.zeros_like(block)
        q_buf[pl.ds(off, half), :] = jnp.where(lane_h < 64, block, zero)
        q_buf[pl.ds(off + half, half), :] = jnp.where(lane_h < 64, swap_halves(block), zero)
        off = off + (count_of(first + source) + 15) // 16 * 16
    total = off

    scale = LOG2E * 64**-0.5

    def attend(at):
        score = dot_t(q_buf[at, :], kv_buf[:cap_k, :128]) + bias
        top = jnp.max(score, axis=1, keepdims=True)
        weight = jnp.exp2((score - top) * scale).astype(BF)
        mixed = dot(weight, kv_buf[:cap_k, :])
        o_buf[at, :] = (mixed[:, :128] / mixed[:, 128:]).astype(BF)

    if cap_q == cap_k:
        for at in range(0, cap_q, cap_q // 4):
            attend(slice(at, at + cap_q // 4))
    else:
        tile = 128

        @pl.loop(0, cap_q // tile)
        def _(step):
            @pl.when(step * tile < total)
            def _():
                attend(pl.ds(pl.multiple_of(step * tile, tile), tile))

    for source in range(HEADS):
        upper = o_buf[pl.ds(offs[source], half), :]
        lower = o_buf[pl.ds(pl.multiple_of(offs[source] + half, 16), half), :]
        out_ref[place_of(source)] = jnp.where(lane_h < 64, swap_halves(upper), lower)


def middle_kernel(
    att_ref, tok_ref, w_out_ref, out_gain_ref, w_dec_ref, mask_ref, pos_ref, gain_ref,
    w_qkv_ref, slots_ref, owner_ref, patch_ref,
    send_ref, y_ref, target_ref, flag_ref, att_buf, qkv_buf, *, groups,
):
    rows, width = tok_ref.shape
    half = rows // 2
    block = rows // groups
    for pair in range(HEADS // 2):
        a, b = att_ref[2 * pair], att_ref[2 * pair + 1]
        cols = slice(128 * pair, 128 * pair + 128)
        att_buf[:half, cols] = jnp.concatenate([a[:, :64], b[:, :64]], axis=1)
        att_buf[half:, cols] = jnp.concatenate([a[:, 64:], b[:, 64:]], axis=1)
    pick = slot_of_row(slots_ref[...])
    seen = jnp.sum(pick, axis=1, keepdims=True)
    attended = dot(pick.astype(BF), att_buf[...]).astype(BF)
    encoded = tok_ref[...].astype(F32) + dot(attended, w_out_ref[...])
    dec_normed = layer_norm(encoded, out_gain_ref[...]).astype(BF)
    dec_tok = dot(dec_normed, w_dec_ref[...]).astype(BF).astype(F32)
    filled = jnp.where(seen > 0.0, dec_tok, as_row(mask_ref[...]))
    decoder_in = (filled + pos_ref[...].astype(F32)).astype(BF)

    owner = owner_ref[...]
    dest = jnp.zeros_like(owner)
    for device in range(1, groups):
        dest = dest + jnp.where(owner >= device * rows, 1, 0)
    local = owner - dest * rows
    first = jnp.min(local.astype(F32), axis=1, keepdims=True).astype(jnp.int32)
    place = dest * block + local - first
    move = slot_of_row(place).astype(BF)
    y = dot(move, decoder_in)
    y_ref[...] = y.astype(BF)
    target_ref[...] = dot(move, patch_ref[...]).astype(BF)
    hidden = jnp.broadcast_to(1.0 - seen, (rows, 128)).astype(BF)
    flag_ref[...] = dot(move, hidden)
    attn_in = layer_norm(y, gain_ref[...]).astype(BF)
    qkv_buf[...] = dot(attn_in, w_qkv_ref[...]).astype(BF).astype(F32)
    att = w_qkv_ref.shape[1] // 3
    size = att // HEADS
    quarter = rows // 4
    for head in range(HEADS):
        at = head * size
        q = qkv_buf[:, at : at + size]
        k = qkv_buf[:, att + at : att + at + size]
        v = qkv_buf[:, 2 * att + at : 2 * att + at + size]
        send_ref[head, :half, :] = jnp.concatenate(
            [k[:half], v[:half], k[half:], v[half:]], axis=1
        ).astype(BF)
        send_ref[head, half:, :] = jnp.concatenate(
            [q[i * quarter : (i + 1) * quarter] for i in range(4)], axis=1
        ).astype(BF)


def dec_attend_kernel(q_ref, kv_ref, out_ref, k_buf, v_buf, *, q_at, rows):
    half = rows // 2
    quarter = rows // 4
    sources = kv_ref.shape[0]
    for source in range(sources):
        for part in range(2):
            block = kv_ref[source, :half, 64 * part : 64 * part + 64]
            at = source * rows + part * half
            k, v = block[:, :32], block[:, 32:]
            k_buf[at : at + half, :] = jnp.concatenate([k, k, k, k], axis=1)
            v_buf[at : at + half, :128] = jnp.concatenate([v, v, v, v], axis=1)
    v_buf[:, 128:] = jnp.ones((v_buf.shape[0], 128), BF)
    scale = LOG2E * 32**-0.5
    lane = lax.broadcasted_iota(jnp.int32, (quarter, 128), 1)
    zone = [(lane >= 32 * i) & (lane < 32 * i + 32) for i in range(4)]

    chunk = 256
    unroll = 4 if sources == HEADS else 1

    def attend(source):
        block = q_ref[source, q_at : q_at + quarter, :].astype(F32)
        q = jnp.concatenate([jnp.where(z, block, 0.0) for z in zone], axis=0).astype(BF)
        top = mixed = None
        for at in range(0, k_buf.shape[0], chunk):
            score = dot_t(q, k_buf[at : at + chunk, :])
            peak = jnp.max(score, axis=1, keepdims=True)
            new = peak if top is None else jnp.maximum(top, peak)
            weight = jnp.exp2((score - new) * scale).astype(BF)
            part = dot(weight, v_buf[at : at + chunk, :])
            mixed = part if top is None else mixed * jnp.exp2((top - new) * scale) + part
            top = new
        mixed = mixed[:, :128] / mixed[:, 128:]
        out = mixed[:quarter]
        for i in range(1, 4):
            out = jnp.where(zone[i], mixed[i * quarter : (i + 1) * quarter], out)
        out_ref[source] = out.astype(BF)

    @pl.loop(0, HEADS // unroll)
    def _(step):
        for i in range(unroll):
            attend(step * unroll + i)


def tail_kernel(
    me_ref, att_ref, y_ref, w_out_ref, feed_gain_ref, w_up_ref, w_down_ref, head_gain_ref,
    w_head_ref, target_ref, flag_ref,
    dec_att_ref, mid_ref, slope_ref, z_ref, dpred_ref, loss_ref, keep_ref, send_ref, *refs,
):
    *zn_refs, feed_buf, zn_buf, split_buf, head_buf = refs
    rows, width = y_ref.shape
    pixels = w_head_ref.shape[1]
    hidden = w_up_ref.shape[1]
    blocks = [att_ref[head].astype(F32) for head in range(HEADS)]
    dec_att_ref[...] = jnp.concatenate(
        [
            jnp.concatenate([b[:, 32 * i : 32 * i + 32] for b in blocks], axis=1)
            for i in range(4)
        ],
        axis=0,
    ).astype(BF)
    mid_ref[...] = y_ref[...].astype(F32) + dot(dec_att_ref[...], w_out_ref[...])
    feed_buf[...] = layer_norm(mid_ref[...], feed_gain_ref[...]).astype(BF)
    z_ref[...] = mid_ref[...]
    tile = 512
    c = math.sqrt(2.0 / math.pi)
    for at in range(0, hidden, tile):
        cols = slice(at, at + tile)
        pre = dot(feed_buf[...], w_up_ref[:, cols])
        square = pre * pre
        t = jnp.tanh(pre * (c + (c * 0.044715) * square))
        gate = 0.5 + 0.5 * t
        slope = gate + (0.5 * pre) * (1.0 - t * t) * (c + (3 * c * 0.044715) * square)
        slope_ref[:, cols] = slope.astype(BF)
        z_ref[...] += dot((pre * gate).astype(BF), w_down_ref[cols, :])

    zn = layer_norm(z_ref[...], head_gain_ref[...])
    zn_buf[...] = zn.astype(BF)
    share = split_buf.shape[1]
    for dest in range(split_buf.shape[0]):
        split_buf[dest] = zn[dest * share : (dest + 1) * share, :].astype(BF)
    if len(zn_refs) == 1:
        zn_refs[0][...] = split_buf[...]
    else:
        for index in range(2 * zn_refs[0].shape[0]):
            zn_refs[index % 2][index // 2] = split_buf[me_ref[1] ^ index]
    flag = flag_ref[:, :1]
    loss = jnp.zeros((1, 1), F32)
    for at in range(0, pixels, tile):
        cols = slice(at, at + tile)
        pred = dot(zn_buf[...], w_head_ref[:, cols])
        err = (pred - target_ref[:, cols].astype(F32)) * flag
        dpred_ref[:, cols] = (err * (2.0 / pixels)).astype(BF)
        loss += jnp.sum(jnp.sum(err * err, axis=1, keepdims=True), axis=0, keepdims=True)
        head_buf[:, cols] = lax.dot_general(
            zn_buf[...], dpred_ref[:, cols], (((0,), (0,)), ((), ())), preferred_element_type=F32
        )
    loss_ref[...] = jnp.broadcast_to(loss * (1.0 / pixels), loss_ref.shape)
    tall = width // 32
    for index in range(32):
        at = pl.multiple_of((index ^ me_ref[0]) * tall, tall)
        ref = send_ref if index % 2 else keep_ref
        ref[index // 2 % 4, index // 8] = head_buf[pl.ds(at, tall), :].astype(BF)


def gather_kernel(me_ref, w_head_ref, *refs, places):
    *parts, out_ref, split_buf, zn_buf = refs
    share = split_buf.shape[1]
    for ref, indices in zip(parts, places):
        for i, index in enumerate(indices):
            split_buf[me_ref[3] ^ index] = ref[i].astype(F32)
    zn_buf[...] = jnp.concatenate(
        [split_buf[device] for device in range(split_buf.shape[0])], axis=0
    ).astype(BF)
    tile = 512
    for at in range(0, w_head_ref.shape[1], tile):
        cols = slice(at, at + tile)
        out_ref[:, cols] = dot(zn_buf[...], w_head_ref[:, cols]).astype(BF)


def head_back_kernel(dpred_ref, z_ref, head_gain_ref, w_head_ref, dz_ref):
    dz_ref[...] = norm_backward(
        z_ref[...], head_gain_ref[...], dot_t(dpred_ref[...], w_head_ref[...])
    ).astype(BF)


def backward_kernel(
    me_ref, dec_att_ref, mid_ref, slope_ref, dz_ref, loss_ref, feed_gain_ref, w_up_ref, w_down_ref,
    keep_ref, send_ref, back_buf, out_buf,
):
    hidden = w_up_ref.shape[1]
    dz = dz_ref[...]
    tile = 512
    for at in range(0, hidden, tile):
        cols = slice(at, at + tile)
        back = dot_t(dz, w_down_ref[cols, :]) * slope_ref[:, cols].astype(F32)
        part = dot_t(back.astype(BF), w_up_ref[:, cols])
        back_buf[...] = part if at == 0 else back_buf[...] + part

    mid_grad = (
        dz.astype(F32) + norm_backward(mid_ref[...], feed_gain_ref[...], back_buf[...])
    ).astype(BF)
    out_buf[...] = lax.dot_general(
        dec_att_ref[...], mid_grad, (((0,), (0,)), ((), ())), preferred_element_type=F32
    )
    loss = loss_ref[...]
    high = loss.astype(BF)
    low = (loss - high.astype(F32)).astype(BF)
    sums = jnp.concatenate([high.astype(F32), low.astype(F32)], axis=0).astype(BF)
    deep = out_buf.shape[0] // 32
    half = out_buf.shape[1] // 2
    for index in range(32):
        at = pl.multiple_of((index ^ me_ref[0]) * deep, deep)
        ref = send_ref if index % 2 else keep_ref
        xy, z = index // 2 % 4, index // 8
        part = out_buf[pl.ds(at, deep), :]
        ref[xy, z, :, :half] = jnp.concatenate([part[:, :half], part[:, half:]], axis=0).astype(BF)
        ref[xy, z, :, half:] = sums


def merge_kernel(
    head_keep_ref, head_got_ref, out_keep_ref, out_got_ref, mine_ref, other_ref, *refs
):
    head = (head_keep_ref[...].astype(F32) + head_got_ref[...].astype(F32)).astype(BF)
    out = (out_keep_ref[...].astype(F32) + out_got_ref[...].astype(F32)).astype(BF)
    pixels = head.shape[3]
    for i in range(4):
        refs[i][:, :, :pixels] = head[i]
        refs[i][:, :, pixels:] = out[i]
    for i in range(1, 4):
        refs[3 + i][0] = mine_ref[i]
        refs[3 + i][1] = other_ref[i]


def add_kernel(*refs, count):
    total = refs[0][...].astype(F32)
    for ref in refs[1:count]:
        total = total + ref[...].astype(F32)
    total = total.astype(BF)
    outs = refs[count:]
    if len(outs) == 1:
        outs[0][...] = total
    else:
        for i, ref in enumerate(outs):
            ref[...] = total[i]


def join_kernel(*refs):
    for i, ref in enumerate(refs[:-1]):
        refs[-1][i] = ref[...]


def place_kernel(me_ref, *refs, masked_total):
    blocks, (head_ref, out_ref, loss_ref) = refs[:8], refs[8:]
    pixels = head_ref.shape[1]
    deep = out_ref.shape[0] // 32
    half = out_ref.shape[1] // 2
    tall = head_ref.shape[0] // 32
    for index in range(32):
        block = index ^ me_ref[0]
        value = blocks[index % 2 * 4 + index // 2 % 4][index // 8].astype(F32)
        head_ref[pl.ds(pl.multiple_of(block * tall, tall), tall), :] = value[:, :pixels]
        at = pl.ds(pl.multiple_of(block * deep, deep), deep)
        out_ref[at, :half] = value[:deep, pixels : pixels + half]
        out_ref[at, half:] = value[deep:, pixels : pixels + half]
    value = blocks[0][0].astype(F32)
    total = value[:8, pixels + half :] + value[8:, pixels + half :]
    loss_ref[0, 0] = jnp.max(total) * (1.0 / masked_total)


def vmem_call(kernel, outs, scratch, inputs, smem=(), smem_out=(), anywhere=(),
              anywhere_out=(), vmem=VMEM_LIMIT, flops=0):
    space = [
        pl.BlockSpec(
            memory_space=pltpu.SMEM if i in smem else pltpu.HBM if i in anywhere else pltpu.VMEM
        )
        for i in range(len(inputs))
    ]
    moved = sum(a.size * a.dtype.itemsize for a in inputs)
    return pl.pallas_call(
        kernel,
        out_shape=outs,
        in_specs=space,
        out_specs=[
            pl.BlockSpec(
                memory_space=pltpu.SMEM
                if i in smem_out
                else pl.ANY
                if i in anywhere_out
                else pltpu.VMEM
            )
            for i in range(len(outs))
        ],
        scratch_shapes=scratch,
        compiler_params=pltpu.CompilerParams(vmem_limit_bytes=vmem),
        cost_estimate=pl.CostEstimate(flops=flops, bytes_accessed=moved, transcendentals=0),
    )(*inputs)


def pinned(x):
    return pltpu.with_memory_space_constraint(x, pltpu.HBM)


def swap(x, axis, groups=None):
    return lax.all_to_all(
        x, axis, split_axis=0, concat_axis=0, tiled=True, axis_index_groups=groups
    )


def all_sum(x, groups):
    size = lax.axis_size("dp")
    me = lax.axis_index("dp")
    stages = []
    step = 1
    while step < size:
        pairs = [(i, i ^ step) for i in range(size)]
        upper = (me // step) % 2
        half = x.shape[0] // 2
        mine = lax.dynamic_slice_in_dim(x, upper * half, half, 0)
        other = lax.dynamic_slice_in_dim(x, (1 - upper) * half, half, 0)
        x = mine + lax.ppermute(other, "dp", pairs)
        stages.append((pairs, upper))
        step *= 2
    rows, width = x.shape
    blocks = swap(x.reshape(groups, rows // groups, width), "ctx")
    total = jnp.sum(blocks.astype(F32), axis=0).astype(BF)
    x = swap(jnp.broadcast_to(total[None], blocks.shape), "ctx").reshape(rows, width)
    for pairs, upper in reversed(stages):
        other = lax.ppermute(x, "dp", pairs)
        low = jnp.where(upper == 0, x, other)
        high = jnp.where(upper == 0, other, x)
        x = jnp.concatenate([low, high], axis=0)
    return x


def across(x, dp_bit, ctx_bits):
    count, groups = lax.axis_size("dp"), lax.axis_size("ctx")
    pairs = [
        (i * groups + j, (i ^ dp_bit) * groups + (j ^ ctx_bits))
        for i in range(count)
        for j in range(groups)
    ]
    return lax.ppermute(x, ("dp", "ctx"), pairs)


PLANE = ((2, 0), (0, 1), (2, 1))
COLUMN = ((0, 2), (0, 4), (0, 6))


def sum_by_permutes(head_keep, head_send, zn_keep, zn_send, head_back, backward, rebuild):
    shape = jax.ShapeDtypeStruct
    head_got = across(head_send, 1, 0)
    zn_got = across(zn_send, 0, 1)
    dz, head_got = lax.optimization_barrier((head_back(), head_got))
    out_keep, out_send = backward(dz)
    out_send, zn_got = lax.optimization_barrier((out_send, zn_got))
    out_got = across(out_send, 1, 0)
    block = shape((head_keep.shape[2], head_keep.shape[3] + out_keep.shape[3]), BF)
    part = shape((4, *block.shape), BF)
    pair = shape((2, *zn_keep.shape[1:]), BF)
    *parts, zn1, zn2, zn3 = vmem_call(
        merge_kernel,
        [part] * 4 + [pair] * 3,
        [],
        [head_keep, head_got, out_keep, out_got, zn_keep, zn_got],
    )
    rest = [across(p, *bits) for p, bits in zip((zn1, zn2, zn3), COLUMN)]
    others = [across(p, *bits) for p, bits in zip(parts[1:], PLANE)]
    mine, *far = lax.optimization_barrier((parts[0], *rest[1:]))
    rest = [rest[0], *far]
    blocks = vmem_call(
        functools.partial(add_kernel, count=4), [block] * 4, [], [*reversed(others), mine]
    )
    others = [across(b, *bits) for b, bits in zip(blocks[1:], COLUMN)]
    (total,) = vmem_call(
        functools.partial(add_kernel, count=4), [block], [], [*reversed(others), blocks[0]]
    )
    (column,) = vmem_call(
        join_kernel,
        [part],
        [],
        [total] + [across(total, *bits) for bits in COLUMN],
    )
    column, reconstruction = lax.optimization_barrier(
        (column, rebuild([zn_keep, zn_got, *rest]))
    )
    ours = [column] + [across(column, *bits) for bits in PLANE]
    return ours, [across(x, 1, 0) for x in ours], reconstruction


def sum_by_blocks(keep, send, groups):
    size = keep.shape[0] * keep.shape[1] * keep.shape[2]
    flat = jnp.concatenate([keep.reshape(size, -1), send.reshape(size, -1)], axis=0)
    unit = lax.axis_size("dp") * groups
    used = flat.shape[0]
    padded = -(-used // unit) * unit
    total = all_sum(jnp.pad(flat, ((0, padded - used), (0, 0))), groups)[:used]
    total = total.reshape(2, *keep.shape)
    return [total[0, i] for i in range(4)], [total[1, i] for i in range(4)]


def on_device(
    patches,
    enc_pos,
    w_embed,
    enc_gain,
    w_qkv,
    w_out,
    enc_out_gain,
    w_dec_embed,
    mask_token,
    dec_pos,
    dec_attn_gain,
    decoder_query_key_value_weight,
    w_dec_out,
    decoder_feed_gain,
    w_up,
    w_down,
    head_gain,
    w_head,
    visible_rows,
    visible_count,
    owner_slot,
):
    groups = lax.axis_size("ctx")
    repeat = groups // HEADS
    teams = [list(range(HEADS * i, HEADS * i + HEADS)) for i in range(repeat)]
    teams = None if repeat == 1 else teams
    dp_me, ctx_me = lax.axis_index("dp"), lax.axis_index("ctx")
    place = dp_me % 2 + 2 * (dp_me // 2) + 4 * (ctx_me % 2) + 8 * (ctx_me // 2)
    if repeat > 1:
        place = jnp.zeros_like(place)
    me = jnp.stack(
        [place, ctx_me, ctx_me // HEADS * HEADS, ctx_me if repeat == 1 else place]
    ).astype(jnp.int32)
    source, me = lax.optimization_barrier((patches[0], me))
    rows, pixels = source.shape
    half, quarter = rows // 2, rows // 4
    share = rows // 3
    width = w_embed.shape[1]
    dec_width = w_dec_embed.shape[1]
    shape = jax.ShapeDtypeStruct

    tall_block = half + rows + 16
    tok, *send = vmem_call(
        embed_kernel,
        [shape((rows, width), BF)]
        + (
            [shape((tall_block, 128), BF)] * HEADS
            if repeat == 1
            else [shape((HEADS, tall_block, 128), BF)]
        ),
        [
            pltpu.VMEM((rows, width), BF),
            pltpu.VMEM((rows, w_qkv.shape[1]), BF),
            pltpu.VMEM(source.shape, BF),
            pltpu.VMEM(enc_pos.shape, BF),
            pltpu.VMEM(w_embed.shape, BF),
            pltpu.VMEM(w_qkv.shape, BF),
            pltpu.VMEM((HEADS, tall_block, 128), BF),
            pltpu.SemaphoreType.DMA,
            pltpu.SemaphoreType.DMA,
            pltpu.SemaphoreType.DMA((pixels // 256,)),
            pltpu.SemaphoreType.DMA((width // 256,)),
            pltpu.SemaphoreType.DMA((HEADS,)),
        ],
        [me]
        + [pinned(x) for x in (source, enc_pos, w_embed, enc_gain, w_qkv, visible_rows)],
        smem=(0,),
        anywhere=(1, 2, 3, 5),
        anywhere_out=range(1, 1 + HEADS),
        vmem=28 << 20,
        flops=2 * rows * width * (pixels + w_qkv.shape[1]),
    )
    if repeat == 1:
        blocks = [across(send[i], 0, i) if i else send[0] for i in ORDER]
        q_at, kv_at = 0, half
    else:
        blocks = [
            swap(send[0][:, :half], "ctx", teams),
            swap(jnp.tile(send[0][:, half:], (repeat, 1, 1)), "ctx"),
        ]
        q_at, kv_at = 0, 0
    cap_k = (share + 16) * groups
    cap_q = min(HEADS * rows, cap_k)
    (att,) = vmem_call(
        functools.partial(
            enc_attend_kernel, q_at=q_at, kv_at=kv_at, rows=rows, cap_q=cap_q, cap_k=cap_k
        ),
        [shape((HEADS, half, 128), BF)],
        [
            pltpu.VMEM((cap_q + rows, 128), BF),
            pltpu.VMEM((cap_k + rows, 256), BF),
            pltpu.VMEM((cap_q + rows, 128), BF),
        ],
        [me, *blocks],
        smem=(0,),
        flops=4 * cap_q * cap_k * 128,
    )
    att = swap(att, "ctx", teams)
    send, y_own, target, flag = vmem_call(
        functools.partial(middle_kernel, groups=groups),
        [
            shape((HEADS, half + quarter, 128), BF),
            shape((rows, dec_width), BF),
            shape((rows, pixels), BF),
            shape((rows, 128), F32),
        ],
        [
            pltpu.VMEM((rows, w_out.shape[0]), BF),
            pltpu.VMEM((rows, decoder_query_key_value_weight.shape[1]), F32),
        ],
        [
            att, tok, w_out, enc_out_gain, w_dec_embed, mask_token, dec_pos,
            dec_attn_gain, decoder_query_key_value_weight, visible_rows, owner_slot, source,
        ],
        flops=2 * rows * width * 1024,
    )
    if repeat == 1:
        q = kv = swap(send, "ctx")
        q_at = half
    else:
        q = swap(send[:, half:], "ctx", teams)
        kv = swap(jnp.tile(send[:, :half], (repeat, 1, 1)), "ctx")
        q_at = 0
    (att,) = vmem_call(
        functools.partial(dec_attend_kernel, q_at=q_at, rows=rows),
        [shape((HEADS, quarter, 128), BF)],
        [pltpu.VMEM((groups * rows, 128), BF), pltpu.VMEM((groups * rows, 256), BF)],
        [q, kv],
        flops=4 * HEADS * rows * groups * rows * 128,
    )
    att = swap(att, "ctx", teams)
    hidden = w_up.shape[1]
    share_rows = rows // groups
    tall = dec_width // 32
    split = (groups, share_rows, dec_width)
    dec_att, y_mid, slope, z, dpred, loss_part, head_keep, head_send, *zn = vmem_call(
        tail_kernel,
        [
            shape((rows, w_dec_out.shape[0]), BF),
            shape((rows, dec_width), F32),
            shape((rows, hidden), BF),
            shape((rows, dec_width), F32),
            shape((rows, pixels), BF),
            shape((8, 128), F32),
        ]
        + [shape((4, 4, tall, pixels), BF)] * 2
        + ([shape((4, *split[1:]), BF)] * 2 if repeat == 1 else [shape(split, BF)]),
        [
            pltpu.VMEM((rows, dec_width), BF),
            pltpu.VMEM((rows, dec_width), BF),
            pltpu.VMEM(split, BF),
            pltpu.VMEM((dec_width, pixels), F32),
        ],
        [
            me, att, y_own, w_dec_out, decoder_feed_gain, w_up, w_down, head_gain, w_head,
            target, flag,
        ],
        smem=(0,),
        flops=2 * rows * dec_width * (2 * hidden + 2 * pixels),
    )

    def head_back():
        return vmem_call(
            head_back_kernel,
            [shape((rows, dec_width), BF)],
            [],
            [dpred, z, head_gain, w_head],
            flops=2 * rows * dec_width * pixels,
        )[0]

    def backward(dz):
        return vmem_call(
            backward_kernel,
            [shape((4, 4, tall, dec_width // 2 + 128), BF)] * 2,
            [
                pltpu.VMEM((rows, dec_width), F32),
                pltpu.VMEM((w_dec_out.shape[0], dec_width), F32),
            ],
            [me, dec_att, y_mid, slope, dz, loss_part, decoder_feed_gain, w_up, w_down],
            smem=(0,),
            flops=40 * rows * dec_width * hidden,
        )

    places = [(0,), (1,), (2, 3), (4, 5), (6, 7)] if repeat == 1 else [tuple(range(groups))]

    def rebuild(parts):
        return vmem_call(
            functools.partial(gather_kernel, places=places),
            [shape((rows, pixels), BF)],
            [pltpu.VMEM(split, F32), pltpu.VMEM((rows, dec_width), BF)],
            [me, w_head, *parts],
            smem=(0,),
            flops=2 * rows * dec_width * pixels,
        )[0]

    if repeat == 1:
        ours, theirs, reconstruction = sum_by_permutes(
            head_keep, head_send, *zn, head_back, backward, rebuild
        )
    else:
        out_keep, out_send = backward(head_back())
        ours, theirs = sum_by_blocks(
            jnp.concatenate([head_keep, out_keep], axis=3),
            jnp.concatenate([head_send, out_send], axis=3),
            groups,
        )
        reconstruction = rebuild([swap(zn[0], "ctx")])
    masked_total = lax.axis_size("dp") * (groups * rows - share * groups)
    grad_head, grad_dec_out, loss = vmem_call(
        functools.partial(place_kernel, masked_total=masked_total),
        [shape(w_head.shape, F32), shape(w_dec_out.shape, F32), shape((1, 1), F32)],
        [],
        [me, *ours, *theirs],
        smem=(0,),
        smem_out=(2,),
    )
    return (reconstruction.reshape(1, rows, pixels), grad_head, grad_dec_out, loss.reshape(()))


def solution(mesh):
    in_specs = (
        P("dp", "ctx", None),
        P("ctx", None),
        P(),
        P(),
        P(),
        P(),
        P(),
        P(),
        P(),
        P("ctx", None),
        P(),
        P(),
        P(),
        P(),
        P(),
        P(),
        P(),
        P(),
        P("dp", "ctx"),
        P("dp", "ctx"),
        P("dp", "ctx"),
    )
    out_specs = (P("dp", "ctx", None), P(), P(), P())
    return jax.shard_map(
        on_device, mesh=mesh, in_specs=in_specs, out_specs=out_specs, check_vma=False
    )
```

```python
import functools
import math

import jax
import jax.numpy as jnp
from jax import lax
from jax.experimental import pallas as pl
from jax.experimental.pallas import tpu as pltpu
from jax.sharding import PartitionSpec as P

HEADS = 8
ORDER = (6, 7, 4, 5, 2, 3, 1, 0)
BF = jnp.bfloat16
F32 = jnp.float32
LOG2E = math.log2(math.e)
VMEM_LIMIT = 24 << 20


def as_row(vector):
    return vector.astype(F32).reshape(1, -1)


def layer_norm(x, gain):
    row_mean = jnp.mean(x, axis=-1, keepdims=True)
    centered_input = x - row_mean
    var = jnp.mean(centered_input * centered_input, axis=-1, keepdims=True)
    return centered_input * lax.rsqrt(var + 1e-06) * as_row(gain)


def norm_backward(z, gain, upstream):
    row_mean = jnp.mean(z, axis=-1, keepdims=True)
    centered_input = z - row_mean
    inverse_scale = lax.rsqrt(
        jnp.mean(centered_input * centered_input, axis=-1, keepdims=True) + 1e-06
    )
    normalized_input = centered_input * inverse_scale
    input_gradient = upstream * as_row(gain)
    return inverse_scale * (
        input_gradient
        - jnp.mean(input_gradient, axis=-1, keepdims=True)
        - normalized_input * jnp.mean(input_gradient * normalized_input, axis=-1, keepdims=True)
    )


def dot(a, b):
    return jnp.dot(a, b, preferred_element_type=F32)


def dot_t(a, b):
    return lax.dot_general(a, b, (((1,), (1,)), ((), ())), preferred_element_type=F32)


def swap_halves(x):
    half = x.shape[1] // 2
    return jnp.concatenate([x[:, half:], x[:, :half]], axis=1)


def slot_of_row(slots_row):
    size = slots_row.shape[1]
    row = lax.broadcasted_iota(jnp.int32, (size, size), 0)
    return jnp.where(row == slots_row, 1.0, 0.0)


def embed_kernel(
    me_ref, patch_hbm, pos_hbm, w_embed_hbm, gain_ref, w_qkv_hbm, slots_ref, *refs,
):
    tok_ref, *send_refs = refs[:-12]
    normed_ref, qkv_ref, patch_ref, pos_ref, w_embed_ref, w_qkv_ref, send_buf = refs[-12:-5]
    patch_sem, pos_sem, embed_sem, qkv_sem, send_sem = refs[-5:]
    rows, width = patch_ref.shape
    half = rows // 2
    att = w_qkv_ref.shape[1] // 3
    size = att // HEADS
    tile = 256

    def pieces(hbm, buf, sem):
        return [
            pltpu.make_async_copy(
                hbm.at[at : at + tile], buf.at[at : at + tile], sem.at[at // tile]
            )
            for at in range(0, buf.shape[0], tile)
        ]

    embed_copies = pieces(w_embed_hbm, w_embed_ref, embed_sem)
    qkv_copies = pieces(w_qkv_hbm, w_qkv_ref, qkv_sem)
    patch_copy = pltpu.make_async_copy(patch_hbm, patch_ref, patch_sem)
    pos_copy = pltpu.make_async_copy(pos_hbm, pos_ref, pos_sem)
    for copy in [patch_copy, *embed_copies, pos_copy, *qkv_copies]:
        copy.start()
    patch_copy.wait()
    total = None
    for step, copy in enumerate(embed_copies):
        copy.wait()
        cols = slice(step * tile, (step + 1) * tile)
        part = dot(patch_ref[:, cols], w_embed_ref[cols, :])
        total = part if total is None else total + part
    pos_copy.wait()
    tok_ref[...] = (total + pos_ref[...].astype(F32)).astype(BF)
    pick = slot_of_row(slots_ref[...]).astype(BF)
    normed = layer_norm(tok_ref[...].astype(F32), gain_ref[...]).astype(BF)
    normed_ref[...] = lax.dot_general(
        pick, normed, (((0,), (0,)), ((), ())), preferred_element_type=F32
    ).astype(BF)
    for copy in qkv_copies:
        copy.wait()
    for step in range(3 * att // tile):
        cols = slice(step * tile, (step + 1) * tile)
        qkv_ref[:, cols] = dot(normed_ref[...], w_qkv_ref[:, cols]).astype(BF)

    count = jnp.sum(jnp.where(slots_ref[...] >= 0, 1.0, 0.0), axis=1, keepdims=True)
    high = jnp.floor(count * (1.0 / 16))
    lane = lax.broadcasted_iota(jnp.int32, (16, 128), 1)
    info = jnp.where(lane < 64, high, count - 16.0 * high).astype(BF)
    for head in range(HEADS):
        at = head * size
        q = qkv_ref[:, at : at + size]
        k = qkv_ref[:, att + at : att + at + size]
        v = qkv_ref[:, 2 * att + at : 2 * att + at + size]
        send_buf[head, :half, :] = jnp.concatenate([q[:half], q[half:]], axis=1)
        send_buf[head, half : half + rows, :] = jnp.concatenate([k, v], axis=1)
        send_buf[head, half + rows :, :] = info
    if len(send_refs) == 1:
        copies = [pltpu.make_async_copy(send_buf, send_refs[0], send_sem.at[0])]
    else:
        copies = [
            pltpu.make_async_copy(send_buf.at[me_ref[1] ^ index], ref, send_sem.at[index])
            for index, ref in enumerate(send_refs)
        ]
    for copy in copies:
        copy.start()
    for copy in copies:
        copy.wait()


def enc_attend_kernel(me_ref, *refs, q_at, kv_at, rows, cap_q, cap_k):
    *blocks, out_ref, q_buf, kv_buf, o_buf = refs
    if len(blocks) == HEADS:
        q_of = kv_of = lambda source: blocks[source]
        place_of = lambda source: me_ref[1] ^ ORDER[source]
        sources, first = HEADS, 0
    else:
        q_of, kv_of = blocks[0].at.__getitem__, blocks[1].at.__getitem__
        place_of = lambda source: source
        sources, first = blocks[1].shape[0], me_ref[2]
    half = rows // 2
    lane16 = lax.broadcasted_iota(jnp.int32, (16, 128), 1)
    lane_h = lax.broadcasted_iota(jnp.int32, (half, 128), 1)

    def count_of(source):
        info = kv_of(source)[kv_at + rows : kv_at + rows + 16, :].astype(F32)
        high = jnp.max(jnp.where(lane16 < 64, info, 0.0)).astype(jnp.int32)
        low = jnp.max(jnp.where(lane16 >= 64, info, 0.0)).astype(jnp.int32)
        return high * 16 + low

    q_buf[...] = jnp.zeros_like(q_buf)
    o_buf[...] = jnp.zeros_like(o_buf)
    kv_buf[:, :128] = jnp.zeros((kv_buf.shape[0], 128), BF)
    kv_buf[:, 128:] = jnp.ones((kv_buf.shape[0], 128), BF)

    key = lax.broadcasted_iota(jnp.int32, (1, cap_k), 1)
    valid = jnp.zeros((1, cap_k), F32)
    off = jnp.int32(0)
    for source in range(sources):
        count = count_of(source)
        off = pl.multiple_of(off, 16)
        kv_buf[pl.ds(off, rows), :128] = kv_of(source)[kv_at : kv_at + rows, :]
        valid = jnp.where((key >= off) & (key < off + count), 1.0, valid)
        off = off + (count + 15) // 16 * 16
    bias = jnp.where(valid > 0.0, 0.0, -1e30)

    offs = []
    off = jnp.int32(0)
    for source in range(HEADS):
        off = pl.multiple_of(off, 16)
        offs.append(off)
        block = q_of(source)[q_at : q_at + half, :]
        zero = jnp.zeros_like(block)
        q_buf[pl.ds(off, half), :] = jnp.where(lane_h < 64, block, zero)
        q_buf[pl.ds(off + half, half), :] = jnp.where(lane_h < 64, swap_halves(block), zero)
        off = off + (count_of(first + source) + 15) // 16 * 16
    total = off

    scale = LOG2E * 64**-0.5

    def attend(at):
        score = dot_t(q_buf[at, :], kv_buf[:cap_k, :128]) + bias
        top = jnp.max(score, axis=1, keepdims=True)
        weight = jnp.exp2((score - top) * scale).astype(BF)
        mixed = dot(weight, kv_buf[:cap_k, :])
        o_buf[at, :] = (mixed[:, :128] / mixed[:, 128:]).astype(BF)

    if cap_q == cap_k:
        for at in range(0, cap_q, cap_q // 4):
            attend(slice(at, at + cap_q // 4))
    else:
        tile = 128

        @pl.loop(0, cap_q // tile)
        def _(step):
            @pl.when(step * tile < total)
            def _():
                attend(pl.ds(pl.multiple_of(step * tile, tile), tile))

    for source in range(HEADS):
        upper = o_buf[pl.ds(offs[source], half), :]
        lower = o_buf[pl.ds(pl.multiple_of(offs[source] + half, 16), half), :]
        out_ref[place_of(source)] = jnp.where(lane_h < 64, swap_halves(upper), lower)


def middle_kernel(
    att_ref, tok_ref, w_out_ref, out_gain_ref, w_dec_ref, mask_ref, pos_ref, gain_ref,
    w_qkv_ref, slots_ref, owner_ref, patch_ref,
    send_ref, y_ref, target_ref, flag_ref, att_buf, qkv_buf, *, groups,
):
    rows, width = tok_ref.shape
    half = rows // 2
    block = rows // groups
    for pair in range(HEADS // 2):
        a, b = att_ref[2 * pair], att_ref[2 * pair + 1]
        cols = slice(128 * pair, 128 * pair + 128)
        att_buf[:half, cols] = jnp.concatenate([a[:, :64], b[:, :64]], axis=1)
        att_buf[half:, cols] = jnp.concatenate([a[:, 64:], b[:, 64:]], axis=1)
    pick = slot_of_row(slots_ref[...])
    seen = jnp.sum(pick, axis=1, keepdims=True)
    attended = dot(pick.astype(BF), att_buf[...]).astype(BF)
    encoded = tok_ref[...].astype(F32) + dot(attended, w_out_ref[...])
    dec_normed = layer_norm(encoded, out_gain_ref[...]).astype(BF)
    dec_tok = dot(dec_normed, w_dec_ref[...]).astype(BF).astype(F32)
    filled = jnp.where(seen > 0.0, dec_tok, as_row(mask_ref[...]))
    decoder_in = (filled + pos_ref[...].astype(F32)).astype(BF)

    owner = owner_ref[...]
    dest = jnp.zeros_like(owner)
    for device in range(1, groups):
        dest = dest + jnp.where(owner >= device * rows, 1, 0)
    local = owner - dest * rows
    first = jnp.min(local.astype(F32), axis=1, keepdims=True).astype(jnp.int32)
    place = dest * block + local - first
    move = slot_of_row(place).astype(BF)
    y = dot(move, decoder_in)
    y_ref[...] = y.astype(BF)
    target_ref[...] = dot(move, patch_ref[...]).astype(BF)
    hidden = jnp.broadcast_to(1.0 - seen, (rows, 128)).astype(BF)
    flag_ref[...] = dot(move, hidden)
    attn_in = layer_norm(y, gain_ref[...]).astype(BF)
    qkv_buf[...] = dot(attn_in, w_qkv_ref[...]).astype(BF).astype(F32)
    att = w_qkv_ref.shape[1] // 3
    size = att // HEADS
    quarter = rows // 4
    for head in range(HEADS):
        at = head * size
        q = qkv_buf[:, at : at + size]
        k = qkv_buf[:, att + at : att + at + size]
        v = qkv_buf[:, 2 * att + at : 2 * att + at + size]
        send_ref[head, :half, :] = jnp.concatenate(
            [k[:half], v[:half], k[half:], v[half:]], axis=1
        ).astype(BF)
        send_ref[head, half:, :] = jnp.concatenate(
            [q[i * quarter : (i + 1) * quarter] for i in range(4)], axis=1
        ).astype(BF)


def dec_attend_kernel(q_ref, kv_ref, out_ref, k_buf, v_buf, *, q_at, rows):
    half = rows // 2
    quarter = rows // 4
    sources = kv_ref.shape[0]
    for source in range(sources):
        for part in range(2):
            block = kv_ref[source, :half, 64 * part : 64 * part + 64]
            at = source * rows + part * half
            k, v = block[:, :32], block[:, 32:]
            k_buf[at : at + half, :] = jnp.concatenate([k, k, k, k], axis=1)
            v_buf[at : at + half, :128] = jnp.concatenate([v, v, v, v], axis=1)
    v_buf[:, 128:] = jnp.ones((v_buf.shape[0], 128), BF)
    scale = LOG2E * 32**-0.5
    lane = lax.broadcasted_iota(jnp.int32, (quarter, 128), 1)
    zone = [(lane >= 32 * i) & (lane < 32 * i + 32) for i in range(4)]

    chunk = 256
    unroll = 4 if sources == HEADS else 1

    def attend(source):
        block = q_ref[source, q_at : q_at + quarter, :].astype(F32)
        q = jnp.concatenate([jnp.where(z, block, 0.0) for z in zone], axis=0).astype(BF)
        top = mixed = None
        for at in range(0, k_buf.shape[0], chunk):
            score = dot_t(q, k_buf[at : at + chunk, :])
            peak = jnp.max(score, axis=1, keepdims=True)
            new = peak if top is None else jnp.maximum(top, peak)
            weight = jnp.exp2((score - new) * scale).astype(BF)
            part = dot(weight, v_buf[at : at + chunk, :])
            mixed = part if top is None else mixed * jnp.exp2((top - new) * scale) + part
            top = new
        mixed = mixed[:, :128] / mixed[:, 128:]
        out = mixed[:quarter]
        for i in range(1, 4):
            out = jnp.where(zone[i], mixed[i * quarter : (i + 1) * quarter], out)
        out_ref[source] = out.astype(BF)

    @pl.loop(0, HEADS // unroll)
    def _(step):
        for i in range(unroll):
            attend(step * unroll + i)


def tail_kernel(
    me_ref, att_ref, y_ref, w_out_ref, feed_gain_ref, w_up_ref, w_down_ref, head_gain_ref,
    w_head_ref, target_ref, flag_ref,
    dec_att_ref, mid_ref, slope_ref, z_ref, dpred_ref, loss_ref, keep_ref, send_ref, *refs,
):
    *zn_refs, feed_buf, zn_buf, split_buf, head_buf = refs
    rows, width = y_ref.shape
    pixels = w_head_ref.shape[1]
    hidden = w_up_ref.shape[1]
    blocks = [att_ref[head].astype(F32) for head in range(HEADS)]
    dec_att_ref[...] = jnp.concatenate(
        [
            jnp.concatenate([b[:, 32 * i : 32 * i + 32] for b in blocks], axis=1)
            for i in range(4)
        ],
        axis=0,
    ).astype(BF)
    mid_ref[...] = y_ref[...].astype(F32) + dot(dec_att_ref[...], w_out_ref[...])
    feed_buf[...] = layer_norm(mid_ref[...], feed_gain_ref[...]).astype(BF)
    z_ref[...] = mid_ref[...]
    tile = 512
    c = math.sqrt(2.0 / math.pi)
    for at in range(0, hidden, tile):
        cols = slice(at, at + tile)
        pre = dot(feed_buf[...], w_up_ref[:, cols])
        square = pre * pre
        t = jnp.tanh(pre * (c + (c * 0.044715) * square))
        gate = 0.5 + 0.5 * t
        slope = gate + (0.5 * pre) * (1.0 - t * t) * (c + (3 * c * 0.044715) * square)
        slope_ref[:, cols] = slope.astype(BF)
        z_ref[...] += dot((pre * gate).astype(BF), w_down_ref[cols, :])

    zn = layer_norm(z_ref[...], head_gain_ref[...])
    zn_buf[...] = zn.astype(BF)
    share = split_buf.shape[1]
    for dest in range(split_buf.shape[0]):
        split_buf[dest] = zn[dest * share : (dest + 1) * share, :].astype(BF)
    if len(zn_refs) == 1:
        zn_refs[0][...] = split_buf[...]
    else:
        for index in range(2 * zn_refs[0].shape[0]):
            zn_refs[index % 2][index // 2] = split_buf[me_ref[1] ^ index]
    flag = flag_ref[:, :1]
    loss = jnp.zeros((1, 1), F32)
    for at in range(0, pixels, tile):
        cols = slice(at, at + tile)
        pred = dot(zn_buf[...], w_head_ref[:, cols])
        err = (pred - target_ref[:, cols].astype(F32)) * flag
        dpred_ref[:, cols] = (err * (2.0 / pixels)).astype(BF)
        loss += jnp.sum(jnp.sum(err * err, axis=1, keepdims=True), axis=0, keepdims=True)
        head_buf[:, cols] = lax.dot_general(
            zn_buf[...], dpred_ref[:, cols], (((0,), (0,)), ((), ())), preferred_element_type=F32
        )
    loss_ref[...] = jnp.broadcast_to(loss * (1.0 / pixels), loss_ref.shape)
    tall = width // 32
    for index in range(32):
        at = pl.multiple_of((index ^ me_ref[0]) * tall, tall)
        ref = send_ref if index % 2 else keep_ref
        ref[index // 2 % 4, index // 8] = head_buf[pl.ds(at, tall), :].astype(BF)


def gather_kernel(me_ref, w_head_ref, *refs, places):
    *parts, out_ref, split_buf, zn_buf = refs
    share = split_buf.shape[1]
    for ref, indices in zip(parts, places):
        for i, index in enumerate(indices):
            split_buf[me_ref[3] ^ index] = ref[i].astype(F32)
    zn_buf[...] = jnp.concatenate(
        [split_buf[device] for device in range(split_buf.shape[0])], axis=0
    ).astype(BF)
    tile = 512
    for at in range(0, w_head_ref.shape[1], tile):
        cols = slice(at, at + tile)
        out_ref[:, cols] = dot(zn_buf[...], w_head_ref[:, cols]).astype(BF)


def head_back_kernel(dpred_ref, z_ref, head_gain_ref, w_head_ref, dz_ref):
    dz_ref[...] = norm_backward(
        z_ref[...], head_gain_ref[...], dot_t(dpred_ref[...], w_head_ref[...])
    ).astype(BF)


def backward_kernel(
    me_ref, dec_att_ref, mid_ref, slope_ref, dz_ref, loss_ref, feed_gain_ref, w_up_ref, w_down_ref,
    keep_ref, send_ref, back_buf, out_buf,
):
    hidden = w_up_ref.shape[1]
    dz = dz_ref[...]
    tile = 512
    for at in range(0, hidden, tile):
        cols = slice(at, at + tile)
        back = dot_t(dz, w_down_ref[cols, :]) * slope_ref[:, cols].astype(F32)
        part = dot_t(back.astype(BF), w_up_ref[:, cols])
        back_buf[...] = part if at == 0 else back_buf[...] + part

    mid_grad = (
        dz.astype(F32) + norm_backward(mid_ref[...], feed_gain_ref[...], back_buf[...])
    ).astype(BF)
    out_buf[...] = lax.dot_general(
        dec_att_ref[...], mid_grad, (((0,), (0,)), ((), ())), preferred_element_type=F32
    )
    loss = loss_ref[...]
    high = loss.astype(BF)
    low = (loss - high.astype(F32)).astype(BF)
    sums = jnp.concatenate([high.astype(F32), low.astype(F32)], axis=0).astype(BF)
    deep = out_buf.shape[0] // 32
    half = out_buf.shape[1] // 2
    for index in range(32):
        at = pl.multiple_of((index ^ me_ref[0]) * deep, deep)
        ref = send_ref if index % 2 else keep_ref
        xy, z = index // 2 % 4, index // 8
        part = out_buf[pl.ds(at, deep), :]
        ref[xy, z, :, :half] = jnp.concatenate([part[:, :half], part[:, half:]], axis=0).astype(BF)
        ref[xy, z, :, half:] = sums


def merge_kernel(
    head_keep_ref, head_got_ref, out_keep_ref, out_got_ref, mine_ref, other_ref, *refs
):
    head = (head_keep_ref[...].astype(F32) + head_got_ref[...].astype(F32)).astype(BF)
    out = (out_keep_ref[...].astype(F32) + out_got_ref[...].astype(F32)).astype(BF)
    pixels = head.shape[3]
    for i in range(4):
        refs[i][:, :, :pixels] = head[i]
        refs[i][:, :, pixels:] = out[i]
    for i in range(1, 4):
        refs[3 + i][0] = mine_ref[i]
        refs[3 + i][1] = other_ref[i]


def add_kernel(*refs, count):
    total = refs[0][...].astype(F32)
    for ref in refs[1:count]:
        total = total + ref[...].astype(F32)
    total = total.astype(BF)
    outs = refs[count:]
    if len(outs) == 1:
        outs[0][...] = total
    else:
        for i, ref in enumerate(outs):
            ref[...] = total[i]


def join_kernel(*refs):
    for i, ref in enumerate(refs[:-1]):
        refs[-1][i] = ref[...]


def place_kernel(me_ref, *refs, masked_total):
    blocks, (head_ref, out_ref, loss_ref) = refs[:8], refs[8:]
    pixels = head_ref.shape[1]
    deep = out_ref.shape[0] // 32
    half = out_ref.shape[1] // 2
    tall = head_ref.shape[0] // 32
    for index in range(32):
        block = index ^ me_ref[0]
        value = blocks[index % 2 * 4 + index // 2 % 4][index // 8].astype(F32)
        head_ref[pl.ds(pl.multiple_of(block * tall, tall), tall), :] = value[:, :pixels]
        at = pl.ds(pl.multiple_of(block * deep, deep), deep)
        out_ref[at, :half] = value[:deep, pixels : pixels + half]
        out_ref[at, half:] = value[deep:, pixels : pixels + half]
    value = blocks[0][0].astype(F32)
    total = value[:8, pixels + half :] + value[8:, pixels + half :]
    loss_ref[0, 0] = jnp.max(total) * (1.0 / masked_total)


def vmem_call(kernel, outs, scratch, inputs, smem=(), smem_out=(), anywhere=(),
              anywhere_out=(), vmem=VMEM_LIMIT, flops=0):
    space = [
        pl.BlockSpec(
            memory_space=pltpu.SMEM if i in smem else pltpu.HBM if i in anywhere else pltpu.VMEM
        )
        for i in range(len(inputs))
    ]
    moved = sum(a.size * a.dtype.itemsize for a in inputs)
    return pl.pallas_call(
        kernel,
        out_shape=outs,
        in_specs=space,
        out_specs=[
            pl.BlockSpec(
                memory_space=pltpu.SMEM
                if i in smem_out
                else pl.ANY
                if i in anywhere_out
                else pltpu.VMEM
            )
            for i in range(len(outs))
        ],
        scratch_shapes=scratch,
        compiler_params=pltpu.CompilerParams(vmem_limit_bytes=vmem),
        cost_estimate=pl.CostEstimate(flops=flops, bytes_accessed=moved, transcendentals=0),
    )(*inputs)


def pinned(x):
    return pltpu.with_memory_space_constraint(x, pltpu.HBM)


def swap(x, axis, groups=None):
    return lax.all_to_all(
        x, axis, split_axis=0, concat_axis=0, tiled=True, axis_index_groups=groups
    )


def all_sum(x, groups):
    size = lax.axis_size("dp")
    me = lax.axis_index("dp")
    stages = []
    step = 1
    while step < size:
        pairs = [(i, i ^ step) for i in range(size)]
        upper = (me // step) % 2
        half = x.shape[0] // 2
        mine = lax.dynamic_slice_in_dim(x, upper * half, half, 0)
        other = lax.dynamic_slice_in_dim(x, (1 - upper) * half, half, 0)
        x = mine + lax.ppermute(other, "dp", pairs)
        stages.append((pairs, upper))
        step *= 2
    rows, width = x.shape
    blocks = swap(x.reshape(groups, rows // groups, width), "ctx")
    total = jnp.sum(blocks.astype(F32), axis=0).astype(BF)
    x = swap(jnp.broadcast_to(total[None], blocks.shape), "ctx").reshape(rows, width)
    for pairs, upper in reversed(stages):
        other = lax.ppermute(x, "dp", pairs)
        low = jnp.where(upper == 0, x, other)
        high = jnp.where(upper == 0, other, x)
        x = jnp.concatenate([low, high], axis=0)
    return x


def across(x, dp_bit, ctx_bits):
    count, groups = lax.axis_size("dp"), lax.axis_size("ctx")
    pairs = [
        (i * groups + j, (i ^ dp_bit) * groups + (j ^ ctx_bits))
        for i in range(count)
        for j in range(groups)
    ]
    return lax.ppermute(x, ("dp", "ctx"), pairs)


PLANE = ((2, 0), (0, 1), (2, 1))
COLUMN = ((0, 2), (0, 4), (0, 6))


def sum_by_permutes(head_keep, head_send, zn_keep, zn_send, head_back, backward, rebuild):
    shape = jax.ShapeDtypeStruct
    head_got = across(head_send, 1, 0)
    zn_got = across(zn_send, 0, 1)
    out_keep, out_send = backward(head_back())
    out_send, head_got, zn_got = lax.optimization_barrier((out_send, head_got, zn_got))
    out_got = across(out_send, 1, 0)
    block = shape((head_keep.shape[2], head_keep.shape[3] + out_keep.shape[3]), BF)
    part = shape((4, *block.shape), BF)
    pair = shape((2, *zn_keep.shape[1:]), BF)
    *parts, zn1, zn2, zn3 = vmem_call(
        merge_kernel,
        [part] * 4 + [pair] * 3,
        [],
        [head_keep, head_got, out_keep, out_got, zn_keep, zn_got],
    )
    rest = [across(p, *bits) for p, bits in zip((zn1, zn2, zn3), COLUMN)]
    others = [across(p, *bits) for p, bits in zip(parts[1:], PLANE)]
    mine, *far = lax.optimization_barrier((parts[0], *rest[1:]))
    rest = [rest[0], *far]
    blocks = vmem_call(
        functools.partial(add_kernel, count=4), [block] * 4, [], [*reversed(others), mine]
    )
    others = [across(b, *bits) for b, bits in zip(blocks[1:], COLUMN)]
    (total,) = vmem_call(
        functools.partial(add_kernel, count=4), [block], [], [*reversed(others), blocks[0]]
    )
    (column,) = vmem_call(
        join_kernel,
        [part],
        [],
        [total] + [across(total, *bits) for bits in COLUMN],
    )
    column, reconstruction = lax.optimization_barrier(
        (column, rebuild([zn_keep, zn_got, *rest]))
    )
    ours = [column] + [across(column, *bits) for bits in PLANE]
    return ours, [across(x, 1, 0) for x in ours], reconstruction


def sum_by_blocks(keep, send, groups):
    size = keep.shape[0] * keep.shape[1] * keep.shape[2]
    flat = jnp.concatenate([keep.reshape(size, -1), send.reshape(size, -1)], axis=0)
    unit = lax.axis_size("dp") * groups
    used = flat.shape[0]
    padded = -(-used // unit) * unit
    total = all_sum(jnp.pad(flat, ((0, padded - used), (0, 0))), groups)[:used]
    total = total.reshape(2, *keep.shape)
    return [total[0, i] for i in range(4)], [total[1, i] for i in range(4)]


def on_device(
    patches,
    enc_pos,
    w_embed,
    enc_gain,
    w_qkv,
    w_out,
    enc_out_gain,
    w_dec_embed,
    mask_token,
    dec_pos,
    dec_attn_gain,
    decoder_query_key_value_weight,
    w_dec_out,
    decoder_feed_gain,
    w_up,
    w_down,
    head_gain,
    w_head,
    visible_rows,
    visible_count,
    owner_slot,
):
    groups = lax.axis_size("ctx")
    repeat = groups // HEADS
    teams = [list(range(HEADS * i, HEADS * i + HEADS)) for i in range(repeat)]
    teams = None if repeat == 1 else teams
    dp_me, ctx_me = lax.axis_index("dp"), lax.axis_index("ctx")
    place = dp_me % 2 + 2 * (dp_me // 2) + 4 * (ctx_me % 2) + 8 * (ctx_me // 2)
    if repeat > 1:
        place = jnp.zeros_like(place)
    me = jnp.stack(
        [place, ctx_me, ctx_me // HEADS * HEADS, ctx_me if repeat == 1 else place]
    ).astype(jnp.int32)
    source, me = lax.optimization_barrier((patches[0], me))
    rows, pixels = source.shape
    half, quarter = rows // 2, rows // 4
    share = rows // 3
    width = w_embed.shape[1]
    dec_width = w_dec_embed.shape[1]
    shape = jax.ShapeDtypeStruct

    tall_block = half + rows + 16
    tok, *send = vmem_call(
        embed_kernel,
        [shape((rows, width), BF)]
        + (
            [shape((tall_block, 128), BF)] * HEADS
            if repeat == 1
            else [shape((HEADS, tall_block, 128), BF)]
        ),
        [
            pltpu.VMEM((rows, width), BF),
            pltpu.VMEM((rows, w_qkv.shape[1]), BF),
            pltpu.VMEM(source.shape, BF),
            pltpu.VMEM(enc_pos.shape, BF),
            pltpu.VMEM(w_embed.shape, BF),
            pltpu.VMEM(w_qkv.shape, BF),
            pltpu.VMEM((HEADS, tall_block, 128), BF),
            pltpu.SemaphoreType.DMA,
            pltpu.SemaphoreType.DMA,
            pltpu.SemaphoreType.DMA((pixels // 256,)),
            pltpu.SemaphoreType.DMA((width // 256,)),
            pltpu.SemaphoreType.DMA((HEADS,)),
        ],
        [me]
        + [pinned(x) for x in (source, enc_pos, w_embed, enc_gain, w_qkv, visible_rows)],
        smem=(0,),
        anywhere=(1, 2, 3, 5),
        anywhere_out=range(1, 1 + HEADS),
        vmem=28 << 20,
        flops=2 * rows * width * (pixels + w_qkv.shape[1]),
    )
    if repeat == 1:
        blocks = [across(send[i], 0, i) if i else send[0] for i in ORDER]
        q_at, kv_at = 0, half
    else:
        blocks = [
            swap(send[0][:, :half], "ctx", teams),
            swap(jnp.tile(send[0][:, half:], (repeat, 1, 1)), "ctx"),
        ]
        q_at, kv_at = 0, 0
    cap_k = (share + 16) * groups
    cap_q = min(HEADS * rows, cap_k)
    (att,) = vmem_call(
        functools.partial(
            enc_attend_kernel, q_at=q_at, kv_at=kv_at, rows=rows, cap_q=cap_q, cap_k=cap_k
        ),
        [shape((HEADS, half, 128), BF)],
        [
            pltpu.VMEM((cap_q + rows, 128), BF),
            pltpu.VMEM((cap_k + rows, 256), BF),
            pltpu.VMEM((cap_q + rows, 128), BF),
        ],
        [me, *blocks],
        smem=(0,),
        flops=4 * cap_q * cap_k * 128,
    )
    att = swap(att, "ctx", teams)
    send, y_own, target, flag = vmem_call(
        functools.partial(middle_kernel, groups=groups),
        [
            shape((HEADS, half + quarter, 128), BF),
            shape((rows, dec_width), BF),
            shape((rows, pixels), BF),
            shape((rows, 128), F32),
        ],
        [
            pltpu.VMEM((rows, w_out.shape[0]), BF),
            pltpu.VMEM((rows, decoder_query_key_value_weight.shape[1]), F32),
        ],
        [
            att, tok, w_out, enc_out_gain, w_dec_embed, mask_token, dec_pos,
            dec_attn_gain, decoder_query_key_value_weight, visible_rows, owner_slot, source,
        ],
        flops=2 * rows * width * 1024,
    )
    if repeat == 1:
        q = kv = swap(send, "ctx")
        q_at = half
    else:
        q = swap(send[:, half:], "ctx", teams)
        kv = swap(jnp.tile(send[:, :half], (repeat, 1, 1)), "ctx")
        q_at = 0
    (att,) = vmem_call(
        functools.partial(dec_attend_kernel, q_at=q_at, rows=rows),
        [shape((HEADS, quarter, 128), BF)],
        [pltpu.VMEM((groups * rows, 128), BF), pltpu.VMEM((groups * rows, 256), BF)],
        [q, kv],
        flops=4 * HEADS * rows * groups * rows * 128,
    )
    att = swap(att, "ctx", teams)
    hidden = w_up.shape[1]
    share_rows = rows // groups
    tall = dec_width // 32
    split = (groups, share_rows, dec_width)
    dec_att, y_mid, slope, z, dpred, loss_part, head_keep, head_send, *zn = vmem_call(
        tail_kernel,
        [
            shape((rows, w_dec_out.shape[0]), BF),
            shape((rows, dec_width), F32),
            shape((rows, hidden), BF),
            shape((rows, dec_width), F32),
            shape((rows, pixels), BF),
            shape((8, 128), F32),
        ]
        + [shape((4, 4, tall, pixels), BF)] * 2
        + ([shape((4, *split[1:]), BF)] * 2 if repeat == 1 else [shape(split, BF)]),
        [
            pltpu.VMEM((rows, dec_width), BF),
            pltpu.VMEM((rows, dec_width), BF),
            pltpu.VMEM(split, BF),
            pltpu.VMEM((dec_width, pixels), F32),
        ],
        [
            me, att, y_own, w_dec_out, decoder_feed_gain, w_up, w_down, head_gain, w_head,
            target, flag,
        ],
        smem=(0,),
        flops=2 * rows * dec_width * (2 * hidden + 2 * pixels),
    )

    def head_back():
        return vmem_call(
            head_back_kernel,
            [shape((rows, dec_width), BF)],
            [],
            [dpred, z, head_gain, w_head],
            flops=2 * rows * dec_width * pixels,
        )[0]

    def backward(dz):
        return vmem_call(
            backward_kernel,
            [shape((4, 4, tall, dec_width // 2 + 128), BF)] * 2,
            [
                pltpu.VMEM((rows, dec_width), F32),
                pltpu.VMEM((w_dec_out.shape[0], dec_width), F32),
            ],
            [me, dec_att, y_mid, slope, dz, loss_part, decoder_feed_gain, w_up, w_down],
            smem=(0,),
            flops=40 * rows * dec_width * hidden,
        )

    places = [(0,), (1,), (2, 3), (4, 5), (6, 7)] if repeat == 1 else [tuple(range(groups))]

    def rebuild(parts):
        return vmem_call(
            functools.partial(gather_kernel, places=places),
            [shape((rows, pixels), BF)],
            [pltpu.VMEM(split, F32), pltpu.VMEM((rows, dec_width), BF)],
            [me, w_head, *parts],
            smem=(0,),
            flops=2 * rows * dec_width * pixels,
        )[0]

    if repeat == 1:
        ours, theirs, reconstruction = sum_by_permutes(
            head_keep, head_send, *zn, head_back, backward, rebuild
        )
    else:
        out_keep, out_send = backward(head_back())
        ours, theirs = sum_by_blocks(
            jnp.concatenate([head_keep, out_keep], axis=3),
            jnp.concatenate([head_send, out_send], axis=3),
            groups,
        )
        reconstruction = rebuild([swap(zn[0], "ctx")])
    masked_total = lax.axis_size("dp") * (groups * rows - share * groups)
    grad_head, grad_dec_out, loss = vmem_call(
        functools.partial(place_kernel, masked_total=masked_total),
        [shape(w_head.shape, F32), shape(w_dec_out.shape, F32), shape((1, 1), F32)],
        [],
        [me, *ours, *theirs],
        smem=(0,),
        smem_out=(2,),
    )
    return (reconstruction.reshape(1, rows, pixels), grad_head, grad_dec_out, loss.reshape(()))


def solution(mesh):
    in_specs = (
        P("dp", "ctx", None),
        P("ctx", None),
        P(),
        P(),
        P(),
        P(),
        P(),
        P(),
        P(),
        P("ctx", None),
        P(),
        P(),
        P(),
        P(),
        P(),
        P(),
        P(),
        P(),
        P("dp", "ctx"),
        P("dp", "ctx"),
        P("dp", "ctx"),
    )
    out_specs = (P("dp", "ctx", None), P(), P(), P())
    return jax.shard_map(
        on_device, mesh=mesh, in_specs=in_specs, out_specs=out_specs, check_vma=False
    )
```

```python
import functools
import math

import jax
import jax.numpy as jnp
from jax import lax
from jax.experimental import pallas as pl
from jax.experimental.pallas import tpu as pltpu
from jax.sharding import PartitionSpec as P

HEADS = 8
ORDER = (6, 7, 4, 5, 2, 3, 1, 0)
BF = jnp.bfloat16
F32 = jnp.float32
LOG2E = math.log2(math.e)
VMEM_LIMIT = 24 << 20


def as_row(vector):
    return vector.astype(F32).reshape(1, -1)


def layer_norm(x, gain):
    row_mean = jnp.mean(x, axis=-1, keepdims=True)
    centered_input = x - row_mean
    var = jnp.mean(centered_input * centered_input, axis=-1, keepdims=True)
    return centered_input * lax.rsqrt(var + 1e-06) * as_row(gain)


def norm_backward(z, gain, upstream):
    row_mean = jnp.mean(z, axis=-1, keepdims=True)
    centered_input = z - row_mean
    inverse_scale = lax.rsqrt(
        jnp.mean(centered_input * centered_input, axis=-1, keepdims=True) + 1e-06
    )
    normalized_input = centered_input * inverse_scale
    input_gradient = upstream * as_row(gain)
    return inverse_scale * (
        input_gradient
        - jnp.mean(input_gradient, axis=-1, keepdims=True)
        - normalized_input * jnp.mean(input_gradient * normalized_input, axis=-1, keepdims=True)
    )


def dot(a, b):
    return jnp.dot(a, b, preferred_element_type=F32)


def dot_t(a, b):
    return lax.dot_general(a, b, (((1,), (1,)), ((), ())), preferred_element_type=F32)


def swap_halves(x):
    half = x.shape[1] // 2
    return jnp.concatenate([x[:, half:], x[:, :half]], axis=1)


def slot_of_row(slots_row):
    size = slots_row.shape[1]
    row = lax.broadcasted_iota(jnp.int32, (size, size), 0)
    return jnp.where(row == slots_row, 1.0, 0.0)


def embed_kernel(
    me_ref, patch_hbm, pos_hbm, w_embed_hbm, gain_ref, w_qkv_hbm, slots_ref, *refs,
):
    tok_ref, *send_refs = refs[:-12]
    normed_ref, qkv_ref, patch_ref, pos_ref, w_embed_ref, w_qkv_ref, send_buf = refs[-12:-5]
    patch_sem, pos_sem, embed_sem, qkv_sem, send_sem = refs[-5:]
    rows, width = patch_ref.shape
    half = rows // 2
    att = w_qkv_ref.shape[1] // 3
    size = att // HEADS
    tile = 256

    def pieces(hbm, buf, sem):
        return [
            pltpu.make_async_copy(
                hbm.at[at : at + tile], buf.at[at : at + tile], sem.at[at // tile]
            )
            for at in range(0, buf.shape[0], tile)
        ]

    embed_copies = pieces(w_embed_hbm, w_embed_ref, embed_sem)
    qkv_copies = pieces(w_qkv_hbm, w_qkv_ref, qkv_sem)
    patch_copy = pltpu.make_async_copy(patch_hbm, patch_ref, patch_sem)
    pos_copy = pltpu.make_async_copy(pos_hbm, pos_ref, pos_sem)
    for copy in [patch_copy, *embed_copies, pos_copy, *qkv_copies]:
        copy.start()
    patch_copy.wait()
    total = None
    for step, copy in enumerate(embed_copies):
        copy.wait()
        cols = slice(step * tile, (step + 1) * tile)
        part = dot(patch_ref[:, cols], w_embed_ref[cols, :])
        total = part if total is None else total + part
    pos_copy.wait()
    tok_ref[...] = (total + pos_ref[...].astype(F32)).astype(BF)
    pick = slot_of_row(slots_ref[...]).astype(BF)
    normed = layer_norm(tok_ref[...].astype(F32), gain_ref[...]).astype(BF)
    normed_ref[...] = lax.dot_general(
        pick, normed, (((0,), (0,)), ((), ())), preferred_element_type=F32
    ).astype(BF)
    for copy in qkv_copies:
        copy.wait()
    for step in range(3 * att // tile):
        cols = slice(step * tile, (step + 1) * tile)
        qkv_ref[:, cols] = dot(normed_ref[...], w_qkv_ref[:, cols]).astype(BF)

    count = jnp.sum(jnp.where(slots_ref[...] >= 0, 1.0, 0.0), axis=1, keepdims=True)
    high = jnp.floor(count * (1.0 / 16))
    lane = lax.broadcasted_iota(jnp.int32, (16, 128), 1)
    info = jnp.where(lane < 64, high, count - 16.0 * high).astype(BF)
    for head in range(HEADS):
        at = head * size
        q = qkv_ref[:, at : at + size]
        k = qkv_ref[:, att + at : att + at + size]
        v = qkv_ref[:, 2 * att + at : 2 * att + at + size]
        send_buf[head, :half, :] = jnp.concatenate([q[:half], q[half:]], axis=1)
        send_buf[head, half : half + rows, :] = jnp.concatenate([k, v], axis=1)
        send_buf[head, half + rows :, :] = info
    if len(send_refs) == 1:
        copies = [pltpu.make_async_copy(send_buf, send_refs[0], send_sem.at[0])]
    else:
        copies = [
            pltpu.make_async_copy(send_buf.at[me_ref[1] ^ index], ref, send_sem.at[index])
            for index, ref in enumerate(send_refs)
        ]
    for copy in copies:
        copy.start()
    for copy in copies:
        copy.wait()


def enc_attend_kernel(me_ref, *refs, q_at, kv_at, rows, cap_q, cap_k):
    *blocks, out_ref, q_buf, kv_buf, o_buf = refs
    if len(blocks) == HEADS:
        q_of = kv_of = lambda source: blocks[source]
        place_of = lambda source: me_ref[1] ^ ORDER[source]
        sources, first = HEADS, 0
    else:
        q_of, kv_of = blocks[0].at.__getitem__, blocks[1].at.__getitem__
        place_of = lambda source: source
        sources, first = blocks[1].shape[0], me_ref[2]
    half = rows // 2
    lane16 = lax.broadcasted_iota(jnp.int32, (16, 128), 1)
    lane_h = lax.broadcasted_iota(jnp.int32, (half, 128), 1)

    def count_of(source):
        info = kv_of(source)[kv_at + rows : kv_at + rows + 16, :].astype(F32)
        high = jnp.max(jnp.where(lane16 < 64, info, 0.0)).astype(jnp.int32)
        low = jnp.max(jnp.where(lane16 >= 64, info, 0.0)).astype(jnp.int32)
        return high * 16 + low

    q_buf[...] = jnp.zeros_like(q_buf)
    o_buf[...] = jnp.zeros_like(o_buf)
    kv_buf[:, :128] = jnp.zeros((kv_buf.shape[0], 128), BF)
    kv_buf[:, 128:] = jnp.ones((kv_buf.shape[0], 128), BF)

    key = lax.broadcasted_iota(jnp.int32, (1, cap_k), 1)
    valid = jnp.zeros((1, cap_k), F32)
    off = jnp.int32(0)
    for source in range(sources):
        count = count_of(source)
        off = pl.multiple_of(off, 16)
        kv_buf[pl.ds(off, rows), :128] = kv_of(source)[kv_at : kv_at + rows, :]
        valid = jnp.where((key >= off) & (key < off + count), 1.0, valid)
        off = off + (count + 15) // 16 * 16
    bias = jnp.where(valid > 0.0, 0.0, -1e30)

    offs = []
    off = jnp.int32(0)
    for source in range(HEADS):
        off = pl.multiple_of(off, 16)
        offs.append(off)
        block = q_of(source)[q_at : q_at + half, :]
        zero = jnp.zeros_like(block)
        q_buf[pl.ds(off, half), :] = jnp.where(lane_h < 64, block, zero)
        q_buf[pl.ds(off + half, half), :] = jnp.where(lane_h < 64, swap_halves(block), zero)
        off = off + (count_of(first + source) + 15) // 16 * 16
    total = off

    scale = LOG2E * 64**-0.5

    def attend(at):
        score = dot_t(q_buf[at, :], kv_buf[:cap_k, :128]) + bias
        top = jnp.max(score, axis=1, keepdims=True)
        weight = jnp.exp2((score - top) * scale).astype(BF)
        mixed = dot(weight, kv_buf[:cap_k, :])
        o_buf[at, :] = (mixed[:, :128] / mixed[:, 128:]).astype(BF)

    if cap_q == cap_k:
        for at in range(0, cap_q, cap_q // 4):
            attend(slice(at, at + cap_q // 4))
    else:
        tile = 128

        @pl.loop(0, cap_q // tile)
        def _(step):
            @pl.when(step * tile < total)
            def _():
                attend(pl.ds(pl.multiple_of(step * tile, tile), tile))

    for source in range(HEADS):
        upper = o_buf[pl.ds(offs[source], half), :]
        lower = o_buf[pl.ds(pl.multiple_of(offs[source] + half, 16), half), :]
        out_ref[place_of(source)] = jnp.where(lane_h < 64, swap_halves(upper), lower)


def middle_kernel(
    att_ref, tok_ref, w_out_ref, out_gain_ref, w_dec_ref, mask_ref, pos_ref, gain_ref,
    w_qkv_ref, slots_ref, owner_ref, patch_ref,
    send_ref, y_ref, target_ref, flag_ref, att_buf, qkv_buf, *, groups,
):
    rows, width = tok_ref.shape
    half = rows // 2
    block = rows // groups
    for pair in range(HEADS // 2):
        a, b = att_ref[2 * pair], att_ref[2 * pair + 1]
        cols = slice(128 * pair, 128 * pair + 128)
        att_buf[:half, cols] = jnp.concatenate([a[:, :64], b[:, :64]], axis=1)
        att_buf[half:, cols] = jnp.concatenate([a[:, 64:], b[:, 64:]], axis=1)
    pick = slot_of_row(slots_ref[...])
    seen = jnp.sum(pick, axis=1, keepdims=True)
    attended = dot(pick.astype(BF), att_buf[...]).astype(BF)
    encoded = tok_ref[...].astype(F32) + dot(attended, w_out_ref[...])
    dec_normed = layer_norm(encoded, out_gain_ref[...]).astype(BF)
    dec_tok = dot(dec_normed, w_dec_ref[...]).astype(BF).astype(F32)
    filled = jnp.where(seen > 0.0, dec_tok, as_row(mask_ref[...]))
    decoder_in = (filled + pos_ref[...].astype(F32)).astype(BF)

    owner = owner_ref[...]
    dest = jnp.zeros_like(owner)
    for device in range(1, groups):
        dest = dest + jnp.where(owner >= device * rows, 1, 0)
    local = owner - dest * rows
    first = jnp.min(local.astype(F32), axis=1, keepdims=True).astype(jnp.int32)
    place = dest * block + local - first
    move = slot_of_row(place).astype(BF)
    y = dot(move, decoder_in)
    y_ref[...] = y.astype(BF)
    target_ref[...] = dot(move, patch_ref[...]).astype(BF)
    hidden = jnp.broadcast_to(1.0 - seen, (rows, 128)).astype(BF)
    flag_ref[...] = dot(move, hidden)
    attn_in = layer_norm(y, gain_ref[...]).astype(BF)
    qkv_buf[...] = dot(attn_in, w_qkv_ref[...]).astype(BF).astype(F32)
    att = w_qkv_ref.shape[1] // 3
    size = att // HEADS
    quarter = rows // 4
    for head in range(HEADS):
        at = head * size
        q = qkv_buf[:, at : at + size]
        k = qkv_buf[:, att + at : att + at + size]
        v = qkv_buf[:, 2 * att + at : 2 * att + at + size]
        send_ref[head, :half, :] = jnp.concatenate(
            [k[:half], v[:half], k[half:], v[half:]], axis=1
        ).astype(BF)
        send_ref[head, half:, :] = jnp.concatenate(
            [q[i * quarter : (i + 1) * quarter] for i in range(4)], axis=1
        ).astype(BF)


def dec_attend_kernel(q_ref, kv_ref, out_ref, k_buf, v_buf, *, q_at, rows):
    half = rows // 2
    quarter = rows // 4
    sources = kv_ref.shape[0]
    for source in range(sources):
        for part in range(2):
            block = kv_ref[source, :half, 64 * part : 64 * part + 64]
            at = source * rows + part * half
            k, v = block[:, :32], block[:, 32:]
            k_buf[at : at + half, :] = jnp.concatenate([k, k, k, k], axis=1)
            v_buf[at : at + half, :128] = jnp.concatenate([v, v, v, v], axis=1)
    v_buf[:, 128:] = jnp.ones((v_buf.shape[0], 128), BF)
    scale = LOG2E * 32**-0.5
    lane = lax.broadcasted_iota(jnp.int32, (quarter, 128), 1)
    zone = [(lane >= 32 * i) & (lane < 32 * i + 32) for i in range(4)]

    chunk = 256
    unroll = 4 if sources == HEADS else 1

    def attend(source):
        block = q_ref[source, q_at : q_at + quarter, :].astype(F32)
        q = jnp.concatenate([jnp.where(z, block, 0.0) for z in zone], axis=0).astype(BF)
        top = mixed = None
        for at in range(0, k_buf.shape[0], chunk):
            score = dot_t(q, k_buf[at : at + chunk, :])
            peak = jnp.max(score, axis=1, keepdims=True)
            new = peak if top is None else jnp.maximum(top, peak)
            weight = jnp.exp2((score - new) * scale).astype(BF)
            part = dot(weight, v_buf[at : at + chunk, :])
            mixed = part if top is None else mixed * jnp.exp2((top - new) * scale) + part
            top = new
        mixed = mixed[:, :128] / mixed[:, 128:]
        out = mixed[:quarter]
        for i in range(1, 4):
            out = jnp.where(zone[i], mixed[i * quarter : (i + 1) * quarter], out)
        out_ref[source] = out.astype(BF)

    @pl.loop(0, HEADS // unroll)
    def _(step):
        for i in range(unroll):
            attend(step * unroll + i)


def tail_kernel(
    me_ref, att_ref, y_ref, w_out_ref, feed_gain_ref, w_up_ref, w_down_ref, head_gain_ref,
    w_head_ref, target_ref, flag_ref,
    dec_att_ref, mid_ref, slope_ref, z_ref, dpred_ref, loss_ref, keep_ref, send_ref, *refs,
):
    *zn_refs, feed_buf, zn_buf, split_buf, head_buf = refs
    rows, width = y_ref.shape
    pixels = w_head_ref.shape[1]
    hidden = w_up_ref.shape[1]
    blocks = [att_ref[head].astype(F32) for head in range(HEADS)]
    dec_att_ref[...] = jnp.concatenate(
        [
            jnp.concatenate([b[:, 32 * i : 32 * i + 32] for b in blocks], axis=1)
            for i in range(4)
        ],
        axis=0,
    ).astype(BF)
    mid_ref[...] = y_ref[...].astype(F32) + dot(dec_att_ref[...], w_out_ref[...])
    feed_buf[...] = layer_norm(mid_ref[...], feed_gain_ref[...]).astype(BF)
    z_ref[...] = mid_ref[...]
    tile = 512
    c = math.sqrt(2.0 / math.pi)
    for at in range(0, hidden, tile):
        cols = slice(at, at + tile)
        pre = dot(feed_buf[...], w_up_ref[:, cols])
        square = pre * pre
        t = jnp.tanh(pre * (c + (c * 0.044715) * square))
        gate = 0.5 + 0.5 * t
        slope = gate + (0.5 * pre) * (1.0 - t * t) * (c + (3 * c * 0.044715) * square)
        slope_ref[:, cols] = slope.astype(BF)
        z_ref[...] += dot((pre * gate).astype(BF), w_down_ref[cols, :])

    zn = layer_norm(z_ref[...], head_gain_ref[...])
    zn_buf[...] = zn.astype(BF)
    share = split_buf.shape[1]
    for dest in range(split_buf.shape[0]):
        split_buf[dest] = zn[dest * share : (dest + 1) * share, :].astype(BF)
    if len(zn_refs) == 1:
        zn_refs[0][...] = split_buf[...]
    else:
        for index in range(2 * zn_refs[0].shape[0]):
            zn_refs[index % 2][index // 2] = split_buf[me_ref[1] ^ index]
    flag = flag_ref[:, :1]
    loss = jnp.zeros((1, 1), F32)
    for at in range(0, pixels, tile):
        cols = slice(at, at + tile)
        pred = dot(zn_buf[...], w_head_ref[:, cols])
        err = (pred - target_ref[:, cols].astype(F32)) * flag
        dpred_ref[:, cols] = (err * (2.0 / pixels)).astype(BF)
        loss += jnp.sum(jnp.sum(err * err, axis=1, keepdims=True), axis=0, keepdims=True)
        head_buf[:, cols] = lax.dot_general(
            zn_buf[...], dpred_ref[:, cols], (((0,), (0,)), ((), ())), preferred_element_type=F32
        )
    loss_ref[...] = jnp.broadcast_to(loss * (1.0 / pixels), loss_ref.shape)
    tall = width // 32
    for index in range(32):
        at = pl.multiple_of((index ^ me_ref[0]) * tall, tall)
        ref = send_ref if index % 2 else keep_ref
        ref[index // 2 % 4, index // 8] = head_buf[pl.ds(at, tall), :].astype(BF)


def gather_kernel(me_ref, w_head_ref, *refs, places):
    *parts, out_ref, split_buf, zn_buf = refs
    share = split_buf.shape[1]
    for ref, indices in zip(parts, places):
        for i, index in enumerate(indices):
            split_buf[me_ref[3] ^ index] = ref[i].astype(F32)
    zn_buf[...] = jnp.concatenate(
        [split_buf[device] for device in range(split_buf.shape[0])], axis=0
    ).astype(BF)
    tile = 512
    for at in range(0, w_head_ref.shape[1], tile):
        cols = slice(at, at + tile)
        out_ref[:, cols] = dot(zn_buf[...], w_head_ref[:, cols]).astype(BF)


def backward_kernel(
    me_ref, dec_att_ref, mid_ref, slope_ref, dpred_ref, z_ref, loss_ref, head_gain_ref, w_head_ref,
    feed_gain_ref, w_up_ref, w_down_ref,
    keep_ref, send_ref, back_buf, out_buf,
):
    hidden = w_up_ref.shape[1]
    dz = norm_backward(
        z_ref[...], head_gain_ref[...], dot_t(dpred_ref[...], w_head_ref[...])
    ).astype(BF)
    tile = 512
    for at in range(0, hidden, tile):
        cols = slice(at, at + tile)
        back = dot_t(dz, w_down_ref[cols, :]) * slope_ref[:, cols].astype(F32)
        part = dot_t(back.astype(BF), w_up_ref[:, cols])
        back_buf[...] = part if at == 0 else back_buf[...] + part

    mid_grad = (
        dz.astype(F32) + norm_backward(mid_ref[...], feed_gain_ref[...], back_buf[...])
    ).astype(BF)
    out_buf[...] = lax.dot_general(
        dec_att_ref[...], mid_grad, (((0,), (0,)), ((), ())), preferred_element_type=F32
    )
    loss = loss_ref[...]
    high = loss.astype(BF)
    low = (loss - high.astype(F32)).astype(BF)
    sums = jnp.concatenate([high.astype(F32), low.astype(F32)], axis=0).astype(BF)
    deep = out_buf.shape[0] // 32
    half = out_buf.shape[1] // 2
    for index in range(32):
        at = pl.multiple_of((index ^ me_ref[0]) * deep, deep)
        ref = send_ref if index % 2 else keep_ref
        xy, z = index // 2 % 4, index // 8
        part = out_buf[pl.ds(at, deep), :]
        ref[xy, z, :, :half] = jnp.concatenate([part[:, :half], part[:, half:]], axis=0).astype(BF)
        ref[xy, z, :, half:] = sums


def merge_kernel(
    head_keep_ref, head_got_ref, out_keep_ref, out_got_ref, mine_ref, other_ref, *refs
):
    head = (head_keep_ref[...].astype(F32) + head_got_ref[...].astype(F32)).astype(BF)
    out = (out_keep_ref[...].astype(F32) + out_got_ref[...].astype(F32)).astype(BF)
    pixels = head.shape[3]
    for i in range(4):
        refs[i][:, :, :pixels] = head[i]
        refs[i][:, :, pixels:] = out[i]
    for i in range(1, 4):
        refs[3 + i][0] = mine_ref[i]
        refs[3 + i][1] = other_ref[i]


def add_kernel(*refs, count):
    total = refs[0][...].astype(F32)
    for ref in refs[1:count]:
        total = total + ref[...].astype(F32)
    total = total.astype(BF)
    outs = refs[count:]
    if len(outs) == 1:
        outs[0][...] = total
    else:
        for i, ref in enumerate(outs):
            ref[...] = total[i]


def join_kernel(*refs):
    for i, ref in enumerate(refs[:-1]):
        refs[-1][i] = ref[...]


def place_kernel(me_ref, *refs, masked_total):
    blocks, (head_ref, out_ref, loss_ref) = refs[:8], refs[8:]
    pixels = head_ref.shape[1]
    deep = out_ref.shape[0] // 32
    half = out_ref.shape[1] // 2
    tall = head_ref.shape[0] // 32
    for index in range(32):
        block = index ^ me_ref[0]
        value = blocks[index % 2 * 4 + index // 2 % 4][index // 8].astype(F32)
        head_ref[pl.ds(pl.multiple_of(block * tall, tall), tall), :] = value[:, :pixels]
        at = pl.ds(pl.multiple_of(block * deep, deep), deep)
        out_ref[at, :half] = value[:deep, pixels : pixels + half]
        out_ref[at, half:] = value[deep:, pixels : pixels + half]
    value = blocks[0][0].astype(F32)
    total = value[:8, pixels + half :] + value[8:, pixels + half :]
    loss_ref[0, 0] = jnp.max(total) * (1.0 / masked_total)


def vmem_call(kernel, outs, scratch, inputs, smem=(), smem_out=(), anywhere=(),
              anywhere_out=(), vmem=VMEM_LIMIT, flops=0):
    space = [
        pl.BlockSpec(
            memory_space=pltpu.SMEM if i in smem else pltpu.HBM if i in anywhere else pltpu.VMEM
        )
        for i in range(len(inputs))
    ]
    moved = sum(a.size * a.dtype.itemsize for a in inputs)
    return pl.pallas_call(
        kernel,
        out_shape=outs,
        in_specs=space,
        out_specs=[
            pl.BlockSpec(
                memory_space=pltpu.SMEM
                if i in smem_out
                else pl.ANY
                if i in anywhere_out
                else pltpu.VMEM
            )
            for i in range(len(outs))
        ],
        scratch_shapes=scratch,
        compiler_params=pltpu.CompilerParams(vmem_limit_bytes=vmem),
        cost_estimate=pl.CostEstimate(flops=flops, bytes_accessed=moved, transcendentals=0),
    )(*inputs)


def pinned(x):
    return pltpu.with_memory_space_constraint(x, pltpu.HBM)


def swap(x, axis, groups=None):
    return lax.all_to_all(
        x, axis, split_axis=0, concat_axis=0, tiled=True, axis_index_groups=groups
    )


def all_sum(x, groups):
    size = lax.axis_size("dp")
    me = lax.axis_index("dp")
    stages = []
    step = 1
    while step < size:
        pairs = [(i, i ^ step) for i in range(size)]
        upper = (me // step) % 2
        half = x.shape[0] // 2
        mine = lax.dynamic_slice_in_dim(x, upper * half, half, 0)
        other = lax.dynamic_slice_in_dim(x, (1 - upper) * half, half, 0)
        x = mine + lax.ppermute(other, "dp", pairs)
        stages.append((pairs, upper))
        step *= 2
    rows, width = x.shape
    blocks = swap(x.reshape(groups, rows // groups, width), "ctx")
    total = jnp.sum(blocks.astype(F32), axis=0).astype(BF)
    x = swap(jnp.broadcast_to(total[None], blocks.shape), "ctx").reshape(rows, width)
    for pairs, upper in reversed(stages):
        other = lax.ppermute(x, "dp", pairs)
        low = jnp.where(upper == 0, x, other)
        high = jnp.where(upper == 0, other, x)
        x = jnp.concatenate([low, high], axis=0)
    return x


def across(x, dp_bit, ctx_bits):
    count, groups = lax.axis_size("dp"), lax.axis_size("ctx")
    pairs = [
        (i * groups + j, (i ^ dp_bit) * groups + (j ^ ctx_bits))
        for i in range(count)
        for j in range(groups)
    ]
    return lax.ppermute(x, ("dp", "ctx"), pairs)


PLANE = ((2, 0), (0, 1), (2, 1))
COLUMN = ((0, 2), (0, 4), (0, 6))


def sum_by_permutes(head_keep, head_send, zn_keep, zn_send, backward, rebuild):
    shape = jax.ShapeDtypeStruct
    head_got = across(head_send, 1, 0)
    zn_got = across(zn_send, 0, 1)
    out_keep, out_send = backward()
    out_send, head_got, zn_got = lax.optimization_barrier((out_send, head_got, zn_got))
    out_got = across(out_send, 1, 0)
    block = shape((head_keep.shape[2], head_keep.shape[3] + out_keep.shape[3]), BF)
    part = shape((4, *block.shape), BF)
    pair = shape((2, *zn_keep.shape[1:]), BF)
    *parts, zn1, zn2, zn3 = vmem_call(
        merge_kernel,
        [part] * 4 + [pair] * 3,
        [],
        [head_keep, head_got, out_keep, out_got, zn_keep, zn_got],
    )
    rest = [across(p, *bits) for p, bits in zip((zn1, zn2, zn3), COLUMN)]
    others = [across(p, *bits) for p, bits in zip(parts[1:], PLANE)]
    mine, *far = lax.optimization_barrier((parts[0], *rest[1:]))
    rest = [rest[0], *far]
    blocks = vmem_call(
        functools.partial(add_kernel, count=4), [block] * 4, [], [*reversed(others), mine]
    )
    others = [across(b, *bits) for b, bits in zip(blocks[1:], COLUMN)]
    (total,) = vmem_call(
        functools.partial(add_kernel, count=4), [block], [], [*reversed(others), blocks[0]]
    )
    (column,) = vmem_call(
        join_kernel,
        [part],
        [],
        [total] + [across(total, *bits) for bits in COLUMN],
    )
    column, reconstruction = lax.optimization_barrier(
        (column, rebuild([zn_keep, zn_got, *rest]))
    )
    ours = [column] + [across(column, *bits) for bits in PLANE]
    return ours, [across(x, 1, 0) for x in ours], reconstruction


def sum_by_blocks(keep, send, groups):
    size = keep.shape[0] * keep.shape[1] * keep.shape[2]
    flat = jnp.concatenate([keep.reshape(size, -1), send.reshape(size, -1)], axis=0)
    unit = lax.axis_size("dp") * groups
    used = flat.shape[0]
    padded = -(-used // unit) * unit
    total = all_sum(jnp.pad(flat, ((0, padded - used), (0, 0))), groups)[:used]
    total = total.reshape(2, *keep.shape)
    return [total[0, i] for i in range(4)], [total[1, i] for i in range(4)]


def on_device(
    patches,
    enc_pos,
    w_embed,
    enc_gain,
    w_qkv,
    w_out,
    enc_out_gain,
    w_dec_embed,
    mask_token,
    dec_pos,
    dec_attn_gain,
    decoder_query_key_value_weight,
    w_dec_out,
    decoder_feed_gain,
    w_up,
    w_down,
    head_gain,
    w_head,
    visible_rows,
    visible_count,
    owner_slot,
):
    groups = lax.axis_size("ctx")
    repeat = groups // HEADS
    teams = [list(range(HEADS * i, HEADS * i + HEADS)) for i in range(repeat)]
    teams = None if repeat == 1 else teams
    dp_me, ctx_me = lax.axis_index("dp"), lax.axis_index("ctx")
    place = dp_me % 2 + 2 * (dp_me // 2) + 4 * (ctx_me % 2) + 8 * (ctx_me // 2)
    if repeat > 1:
        place = jnp.zeros_like(place)
    me = jnp.stack(
        [place, ctx_me, ctx_me // HEADS * HEADS, ctx_me if repeat == 1 else place]
    ).astype(jnp.int32)
    source, me = lax.optimization_barrier((patches[0], me))
    rows, pixels = source.shape
    half, quarter = rows // 2, rows // 4
    share = rows // 3
    width = w_embed.shape[1]
    dec_width = w_dec_embed.shape[1]
    shape = jax.ShapeDtypeStruct

    tall_block = half + rows + 16
    tok, *send = vmem_call(
        embed_kernel,
        [shape((rows, width), BF)]
        + (
            [shape((tall_block, 128), BF)] * HEADS
            if repeat == 1
            else [shape((HEADS, tall_block, 128), BF)]
        ),
        [
            pltpu.VMEM((rows, width), BF),
            pltpu.VMEM((rows, w_qkv.shape[1]), BF),
            pltpu.VMEM(source.shape, BF),
            pltpu.VMEM(enc_pos.shape, BF),
            pltpu.VMEM(w_embed.shape, BF),
            pltpu.VMEM(w_qkv.shape, BF),
            pltpu.VMEM((HEADS, tall_block, 128), BF),
            pltpu.SemaphoreType.DMA,
            pltpu.SemaphoreType.DMA,
            pltpu.SemaphoreType.DMA((pixels // 256,)),
            pltpu.SemaphoreType.DMA((width // 256,)),
            pltpu.SemaphoreType.DMA((HEADS,)),
        ],
        [me]
        + [pinned(x) for x in (source, enc_pos, w_embed, enc_gain, w_qkv, visible_rows)],
        smem=(0,),
        anywhere=(1, 2, 3, 5),
        anywhere_out=range(1, 1 + HEADS),
        vmem=28 << 20,
        flops=2 * rows * width * (pixels + w_qkv.shape[1]),
    )
    if repeat == 1:
        blocks = [across(send[i], 0, i) if i else send[0] for i in ORDER]
        q_at, kv_at = 0, half
    else:
        blocks = [
            swap(send[0][:, :half], "ctx", teams),
            swap(jnp.tile(send[0][:, half:], (repeat, 1, 1)), "ctx"),
        ]
        q_at, kv_at = 0, 0
    cap_k = (share + 16) * groups
    cap_q = min(HEADS * rows, cap_k)
    (att,) = vmem_call(
        functools.partial(
            enc_attend_kernel, q_at=q_at, kv_at=kv_at, rows=rows, cap_q=cap_q, cap_k=cap_k
        ),
        [shape((HEADS, half, 128), BF)],
        [
            pltpu.VMEM((cap_q + rows, 128), BF),
            pltpu.VMEM((cap_k + rows, 256), BF),
            pltpu.VMEM((cap_q + rows, 128), BF),
        ],
        [me, *blocks],
        smem=(0,),
        flops=4 * cap_q * cap_k * 128,
    )
    att = swap(att, "ctx", teams)
    send, y_own, target, flag = vmem_call(
        functools.partial(middle_kernel, groups=groups),
        [
            shape((HEADS, half + quarter, 128), BF),
            shape((rows, dec_width), BF),
            shape((rows, pixels), BF),
            shape((rows, 128), F32),
        ],
        [
            pltpu.VMEM((rows, w_out.shape[0]), BF),
            pltpu.VMEM((rows, decoder_query_key_value_weight.shape[1]), F32),
        ],
        [
            att, tok, w_out, enc_out_gain, w_dec_embed, mask_token, dec_pos,
            dec_attn_gain, decoder_query_key_value_weight, visible_rows, owner_slot, source,
        ],
        flops=2 * rows * width * 1024,
    )
    if repeat == 1:
        q = kv = swap(send, "ctx")
        q_at = half
    else:
        q = swap(send[:, half:], "ctx", teams)
        kv = swap(jnp.tile(send[:, :half], (repeat, 1, 1)), "ctx")
        q_at = 0
    (att,) = vmem_call(
        functools.partial(dec_attend_kernel, q_at=q_at, rows=rows),
        [shape((HEADS, quarter, 128), BF)],
        [pltpu.VMEM((groups * rows, 128), BF), pltpu.VMEM((groups * rows, 256), BF)],
        [q, kv],
        flops=4 * HEADS * rows * groups * rows * 128,
    )
    att = swap(att, "ctx", teams)
    hidden = w_up.shape[1]
    share_rows = rows // groups
    tall = dec_width // 32
    split = (groups, share_rows, dec_width)
    dec_att, y_mid, slope, z, dpred, loss_part, head_keep, head_send, *zn = vmem_call(
        tail_kernel,
        [
            shape((rows, w_dec_out.shape[0]), BF),
            shape((rows, dec_width), F32),
            shape((rows, hidden), BF),
            shape((rows, dec_width), F32),
            shape((rows, pixels), BF),
            shape((8, 128), F32),
        ]
        + [shape((4, 4, tall, pixels), BF)] * 2
        + ([shape((4, *split[1:]), BF)] * 2 if repeat == 1 else [shape(split, BF)]),
        [
            pltpu.VMEM((rows, dec_width), BF),
            pltpu.VMEM((rows, dec_width), BF),
            pltpu.VMEM(split, BF),
            pltpu.VMEM((dec_width, pixels), F32),
        ],
        [
            me, att, y_own, w_dec_out, decoder_feed_gain, w_up, w_down, head_gain, w_head,
            target, flag,
        ],
        smem=(0,),
        flops=2 * rows * dec_width * (2 * hidden + 2 * pixels),
    )

    def backward():
        return vmem_call(
            backward_kernel,
            [shape((4, 4, tall, dec_width // 2 + 128), BF)] * 2,
            [
                pltpu.VMEM((rows, dec_width), F32),
                pltpu.VMEM((w_dec_out.shape[0], dec_width), F32),
            ],
            [
                me, dec_att, y_mid, slope, dpred, z, loss_part, head_gain, w_head,
                decoder_feed_gain, w_up, w_down,
            ],
            smem=(0,),
            flops=40 * rows * dec_width * hidden,
        )

    places = [(0,), (1,), (2, 3), (4, 5), (6, 7)] if repeat == 1 else [tuple(range(groups))]

    def rebuild(parts):
        return vmem_call(
            functools.partial(gather_kernel, places=places),
            [shape((rows, pixels), BF)],
            [pltpu.VMEM(split, F32), pltpu.VMEM((rows, dec_width), BF)],
            [me, w_head, *parts],
            smem=(0,),
            flops=2 * rows * dec_width * pixels,
        )[0]

    if repeat == 1:
        ours, theirs, reconstruction = sum_by_permutes(
            head_keep, head_send, *zn, backward, rebuild
        )
    else:
        out_keep, out_send = backward()
        ours, theirs = sum_by_blocks(
            jnp.concatenate([head_keep, out_keep], axis=3),
            jnp.concatenate([head_send, out_send], axis=3),
            groups,
        )
        reconstruction = rebuild([swap(zn[0], "ctx")])
    masked_total = lax.axis_size("dp") * (groups * rows - share * groups)
    grad_head, grad_dec_out, loss = vmem_call(
        functools.partial(place_kernel, masked_total=masked_total),
        [shape(w_head.shape, F32), shape(w_dec_out.shape, F32), shape((1, 1), F32)],
        [],
        [me, *ours, *theirs],
        smem=(0,),
        smem_out=(2,),
    )
    return (reconstruction.reshape(1, rows, pixels), grad_head, grad_dec_out, loss.reshape(()))


def solution(mesh):
    in_specs = (
        P("dp", "ctx", None),
        P("ctx", None),
        P(),
        P(),
        P(),
        P(),
        P(),
        P(),
        P(),
        P("ctx", None),
        P(),
        P(),
        P(),
        P(),
        P(),
        P(),
        P(),
        P(),
        P("dp", "ctx"),
        P("dp", "ctx"),
        P("dp", "ctx"),
    )
    out_specs = (P("dp", "ctx", None), P(), P(), P())
    return jax.shard_map(
        on_device, mesh=mesh, in_specs=in_specs, out_specs=out_specs, check_vma=False
    )
```

```python
import functools
import math

import jax
import jax.numpy as jnp
from jax import lax
from jax.experimental import pallas as pl
from jax.experimental.pallas import tpu as pltpu
from jax.sharding import PartitionSpec as P

HEADS = 8
ORDER = (6, 7, 4, 5, 2, 3, 1, 0)
BF = jnp.bfloat16
F32 = jnp.float32
LOG2E = math.log2(math.e)
VMEM_LIMIT = 24 << 20


def as_row(vector):
    return vector.astype(F32).reshape(1, -1)


def layer_norm(x, gain):
    row_mean = jnp.mean(x, axis=-1, keepdims=True)
    centered_input = x - row_mean
    var = jnp.mean(centered_input * centered_input, axis=-1, keepdims=True)
    return centered_input * lax.rsqrt(var + 1e-06) * as_row(gain)


def norm_backward(z, gain, upstream):
    row_mean = jnp.mean(z, axis=-1, keepdims=True)
    centered_input = z - row_mean
    inverse_scale = lax.rsqrt(
        jnp.mean(centered_input * centered_input, axis=-1, keepdims=True) + 1e-06
    )
    normalized_input = centered_input * inverse_scale
    input_gradient = upstream * as_row(gain)
    return inverse_scale * (
        input_gradient
        - jnp.mean(input_gradient, axis=-1, keepdims=True)
        - normalized_input * jnp.mean(input_gradient * normalized_input, axis=-1, keepdims=True)
    )


def dot(a, b):
    return jnp.dot(a, b, preferred_element_type=F32)


def dot_t(a, b):
    return lax.dot_general(a, b, (((1,), (1,)), ((), ())), preferred_element_type=F32)


def swap_halves(x):
    half = x.shape[1] // 2
    return jnp.concatenate([x[:, half:], x[:, :half]], axis=1)


def slot_of_row(slots_row):
    size = slots_row.shape[1]
    row = lax.broadcasted_iota(jnp.int32, (size, size), 0)
    return jnp.where(row == slots_row, 1.0, 0.0)


def embed_kernel(
    me_ref, patch_hbm, pos_hbm, w_embed_hbm, gain_ref, w_qkv_hbm, slots_ref, *refs,
):
    tok_ref, *send_refs = refs[:-12]
    normed_ref, qkv_ref, patch_ref, pos_ref, w_embed_ref, w_qkv_ref, send_buf = refs[-12:-5]
    patch_sem, pos_sem, embed_sem, qkv_sem, send_sem = refs[-5:]
    rows, width = patch_ref.shape
    half = rows // 2
    att = w_qkv_ref.shape[1] // 3
    size = att // HEADS
    tile = 256

    def pieces(hbm, buf, sem):
        return [
            pltpu.make_async_copy(
                hbm.at[at : at + tile], buf.at[at : at + tile], sem.at[at // tile]
            )
            for at in range(0, buf.shape[0], tile)
        ]

    embed_copies = pieces(w_embed_hbm, w_embed_ref, embed_sem)
    qkv_copies = pieces(w_qkv_hbm, w_qkv_ref, qkv_sem)
    patch_copy = pltpu.make_async_copy(patch_hbm, patch_ref, patch_sem)
    pos_copy = pltpu.make_async_copy(pos_hbm, pos_ref, pos_sem)
    for copy in [patch_copy, *embed_copies, pos_copy, *qkv_copies]:
        copy.start()
    patch_copy.wait()
    total = None
    for step, copy in enumerate(embed_copies):
        copy.wait()
        cols = slice(step * tile, (step + 1) * tile)
        part = dot(patch_ref[:, cols], w_embed_ref[cols, :])
        total = part if total is None else total + part
    pos_copy.wait()
    tok_ref[...] = (total + pos_ref[...].astype(F32)).astype(BF)
    pick = slot_of_row(slots_ref[...]).astype(BF)
    normed = layer_norm(tok_ref[...].astype(F32), gain_ref[...]).astype(BF)
    normed_ref[...] = lax.dot_general(
        pick, normed, (((0,), (0,)), ((), ())), preferred_element_type=F32
    ).astype(BF)
    for copy in qkv_copies:
        copy.wait()
    for step in range(3 * att // tile):
        cols = slice(step * tile, (step + 1) * tile)
        qkv_ref[:, cols] = dot(normed_ref[...], w_qkv_ref[:, cols]).astype(BF)

    count = jnp.sum(jnp.where(slots_ref[...] >= 0, 1.0, 0.0), axis=1, keepdims=True)
    high = jnp.floor(count * (1.0 / 16))
    lane = lax.broadcasted_iota(jnp.int32, (16, 128), 1)
    info = jnp.where(lane < 64, high, count - 16.0 * high).astype(BF)
    for head in range(HEADS):
        at = head * size
        q = qkv_ref[:, at : at + size]
        k = qkv_ref[:, att + at : att + at + size]
        v = qkv_ref[:, 2 * att + at : 2 * att + at + size]
        send_buf[head, :half, :] = jnp.concatenate([q[:half], q[half:]], axis=1)
        send_buf[head, half : half + rows, :] = jnp.concatenate([k, v], axis=1)
        send_buf[head, half + rows :, :] = info
    if len(send_refs) == 1:
        copies = [pltpu.make_async_copy(send_buf, send_refs[0], send_sem.at[0])]
    else:
        copies = [
            pltpu.make_async_copy(send_buf.at[me_ref[1] ^ index], ref, send_sem.at[index])
            for index, ref in enumerate(send_refs)
        ]
    for copy in copies:
        copy.start()
    for copy in copies:
        copy.wait()


def enc_attend_kernel(me_ref, *refs, q_at, kv_at, rows, cap_q, cap_k):
    *blocks, out_ref, q_buf, kv_buf, o_buf = refs
    if len(blocks) == HEADS:
        q_of = kv_of = lambda source: blocks[source]
        place_of = lambda source: me_ref[1] ^ ORDER[source]
        sources, first = HEADS, 0
    else:
        q_of, kv_of = blocks[0].at.__getitem__, blocks[1].at.__getitem__
        place_of = lambda source: source
        sources, first = blocks[1].shape[0], me_ref[2]
    half = rows // 2
    lane16 = lax.broadcasted_iota(jnp.int32, (16, 128), 1)
    lane_h = lax.broadcasted_iota(jnp.int32, (half, 128), 1)

    def count_of(source):
        info = kv_of(source)[kv_at + rows : kv_at + rows + 16, :].astype(F32)
        high = jnp.max(jnp.where(lane16 < 64, info, 0.0)).astype(jnp.int32)
        low = jnp.max(jnp.where(lane16 >= 64, info, 0.0)).astype(jnp.int32)
        return high * 16 + low

    q_buf[...] = jnp.zeros_like(q_buf)
    o_buf[...] = jnp.zeros_like(o_buf)
    kv_buf[:, :128] = jnp.zeros((kv_buf.shape[0], 128), BF)
    kv_buf[:, 128:] = jnp.ones((kv_buf.shape[0], 128), BF)

    key = lax.broadcasted_iota(jnp.int32, (1, cap_k), 1)
    valid = jnp.zeros((1, cap_k), F32)
    off = jnp.int32(0)
    for source in range(sources):
        count = count_of(source)
        off = pl.multiple_of(off, 16)
        kv_buf[pl.ds(off, rows), :128] = kv_of(source)[kv_at : kv_at + rows, :]
        valid = jnp.where((key >= off) & (key < off + count), 1.0, valid)
        off = off + (count + 15) // 16 * 16
    bias = jnp.where(valid > 0.0, 0.0, -1e30)

    offs = []
    off = jnp.int32(0)
    for source in range(HEADS):
        off = pl.multiple_of(off, 16)
        offs.append(off)
        block = q_of(source)[q_at : q_at + half, :]
        zero = jnp.zeros_like(block)
        q_buf[pl.ds(off, half), :] = jnp.where(lane_h < 64, block, zero)
        q_buf[pl.ds(off + half, half), :] = jnp.where(lane_h < 64, swap_halves(block), zero)
        off = off + (count_of(first + source) + 15) // 16 * 16
    total = off

    scale = LOG2E * 64**-0.5

    def attend(at):
        score = dot_t(q_buf[at, :], kv_buf[:cap_k, :128]) + bias
        top = jnp.max(score, axis=1, keepdims=True)
        weight = jnp.exp2((score - top) * scale).astype(BF)
        mixed = dot(weight, kv_buf[:cap_k, :])
        o_buf[at, :] = (mixed[:, :128] / mixed[:, 128:]).astype(BF)

    if cap_q == cap_k:
        for at in range(0, cap_q, cap_q // 4):
            attend(slice(at, at + cap_q // 4))
    else:
        tile = 128

        @pl.loop(0, cap_q // tile)
        def _(step):
            @pl.when(step * tile < total)
            def _():
                attend(pl.ds(pl.multiple_of(step * tile, tile), tile))

    for source in range(HEADS):
        upper = o_buf[pl.ds(offs[source], half), :]
        lower = o_buf[pl.ds(pl.multiple_of(offs[source] + half, 16), half), :]
        out_ref[place_of(source)] = jnp.where(lane_h < 64, swap_halves(upper), lower)


def middle_kernel(
    att_ref, tok_ref, w_out_ref, out_gain_ref, w_dec_ref, mask_ref, pos_ref, gain_ref,
    w_qkv_ref, slots_ref, owner_ref, patch_ref,
    send_ref, y_ref, target_ref, flag_ref, att_buf, qkv_buf, *, groups,
):
    rows, width = tok_ref.shape
    half = rows // 2
    block = rows // groups
    for pair in range(HEADS // 2):
        a, b = att_ref[2 * pair], att_ref[2 * pair + 1]
        cols = slice(128 * pair, 128 * pair + 128)
        att_buf[:half, cols] = jnp.concatenate([a[:, :64], b[:, :64]], axis=1)
        att_buf[half:, cols] = jnp.concatenate([a[:, 64:], b[:, 64:]], axis=1)
    pick = slot_of_row(slots_ref[...])
    seen = jnp.sum(pick, axis=1, keepdims=True)
    attended = dot(pick.astype(BF), att_buf[...]).astype(BF)
    encoded = tok_ref[...].astype(F32) + dot(attended, w_out_ref[...])
    dec_normed = layer_norm(encoded, out_gain_ref[...]).astype(BF)
    dec_tok = dot(dec_normed, w_dec_ref[...]).astype(BF).astype(F32)
    filled = jnp.where(seen > 0.0, dec_tok, as_row(mask_ref[...]))
    decoder_in = (filled + pos_ref[...].astype(F32)).astype(BF)

    owner = owner_ref[...]
    dest = jnp.zeros_like(owner)
    for device in range(1, groups):
        dest = dest + jnp.where(owner >= device * rows, 1, 0)
    local = owner - dest * rows
    first = jnp.min(local.astype(F32), axis=1, keepdims=True).astype(jnp.int32)
    place = dest * block + local - first
    move = slot_of_row(place).astype(BF)
    y = dot(move, decoder_in)
    y_ref[...] = y.astype(BF)
    target_ref[...] = dot(move, patch_ref[...]).astype(BF)
    hidden = jnp.broadcast_to(1.0 - seen, (rows, 128)).astype(BF)
    flag_ref[...] = dot(move, hidden)
    attn_in = layer_norm(y, gain_ref[...]).astype(BF)
    qkv_buf[...] = dot(attn_in, w_qkv_ref[...]).astype(BF).astype(F32)
    att = w_qkv_ref.shape[1] // 3
    size = att // HEADS
    quarter = rows // 4
    for head in range(HEADS):
        at = head * size
        q = qkv_buf[:, at : at + size]
        k = qkv_buf[:, att + at : att + at + size]
        v = qkv_buf[:, 2 * att + at : 2 * att + at + size]
        send_ref[head, :half, :] = jnp.concatenate(
            [k[:half], v[:half], k[half:], v[half:]], axis=1
        ).astype(BF)
        send_ref[head, half:, :] = jnp.concatenate(
            [q[i * quarter : (i + 1) * quarter] for i in range(4)], axis=1
        ).astype(BF)


def dec_attend_kernel(q_ref, kv_ref, out_ref, k_buf, v_buf, *, q_at, rows):
    half = rows // 2
    quarter = rows // 4
    sources = kv_ref.shape[0]
    for source in range(sources):
        for part in range(2):
            block = kv_ref[source, :half, 64 * part : 64 * part + 64]
            at = source * rows + part * half
            k, v = block[:, :32], block[:, 32:]
            k_buf[at : at + half, :] = jnp.concatenate([k, k, k, k], axis=1)
            v_buf[at : at + half, :128] = jnp.concatenate([v, v, v, v], axis=1)
    v_buf[:, 128:] = jnp.ones((v_buf.shape[0], 128), BF)
    scale = LOG2E * 32**-0.5
    lane = lax.broadcasted_iota(jnp.int32, (quarter, 128), 1)
    zone = [(lane >= 32 * i) & (lane < 32 * i + 32) for i in range(4)]

    chunk = 256
    unroll = 4 if sources == HEADS else 1

    def attend(source):
        block = q_ref[source, q_at : q_at + quarter, :].astype(F32)
        q = jnp.concatenate([jnp.where(z, block, 0.0) for z in zone], axis=0).astype(BF)
        top = mixed = None
        for at in range(0, k_buf.shape[0], chunk):
            score = dot_t(q, k_buf[at : at + chunk, :])
            peak = jnp.max(score, axis=1, keepdims=True)
            new = peak if top is None else jnp.maximum(top, peak)
            weight = jnp.exp2((score - new) * scale).astype(BF)
            part = dot(weight, v_buf[at : at + chunk, :])
            mixed = part if top is None else mixed * jnp.exp2((top - new) * scale) + part
            top = new
        mixed = mixed[:, :128] / mixed[:, 128:]
        out = mixed[:quarter]
        for i in range(1, 4):
            out = jnp.where(zone[i], mixed[i * quarter : (i + 1) * quarter], out)
        out_ref[source] = out.astype(BF)

    @pl.loop(0, HEADS // unroll)
    def _(step):
        for i in range(unroll):
            attend(step * unroll + i)


def tail_kernel(
    me_ref, att_ref, y_ref, w_out_ref, feed_gain_ref, w_up_ref, w_down_ref, head_gain_ref,
    w_head_ref, target_ref, flag_ref,
    dec_att_ref, mid_ref, slope_ref, z_ref, dpred_ref, loss_ref, keep_ref, send_ref, *refs,
):
    *zn_refs, feed_buf, zn_buf, split_buf, head_buf = refs
    rows, width = y_ref.shape
    pixels = w_head_ref.shape[1]
    hidden = w_up_ref.shape[1]
    blocks = [att_ref[head].astype(F32) for head in range(HEADS)]
    dec_att_ref[...] = jnp.concatenate(
        [
            jnp.concatenate([b[:, 32 * i : 32 * i + 32] for b in blocks], axis=1)
            for i in range(4)
        ],
        axis=0,
    ).astype(BF)
    mid_ref[...] = y_ref[...].astype(F32) + dot(dec_att_ref[...], w_out_ref[...])
    feed_buf[...] = layer_norm(mid_ref[...], feed_gain_ref[...]).astype(BF)
    z_ref[...] = mid_ref[...]
    tile = 512
    c = math.sqrt(2.0 / math.pi)
    for at in range(0, hidden, tile):
        cols = slice(at, at + tile)
        pre = dot(feed_buf[...], w_up_ref[:, cols])
        square = pre * pre
        t = jnp.tanh(pre * (c + (c * 0.044715) * square))
        gate = 0.5 + 0.5 * t
        act = pre * gate
        slope = gate + act * (1.0 - gate) * (2 * c + (6 * c * 0.044715) * square)
        slope_ref[:, cols] = slope.astype(BF)
        z_ref[...] += dot(act.astype(BF), w_down_ref[cols, :])

    zn = layer_norm(z_ref[...], head_gain_ref[...])
    zn_buf[...] = zn.astype(BF)
    share = split_buf.shape[1]
    for dest in range(split_buf.shape[0]):
        split_buf[dest] = zn[dest * share : (dest + 1) * share, :].astype(BF)
    if len(zn_refs) == 1:
        zn_refs[0][...] = split_buf[...]
    else:
        for index in range(2 * zn_refs[0].shape[0]):
            zn_refs[index % 2][index // 2] = split_buf[me_ref[1] ^ index]
    flag = flag_ref[:, :1]
    loss = jnp.zeros((1, 1), F32)
    for at in range(0, pixels, tile):
        cols = slice(at, at + tile)
        pred = dot(zn_buf[...], w_head_ref[:, cols])
        err = (pred - target_ref[:, cols].astype(F32)) * flag
        dpred_ref[:, cols] = (err * (2.0 / pixels)).astype(BF)
        loss += jnp.sum(jnp.sum(err * err, axis=1, keepdims=True), axis=0, keepdims=True)
        head_buf[:, cols] = lax.dot_general(
            zn_buf[...], dpred_ref[:, cols], (((0,), (0,)), ((), ())), preferred_element_type=F32
        )
    loss_ref[...] = jnp.broadcast_to(loss * (1.0 / pixels), loss_ref.shape)
    tall = width // 32
    for index in range(32):
        at = pl.multiple_of((index ^ me_ref[0]) * tall, tall)
        ref = send_ref if index % 2 else keep_ref
        ref[index // 2 % 4, index // 8] = head_buf[pl.ds(at, tall), :].astype(BF)


def gather_kernel(me_ref, w_head_ref, *refs, places):
    *parts, out_ref, split_buf, zn_buf = refs
    share = split_buf.shape[1]
    for ref, indices in zip(parts, places):
        for i, index in enumerate(indices):
            split_buf[me_ref[3] ^ index] = ref[i].astype(F32)
    zn_buf[...] = jnp.concatenate(
        [split_buf[device] for device in range(split_buf.shape[0])], axis=0
    ).astype(BF)
    tile = 512
    for at in range(0, w_head_ref.shape[1], tile):
        cols = slice(at, at + tile)
        out_ref[:, cols] = dot(zn_buf[...], w_head_ref[:, cols]).astype(BF)


def backward_kernel(
    me_ref, dec_att_ref, mid_ref, slope_ref, dpred_ref, z_ref, loss_ref, head_gain_ref, w_head_ref,
    feed_gain_ref, w_up_ref, w_down_ref,
    keep_ref, send_ref, back_buf, out_buf,
):
    hidden = w_up_ref.shape[1]
    dz = norm_backward(
        z_ref[...], head_gain_ref[...], dot_t(dpred_ref[...], w_head_ref[...])
    ).astype(BF)
    tile = 512
    for at in range(0, hidden, tile):
        cols = slice(at, at + tile)
        back = dot_t(dz, w_down_ref[cols, :]) * slope_ref[:, cols].astype(F32)
        part = dot_t(back.astype(BF), w_up_ref[:, cols])
        back_buf[...] = part if at == 0 else back_buf[...] + part

    mid_grad = (
        dz.astype(F32) + norm_backward(mid_ref[...], feed_gain_ref[...], back_buf[...])
    ).astype(BF)
    out_buf[...] = lax.dot_general(
        dec_att_ref[...], mid_grad, (((0,), (0,)), ((), ())), preferred_element_type=F32
    )
    loss = loss_ref[...]
    high = loss.astype(BF)
    low = (loss - high.astype(F32)).astype(BF)
    sums = jnp.concatenate([high.astype(F32), low.astype(F32)], axis=0).astype(BF)
    deep = out_buf.shape[0] // 32
    half = out_buf.shape[1] // 2
    for index in range(32):
        at = pl.multiple_of((index ^ me_ref[0]) * deep, deep)
        ref = send_ref if index % 2 else keep_ref
        xy, z = index // 2 % 4, index // 8
        part = out_buf[pl.ds(at, deep), :]
        ref[xy, z, :, :half] = jnp.concatenate([part[:, :half], part[:, half:]], axis=0).astype(BF)
        ref[xy, z, :, half:] = sums


def merge_kernel(
    head_keep_ref, head_got_ref, out_keep_ref, out_got_ref, mine_ref, other_ref, *refs
):
    head = (head_keep_ref[...].astype(F32) + head_got_ref[...].astype(F32)).astype(BF)
    out = (out_keep_ref[...].astype(F32) + out_got_ref[...].astype(F32)).astype(BF)
    pixels = head.shape[3]
    for i in range(4):
        refs[i][:, :, :pixels] = head[i]
        refs[i][:, :, pixels:] = out[i]
    for i in range(1, 4):
        refs[3 + i][0] = mine_ref[i]
        refs[3 + i][1] = other_ref[i]


def add_kernel(*refs, count):
    total = refs[0][...].astype(F32)
    for ref in refs[1:count]:
        total = total + ref[...].astype(F32)
    total = total.astype(BF)
    outs = refs[count:]
    if len(outs) == 1:
        outs[0][...] = total
    else:
        for i, ref in enumerate(outs):
            ref[...] = total[i]


def join_kernel(*refs):
    for i, ref in enumerate(refs[:-1]):
        refs[-1][i] = ref[...]


def place_kernel(me_ref, *refs, masked_total):
    blocks, (head_ref, out_ref, loss_ref) = refs[:8], refs[8:]
    pixels = head_ref.shape[1]
    deep = out_ref.shape[0] // 32
    half = out_ref.shape[1] // 2
    tall = head_ref.shape[0] // 32
    for index in range(32):
        block = index ^ me_ref[0]
        value = blocks[index % 2 * 4 + index // 2 % 4][index // 8].astype(F32)
        head_ref[pl.ds(pl.multiple_of(block * tall, tall), tall), :] = value[:, :pixels]
        at = pl.ds(pl.multiple_of(block * deep, deep), deep)
        out_ref[at, :half] = value[:deep, pixels : pixels + half]
        out_ref[at, half:] = value[deep:, pixels : pixels + half]
    value = blocks[0][0].astype(F32)
    total = value[:8, pixels + half :] + value[8:, pixels + half :]
    loss_ref[0, 0] = jnp.max(total) * (1.0 / masked_total)


def vmem_call(kernel, outs, scratch, inputs, smem=(), smem_out=(), anywhere=(),
              anywhere_out=(), vmem=VMEM_LIMIT, flops=0):
    space = [
        pl.BlockSpec(
            memory_space=pltpu.SMEM if i in smem else pltpu.HBM if i in anywhere else pltpu.VMEM
        )
        for i in range(len(inputs))
    ]
    moved = sum(a.size * a.dtype.itemsize for a in inputs)
    return pl.pallas_call(
        kernel,
        out_shape=outs,
        in_specs=space,
        out_specs=[
            pl.BlockSpec(
                memory_space=pltpu.SMEM
                if i in smem_out
                else pl.ANY
                if i in anywhere_out
                else pltpu.VMEM
            )
            for i in range(len(outs))
        ],
        scratch_shapes=scratch,
        compiler_params=pltpu.CompilerParams(vmem_limit_bytes=vmem),
        cost_estimate=pl.CostEstimate(flops=flops, bytes_accessed=moved, transcendentals=0),
    )(*inputs)


def pinned(x):
    return pltpu.with_memory_space_constraint(x, pltpu.HBM)


def swap(x, axis, groups=None):
    return lax.all_to_all(
        x, axis, split_axis=0, concat_axis=0, tiled=True, axis_index_groups=groups
    )


def all_sum(x, groups):
    size = lax.axis_size("dp")
    me = lax.axis_index("dp")
    stages = []
    step = 1
    while step < size:
        pairs = [(i, i ^ step) for i in range(size)]
        upper = (me // step) % 2
        half = x.shape[0] // 2
        mine = lax.dynamic_slice_in_dim(x, upper * half, half, 0)
        other = lax.dynamic_slice_in_dim(x, (1 - upper) * half, half, 0)
        x = mine + lax.ppermute(other, "dp", pairs)
        stages.append((pairs, upper))
        step *= 2
    rows, width = x.shape
    blocks = swap(x.reshape(groups, rows // groups, width), "ctx")
    total = jnp.sum(blocks.astype(F32), axis=0).astype(BF)
    x = swap(jnp.broadcast_to(total[None], blocks.shape), "ctx").reshape(rows, width)
    for pairs, upper in reversed(stages):
        other = lax.ppermute(x, "dp", pairs)
        low = jnp.where(upper == 0, x, other)
        high = jnp.where(upper == 0, other, x)
        x = jnp.concatenate([low, high], axis=0)
    return x


def across(x, dp_bit, ctx_bits):
    count, groups = lax.axis_size("dp"), lax.axis_size("ctx")
    pairs = [
        (i * groups + j, (i ^ dp_bit) * groups + (j ^ ctx_bits))
        for i in range(count)
        for j in range(groups)
    ]
    return lax.ppermute(x, ("dp", "ctx"), pairs)


PLANE = ((2, 0), (0, 1), (2, 1))
COLUMN = ((0, 2), (0, 4), (0, 6))


def sum_by_permutes(head_keep, head_send, zn_keep, zn_send, backward, rebuild):
    shape = jax.ShapeDtypeStruct
    head_got = across(head_send, 1, 0)
    zn_got = across(zn_send, 0, 1)
    out_keep, out_send = backward()
    out_send, head_got, zn_got = lax.optimization_barrier((out_send, head_got, zn_got))
    out_got = across(out_send, 1, 0)
    block = shape((head_keep.shape[2], head_keep.shape[3] + out_keep.shape[3]), BF)
    part = shape((4, *block.shape), BF)
    pair = shape((2, *zn_keep.shape[1:]), BF)
    *parts, zn1, zn2, zn3 = vmem_call(
        merge_kernel,
        [part] * 4 + [pair] * 3,
        [],
        [head_keep, head_got, out_keep, out_got, zn_keep, zn_got],
    )
    rest = [across(p, *bits) for p, bits in zip((zn1, zn2, zn3), COLUMN)]
    others = [across(p, *bits) for p, bits in zip(parts[1:], PLANE)]
    mine, *far = lax.optimization_barrier((parts[0], *rest[1:]))
    rest = [rest[0], *far]
    blocks = vmem_call(
        functools.partial(add_kernel, count=4), [block] * 4, [], [*reversed(others), mine]
    )
    others = [across(b, *bits) for b, bits in zip(blocks[1:], COLUMN)]
    (total,) = vmem_call(
        functools.partial(add_kernel, count=4), [block], [], [*reversed(others), blocks[0]]
    )
    (column,) = vmem_call(
        join_kernel,
        [part],
        [],
        [total] + [across(total, *bits) for bits in COLUMN],
    )
    column, reconstruction = lax.optimization_barrier(
        (column, rebuild([zn_keep, zn_got, *rest]))
    )
    ours = [column] + [across(column, *bits) for bits in PLANE]
    return ours, [across(x, 1, 0) for x in ours], reconstruction


def sum_by_blocks(keep, send, groups):
    size = keep.shape[0] * keep.shape[1] * keep.shape[2]
    flat = jnp.concatenate([keep.reshape(size, -1), send.reshape(size, -1)], axis=0)
    unit = lax.axis_size("dp") * groups
    used = flat.shape[0]
    padded = -(-used // unit) * unit
    total = all_sum(jnp.pad(flat, ((0, padded - used), (0, 0))), groups)[:used]
    total = total.reshape(2, *keep.shape)
    return [total[0, i] for i in range(4)], [total[1, i] for i in range(4)]


def on_device(
    patches,
    enc_pos,
    w_embed,
    enc_gain,
    w_qkv,
    w_out,
    enc_out_gain,
    w_dec_embed,
    mask_token,
    dec_pos,
    dec_attn_gain,
    decoder_query_key_value_weight,
    w_dec_out,
    decoder_feed_gain,
    w_up,
    w_down,
    head_gain,
    w_head,
    visible_rows,
    visible_count,
    owner_slot,
):
    groups = lax.axis_size("ctx")
    repeat = groups // HEADS
    teams = [list(range(HEADS * i, HEADS * i + HEADS)) for i in range(repeat)]
    teams = None if repeat == 1 else teams
    dp_me, ctx_me = lax.axis_index("dp"), lax.axis_index("ctx")
    place = dp_me % 2 + 2 * (dp_me // 2) + 4 * (ctx_me % 2) + 8 * (ctx_me // 2)
    if repeat > 1:
        place = jnp.zeros_like(place)
    me = jnp.stack(
        [place, ctx_me, ctx_me // HEADS * HEADS, ctx_me if repeat == 1 else place]
    ).astype(jnp.int32)
    source, me = lax.optimization_barrier((patches[0], me))
    rows, pixels = source.shape
    half, quarter = rows // 2, rows // 4
    share = rows // 3
    width = w_embed.shape[1]
    dec_width = w_dec_embed.shape[1]
    shape = jax.ShapeDtypeStruct

    tall_block = half + rows + 16
    tok, *send = vmem_call(
        embed_kernel,
        [shape((rows, width), BF)]
        + (
            [shape((tall_block, 128), BF)] * HEADS
            if repeat == 1
            else [shape((HEADS, tall_block, 128), BF)]
        ),
        [
            pltpu.VMEM((rows, width), BF),
            pltpu.VMEM((rows, w_qkv.shape[1]), BF),
            pltpu.VMEM(source.shape, BF),
            pltpu.VMEM(enc_pos.shape, BF),
            pltpu.VMEM(w_embed.shape, BF),
            pltpu.VMEM(w_qkv.shape, BF),
            pltpu.VMEM((HEADS, tall_block, 128), BF),
            pltpu.SemaphoreType.DMA,
            pltpu.SemaphoreType.DMA,
            pltpu.SemaphoreType.DMA((pixels // 256,)),
            pltpu.SemaphoreType.DMA((width // 256,)),
            pltpu.SemaphoreType.DMA((HEADS,)),
        ],
        [me]
        + [pinned(x) for x in (source, enc_pos, w_embed, enc_gain, w_qkv, visible_rows)],
        smem=(0,),
        anywhere=(1, 2, 3, 5),
        anywhere_out=range(1, 1 + HEADS),
        vmem=28 << 20,
        flops=2 * rows * width * (pixels + w_qkv.shape[1]),
    )
    if repeat == 1:
        blocks = [across(send[i], 0, i) if i else send[0] for i in ORDER]
        q_at, kv_at = 0, half
    else:
        blocks = [
            swap(send[0][:, :half], "ctx", teams),
            swap(jnp.tile(send[0][:, half:], (repeat, 1, 1)), "ctx"),
        ]
        q_at, kv_at = 0, 0
    cap_k = (share + 16) * groups
    cap_q = min(HEADS * rows, cap_k)
    (att,) = vmem_call(
        functools.partial(
            enc_attend_kernel, q_at=q_at, kv_at=kv_at, rows=rows, cap_q=cap_q, cap_k=cap_k
        ),
        [shape((HEADS, half, 128), BF)],
        [
            pltpu.VMEM((cap_q + rows, 128), BF),
            pltpu.VMEM((cap_k + rows, 256), BF),
            pltpu.VMEM((cap_q + rows, 128), BF),
        ],
        [me, *blocks],
        smem=(0,),
        flops=4 * cap_q * cap_k * 128,
    )
    att = swap(att, "ctx", teams)
    send, y_own, target, flag = vmem_call(
        functools.partial(middle_kernel, groups=groups),
        [
            shape((HEADS, half + quarter, 128), BF),
            shape((rows, dec_width), BF),
            shape((rows, pixels), BF),
            shape((rows, 128), F32),
        ],
        [
            pltpu.VMEM((rows, w_out.shape[0]), BF),
            pltpu.VMEM((rows, decoder_query_key_value_weight.shape[1]), F32),
        ],
        [
            att, tok, w_out, enc_out_gain, w_dec_embed, mask_token, dec_pos,
            dec_attn_gain, decoder_query_key_value_weight, visible_rows, owner_slot, source,
        ],
        flops=2 * rows * width * 1024,
    )
    if repeat == 1:
        q = kv = swap(send, "ctx")
        q_at = half
    else:
        q = swap(send[:, half:], "ctx", teams)
        kv = swap(jnp.tile(send[:, :half], (repeat, 1, 1)), "ctx")
        q_at = 0
    (att,) = vmem_call(
        functools.partial(dec_attend_kernel, q_at=q_at, rows=rows),
        [shape((HEADS, quarter, 128), BF)],
        [pltpu.VMEM((groups * rows, 128), BF), pltpu.VMEM((groups * rows, 256), BF)],
        [q, kv],
        flops=4 * HEADS * rows * groups * rows * 128,
    )
    att = swap(att, "ctx", teams)
    hidden = w_up.shape[1]
    share_rows = rows // groups
    tall = dec_width // 32
    split = (groups, share_rows, dec_width)
    dec_att, y_mid, slope, z, dpred, loss_part, head_keep, head_send, *zn = vmem_call(
        tail_kernel,
        [
            shape((rows, w_dec_out.shape[0]), BF),
            shape((rows, dec_width), F32),
            shape((rows, hidden), BF),
            shape((rows, dec_width), F32),
            shape((rows, pixels), BF),
            shape((8, 128), F32),
        ]
        + [shape((4, 4, tall, pixels), BF)] * 2
        + ([shape((4, *split[1:]), BF)] * 2 if repeat == 1 else [shape(split, BF)]),
        [
            pltpu.VMEM((rows, dec_width), BF),
            pltpu.VMEM((rows, dec_width), BF),
            pltpu.VMEM(split, BF),
            pltpu.VMEM((dec_width, pixels), F32),
        ],
        [
            me, att, y_own, w_dec_out, decoder_feed_gain, w_up, w_down, head_gain, w_head,
            target, flag,
        ],
        smem=(0,),
        flops=2 * rows * dec_width * (2 * hidden + 2 * pixels),
    )

    def backward():
        return vmem_call(
            backward_kernel,
            [shape((4, 4, tall, dec_width // 2 + 128), BF)] * 2,
            [
                pltpu.VMEM((rows, dec_width), F32),
                pltpu.VMEM((w_dec_out.shape[0], dec_width), F32),
            ],
            [
                me, dec_att, y_mid, slope, dpred, z, loss_part, head_gain, w_head,
                decoder_feed_gain, w_up, w_down,
            ],
            smem=(0,),
            flops=40 * rows * dec_width * hidden,
        )

    places = [(0,), (1,), (2, 3), (4, 5), (6, 7)] if repeat == 1 else [tuple(range(groups))]

    def rebuild(parts):
        return vmem_call(
            functools.partial(gather_kernel, places=places),
            [shape((rows, pixels), BF)],
            [pltpu.VMEM(split, F32), pltpu.VMEM((rows, dec_width), BF)],
            [me, w_head, *parts],
            smem=(0,),
            flops=2 * rows * dec_width * pixels,
        )[0]

    if repeat == 1:
        ours, theirs, reconstruction = sum_by_permutes(
            head_keep, head_send, *zn, backward, rebuild
        )
    else:
        out_keep, out_send = backward()
        ours, theirs = sum_by_blocks(
            jnp.concatenate([head_keep, out_keep], axis=3),
            jnp.concatenate([head_send, out_send], axis=3),
            groups,
        )
        reconstruction = rebuild([swap(zn[0], "ctx")])
    masked_total = lax.axis_size("dp") * (groups * rows - share * groups)
    grad_head, grad_dec_out, loss = vmem_call(
        functools.partial(place_kernel, masked_total=masked_total),
        [shape(w_head.shape, F32), shape(w_dec_out.shape, F32), shape((1, 1), F32)],
        [],
        [me, *ours, *theirs],
        smem=(0,),
        smem_out=(2,),
    )
    return (reconstruction.reshape(1, rows, pixels), grad_head, grad_dec_out, loss.reshape(()))


def solution(mesh):
    in_specs = (
        P("dp", "ctx", None),
        P("ctx", None),
        P(),
        P(),
        P(),
        P(),
        P(),
        P(),
        P(),
        P("ctx", None),
        P(),
        P(),
        P(),
        P(),
        P(),
        P(),
        P(),
        P(),
        P("dp", "ctx"),
        P("dp", "ctx"),
        P("dp", "ctx"),
    )
    out_specs = (P("dp", "ctx", None), P(), P(), P())
    return jax.shard_map(
        on_device, mesh=mesh, in_specs=in_specs, out_specs=out_specs, check_vma=False
    )
```
